256 devices in a mesh: frame: 64 (over y, x_lo, z), head: 4 (over x_hi, core).
Axes of the slice: x: 4 (x_hi: 2, x_lo: 2; x = x_hi * 2 + x_lo), y: 4, z: 8, core: 2. Of those that a mesh axis runs over, the one named last changes fastest.
Arguments:
- q_raw: bfloat16 [2, 24576, 5120], P(None, 'frame', 'head'), may hold values from -200 to 200
- k_raw: bfloat16 [2, 24576, 5120], P(None, 'frame', 'head'), may hold values from -200 to 200
- v_in: bfloat16 [2, 24576, 5120], P(None, 'frame', 'head'), may hold values from -6 to 6
- cross_q_raw: bfloat16 [2, 24576, 5120], P(None, 'frame', 'head'), may hold values from -200 to 200
- text_k_raw: bfloat16 [2, 512, 5120], P(None, 'frame', 'head'), may hold values from -200 to 200
- text_v: bfloat16 [2, 512, 5120], P(None, 'frame', 'head'), may hold values from -6 to 6
- q_gain: float32 [5120], P('head'), may hold values from 0.5 to 1.5
- k_gain: float32 [5120], P('head'), may hold values from 0.5 to 1.5
- cross_q_gain: float32 [5120], P('head'), may hold values from 0.5 to 1.5
- text_k_gain: float32 [5120], P('head'), may hold values from 0.5 to 1.5
- nbr: int32 [192, 14], P('frame'), may hold values from 0 to 191, as said below
- nbr_count: int32 [192], P('frame'), may hold values from 7 to 14
- text_len: int32 [2], replicated, may hold values from 256 to 512
Outputs:
- self_out: bfloat16 [2, 24576, 5120], P(None, 'frame', 'head')
- cross_out: bfloat16 [2, 24576, 5120], P(None, 'frame', 'head')
The draws below stay inside these ranges and needn't reach their ends.
Inputs may be any that keep to these rules, and one draw needn't show every extreme that they name: Row r of nbr begins with r; its first nbr_count[r] entries are distinct tiles whose frame shard (tile // 3) lies at most 2 from that of r; its other entries equal r.
All inputs are finite; a program needn't handle non-finite values.
Results may differ from the reference program's by a relative error of at most 0.002.
The reference program's roundings to bfloat16 on the way (of `queries`, `key_rows`, `cross_queries`, `text_keys`, `self_weights` and `cross_weights`) count: a program that leaves them out, or rounds other values in their place, can miss the bound.
Values may be sent and summed in bfloat16 or wider, within the bound.
A program may use at most 192 MiB of HBM per device.

```python
import math
import jax
import jax.numpy as jnp
from jax import lax

D = 5120
HEADS = 40
HD = 128
TXT = 512
TILE = 128
NB = 14
REACH = 2
TILES_DEV = 3
TILES = 192
TOKENS = 24576
N_FRAME = 64


def stream(key, label):
    return jax.random.fold_in(key, label)


def rough_rows(key, row_total, salt):
    column = jnp.arange(D, dtype=jnp.float32)
    column_scale = jnp.exp(column / D * math.log(3.0) + jax.random.uniform(stream(key, salt + 1), (D,), jnp.float32, 0.0, math.log(10.0)))
    row_scale = jnp.exp(jax.random.uniform(stream(key, salt + 2), (2, row_total, 1), jnp.float32, 0.0, math.log(10.0)))
    base = jnp.clip(jax.random.normal(stream(key, salt + 3), (2, row_total, D), jnp.float32), -6.0, 6.0)
    return 0.1 * base * column_scale * row_scale


def query_like(key, salt):
    field = rough_rows(key, TOKENS, salt)
    return field


def draw_q_raw(key, part):
    return query_like(key, 100).astype(jnp.bfloat16)


def draw_cross_q_raw(key, part):
    return query_like(key, 300).astype(jnp.bfloat16)


def draw_k_raw(key, part):
    field = rough_rows(key, TOKENS, 200)
    return field.astype(jnp.bfloat16)


def draw_text_k_raw(key, part):
    field = rough_rows(key, TXT, 400)
    return field.astype(jnp.bfloat16)


def tile_lists(key):
    reader = jnp.arange(TILES, dtype=jnp.int32)
    reader_shard = reader // TILES_DEV
    shard_steps = jnp.arange(2 * REACH + 1, dtype=jnp.int32) - REACH
    inner_tile = jnp.arange(TILES_DEV, dtype=jnp.int32)
    candidates_total = (2 * REACH + 1) * TILES_DEV
    candidate_shard = jnp.broadcast_to(reader_shard[:, None, None] + shard_steps[None, :, None], (TILES, 2 * REACH + 1, TILES_DEV))
    candidate = (candidate_shard * TILES_DEV + inner_tile[None, None, :]).reshape(TILES, candidates_total)
    usable = ((candidate_shard >= 0) & (candidate_shard < N_FRAME)).reshape(TILES, candidates_total) & (candidate != reader[:, None])
    ranking = jax.random.randint(stream(key, 501), (TILES, candidates_total), 0, 2 ** 20) * candidates_total + jnp.arange(candidates_total, dtype=jnp.int32)[None, :]
    ranking = jnp.where(usable, ranking, ranking + 2 ** 28)
    ranked_order = jnp.argsort(ranking, axis=1, stable=True)
    picked = jnp.take_along_axis(candidate, ranked_order[:, :NB - 1], axis=1)
    usable_count = jnp.sum(usable.astype(jnp.int32), axis=1)
    drawn_count = jax.random.randint(stream(key, 502), (TILES,), NB // 2, NB + 1)
    forced = (reader % 3 == 0) & (reader_shard >= REACH) & (reader_shard < N_FRAME - REACH)
    live_count = jnp.minimum(jnp.where(forced, NB, drawn_count), usable_count + 1).astype(jnp.int32)
    slot_index = jnp.arange(1, NB, dtype=jnp.int32)
    others_list = jnp.where(slot_index[None, :] < live_count[:, None], picked, reader[:, None])
    neighbour_list = jnp.concatenate([reader[:, None], others_list], axis=1).astype(jnp.int32)
    return (neighbour_list, live_count)


def draw_nbr(key, part):
    return tile_lists(key)[0]


def draw_nbr_count(key, part):
    return tile_lists(key)[1]


def block_levels(stream_key, extent, pieces, least, largest):
    level = 1.0
    for dim, parts in pieces:
        draws = jax.random.uniform(jax.random.fold_in(jax.random.fold_in(stream_key, 6), dim), (parts,), jnp.float32, least / len(pieces), largest / len(pieces))
        level = level * jnp.repeat(jnp.exp(draws), extent[dim] // parts).reshape((-1,) + (1,) * (len(extent) - 1 - dim))
    return level


def scatter_about(key, extent, scale, most, pieces=(), kind=jnp.bfloat16):
    loudness = block_levels(key, extent, pieces, -0.22, 0.18) if pieces else 1.0
    values = jax.random.normal(key, extent, jnp.float32) * scale * loudness
    return jnp.minimum(jnp.maximum(values, -most), most).astype(kind)


def setup_inputs(seed: int = 0) -> dict:
    key_of = jax.random.split(jax.random.key(seed), 14)
    return {
        "q_raw": draw_q_raw(jax.random.fold_in(key_of[13], 71), 0),
        "k_raw": draw_k_raw(jax.random.fold_in(key_of[13], 71), 0),
        "v_in": scatter_about(key_of[2], (2, TOKENS, D), 1.0, 6.0, ((1, 64), (2, 4))),
        "cross_q_raw": draw_cross_q_raw(jax.random.fold_in(key_of[13], 71), 0),
        "text_k_raw": draw_text_k_raw(jax.random.fold_in(key_of[13], 71), 0),
        "text_v": scatter_about(key_of[5], (2, TXT, D), 1.0, 6.0, ((1, 64), (2, 4))),
        "q_gain": jnp.clip(1.0 + 0.1 * jax.random.normal(key_of[6], (D,), jnp.float32), 0.5, 1.5),
        "k_gain": jnp.clip(1.0 + 0.1 * jax.random.normal(key_of[7], (D,), jnp.float32), 0.5, 1.5),
        "cross_q_gain": jnp.clip(1.0 + 0.1 * jax.random.normal(key_of[8], (D,), jnp.float32), 0.5, 1.5),
        "text_k_gain": jnp.clip(1.0 + 0.1 * jax.random.normal(key_of[9], (D,), jnp.float32), 0.5, 1.5),
        "nbr": draw_nbr(jax.random.fold_in(key_of[13], 71), 0),
        "nbr_count": draw_nbr_count(jax.random.fold_in(key_of[13], 71), 0),
        "text_len": jax.random.randint(key_of[12], (2,), TXT // 2, TXT + 1).astype(jnp.int32),
    }


EPSILON = 1e-06

def rms_scaled(tensor, gain_vector):
    values = tensor.astype(jnp.float32)
    mean_square = lax.optimization_barrier(jnp.mean(values * values, axis=-1, keepdims=True))
    return (values * lax.rsqrt(mean_square + EPSILON) * gain_vector).astype(jnp.bfloat16)

def soft_weights(scores):
    row_top = lax.optimization_barrier(jnp.max(scores, axis=-1, keepdims=True))
    powers = jnp.exp(scores - row_top)
    return (powers / lax.optimization_barrier(jnp.sum(powers, axis=-1, keepdims=True))).astype(jnp.bfloat16)

def reference(q_raw, k_raw, v_in, cross_q_raw, text_k_raw, text_v, q_gain, k_gain, cross_q_gain, text_k_gain, nbr, nbr_count, text_len):
    queries = rms_scaled(q_raw, q_gain)
    key_rows = rms_scaled(k_raw, k_gain)
    cross_queries = rms_scaled(cross_q_raw, cross_q_gain)
    text_keys = rms_scaled(text_k_raw, text_k_gain)
    score_scale = 1.0 / math.sqrt(HD)
    slot_tile = jnp.arange(NB * TILE, dtype=jnp.int32) // TILE
    text_mask = jnp.arange(TXT, dtype=jnp.int32)[None, :] < text_len[:, None]
    text_heads = text_keys.astype(jnp.float32).reshape(2, TXT, HEADS, HD)
    text_values = text_v.astype(jnp.float32).reshape(2, TXT, HEADS, HD)

    def take_tile(neighbour):
        row_start = neighbour * TILE
        return (lax.dynamic_slice_in_dim(key_rows, row_start, TILE, 1), lax.dynamic_slice_in_dim(v_in, row_start, TILE, 1))

    def one_tile(tile_index):
        row_start = tile_index * TILE
        query_rows = lax.dynamic_slice_in_dim(queries, row_start, TILE, 1).astype(jnp.float32).reshape(2, TILE, HEADS, HD)
        near_keys, near_values = jax.vmap(take_tile, out_axes=1)(nbr[tile_index])
        near_keys = near_keys.reshape(2, NB * TILE, HEADS, HD).astype(jnp.float32)
        near_values = near_values.reshape(2, NB * TILE, HEADS, HD).astype(jnp.float32)
        self_scores = jnp.einsum('cqhd,ckhd->chqk', query_rows, near_keys) * score_scale
        live_mask = slot_tile < nbr_count[tile_index]
        self_scores = jnp.where(live_mask[None, None, None, :], self_scores, -1e+30)
        self_weights = soft_weights(self_scores).astype(jnp.float32)
        self_rows = jnp.einsum('chqk,ckhd->cqhd', self_weights, near_values).astype(jnp.bfloat16).reshape(2, TILE, D)
        cross_rows_in = lax.dynamic_slice_in_dim(cross_queries, row_start, TILE, 1).astype(jnp.float32).reshape(2, TILE, HEADS, HD)
        cross_scores = jnp.einsum('cqhd,ckhd->chqk', cross_rows_in, text_heads) * score_scale
        cross_scores = jnp.where(text_mask[:, None, None, :], cross_scores, -1e+30)
        cross_weights = soft_weights(cross_scores).astype(jnp.float32)
        cross_rows = jnp.einsum('chqk,ckhd->cqhd', cross_weights, text_values).astype(jnp.bfloat16).reshape(2, TILE, D)
        return (self_rows, cross_rows)
    self_tiles, cross_tiles = lax.map(one_tile, jnp.arange(TILES, dtype=jnp.int32))
    self_out = jnp.transpose(self_tiles, (1, 0, 2, 3)).reshape(2, TOKENS, D)
    cross_out = jnp.transpose(cross_tiles, (1, 0, 2, 3)).reshape(2, TOKENS, D)
    return (self_out, cross_out)
```

```python
import functools
import math

import jax
import jax.numpy as jnp
from jax import lax
from jax.experimental import pallas as pl
from jax.experimental.pallas import tpu as pltpu
from jax.sharding import PartitionSpec as P

D = 5120
HD = 128
NB = 14
REACH = 2


EPSILON = 1e-06


def from_behind(value, axis, by):
    length = lax.axis_size(axis)
    pairs = [(i, i + by) for i in range(length) if 0 <= i + by < length]
    return lax.ppermute(value, axis, pairs)


def swap_with(value, axis, bit):
    length = lax.axis_size(axis)
    pairs = [(i, i ^ bit) for i in range(length)]
    return lax.ppermute(value, axis, pairs)


def squares(tensor):
    values = tensor.astype(jnp.float32)
    return jnp.sum(values * values, axis=-1)


def scaled(tensor, totals, gain_vector):
    factor = lax.rsqrt(totals / D + EPSILON)[..., None]
    return (tensor.astype(jnp.float32) * factor * gain_vector).astype(jnp.bfloat16)


def attend_kernel(q_ref, k_ref, v_ref, mask_ref, o_ref, *, score_scale, tiles):
    q = q_ref[0]
    k = k_ref[0]
    scores = lax.dot_general(
        q, k, (((1,), (1,)), ((), ())), preferred_element_type=jnp.float32
    ) * score_scale
    rows, key_len = scores.shape
    scores = scores.reshape(tiles, rows // tiles, key_len)
    scores = jnp.where(mask_ref[...] > 0, scores, -1e30)
    row_top = jnp.max(scores, axis=-1, keepdims=True)
    powers = jnp.exp(scores - row_top)
    weights = (powers / jnp.sum(powers, axis=-1, keepdims=True)).astype(jnp.bfloat16)
    weights = weights.reshape(rows, key_len)
    out = jnp.dot(weights, v_ref[0], preferred_element_type=jnp.float32)
    o_ref[0] = out.astype(o_ref.dtype)


def attend(queries, keys, values, mask, mask_by_row, tile_len):
    rows, tok, width = queries.shape
    key_len = keys.shape[1]
    groups = width // HD
    tiles = tok // tile_len
    if mask_by_row:
        mask_spec = pl.BlockSpec((1, 1, key_len), lambda c, h: (c, 0, 0))
    else:
        mask_spec = pl.BlockSpec((tiles, 1, key_len), lambda c, h: (0, 0, 0))
    return pl.pallas_call(
        functools.partial(attend_kernel, score_scale=1.0 / math.sqrt(HD), tiles=tiles),
        out_shape=jax.ShapeDtypeStruct(queries.shape, jnp.bfloat16),
        grid=(rows, groups),
        in_specs=[
            pl.BlockSpec((1, tok, HD), lambda c, h: (c, 0, h)),
            pl.BlockSpec((1, key_len, HD), lambda c, h: (c, 0, h)),
            pl.BlockSpec((1, key_len, HD), lambda c, h: (c, 0, h)),
            mask_spec,
        ],
        out_specs=pl.BlockSpec((1, tok, HD), lambda c, h: (c, 0, h)),
        cost_estimate=pl.CostEstimate(
            flops=4 * rows * tok * key_len * width,
            transcendentals=rows * tok * key_len * groups,
            bytes_accessed=2 * (2 * queries.size + 2 * keys.size),
        ),
    )(queries, keys, values, mask)


def body(
    q_raw,
    k_raw,
    v_in,
    cross_q_raw,
    text_k_raw,
    text_v,
    q_gain,
    k_gain,
    cross_q_gain,
    text_k_gain,
    nbr,
    nbr_count,
    text_len,
):
    tok_dev = q_raw.shape[1]
    tiles_dev = nbr.shape[0]
    tile_len = tok_dev // tiles_dev
    n_frame = lax.axis_size("frame")

    kv_own = jnp.stack([k_raw, v_in])
    kv_prev1 = from_behind(kv_own, "frame", 1)
    kv_next1 = from_behind(kv_own, "frame", -1)
    kv_prev2 = from_behind(kv_prev1, "frame", 1)
    kv_next2 = from_behind(kv_next1, "frame", -1)

    q_total, k_total, cross_total, text_total = lax.psum(
        (squares(q_raw), squares(k_raw), squares(cross_q_raw), squares(text_k_raw)), "head"
    )
    tot_prev1 = from_behind(k_total, "frame", 1)
    tot_next1 = from_behind(k_total, "frame", -1)
    tot_prev2 = from_behind(tot_prev1, "frame", 1)
    tot_next2 = from_behind(tot_next1, "frame", -1)

    text_local = scaled(text_k_raw, text_total, text_k_gain)
    held = jnp.stack([text_local, text_v])[:, :, None]
    held, kv_prev1, kv_next1 = lax.optimization_barrier((held, kv_prev1, kv_next1))
    me = lax.axis_index("frame")
    order = [4, 2, 1, 32, 16, 8]
    order = [b for b in order if b < n_frame]
    for bit in order:
        got = swap_with(held, "frame", bit)
        upper = (me & bit) != 0
        low = jnp.where(upper, got, held)
        high = jnp.where(upper, held, got)
        held = jnp.concatenate([low, high], axis=2)
    steps = len(order)
    txt_rows = held.shape[3]
    held = held.reshape((2, 2) + (2,) * steps + held.shape[3:])
    bits_sorted = sorted(order, reverse=True)
    pos_of = {b: steps - 1 - i for i, b in enumerate(order)}
    perm = [0, 1] + [2 + pos_of[b] for b in bits_sorted] + [2 + steps, 3 + steps]
    held = jnp.transpose(held, perm).reshape(2, 2, n_frame * txt_rows, held.shape[-1])
    text_keys, text_values = held[0], held[1]

    queries = scaled(q_raw, q_total, q_gain)
    cross_queries = scaled(cross_q_raw, cross_total, cross_q_gain)

    text_total_len = text_keys.shape[1]
    text_mask = (
        jnp.arange(text_total_len, dtype=jnp.int32)[None, :] < text_len[:, None]
    ).astype(jnp.int32)[:, None, :]
    cross_out = attend(cross_queries, text_keys, text_values, text_mask, True, tile_len)
    cross_out, kv_prev2, kv_next2 = lax.optimization_barrier((cross_out, kv_prev2, kv_next2))

    kv_all = jnp.concatenate([kv_prev2, kv_prev1, kv_own, kv_next1, kv_next2], axis=2)
    tot_all = jnp.concatenate([tot_prev2, tot_prev1, k_total, tot_next1, tot_next2], axis=1)
    keys_all = scaled(kv_all[0], tot_all, k_gain)
    values_all = kv_all[1]

    slots_total = (2 * REACH + 1) * tiles_dev
    first_tile = (me - REACH) * tiles_dev
    cand = first_tile + jnp.arange(slots_total, dtype=jnp.int32)
    live_slot = jnp.arange(NB, dtype=jnp.int32)[None, :] < nbr_count[:, None]
    hit = (nbr[:, :, None] == cand[None, None, :]) & live_slot[:, :, None]
    live = jnp.any(hit, axis=1)
    self_mask = jnp.repeat(live.astype(jnp.int32), tile_len, axis=1)[:, None, :]
    self_out = attend(queries, keys_all, values_all, self_mask, False, tile_len)
    return (self_out, cross_out)


def solution(mesh):
    in_specs = (
        P(None, "frame", "head"),
        P(None, "frame", "head"),
        P(None, "frame", "head"),
        P(None, "frame", "head"),
        P(None, "frame", "head"),
        P(None, "frame", "head"),
        P("head"),
        P("head"),
        P("head"),
        P("head"),
        P("frame", None),
        P("frame"),
        P(),
    )
    out_specs = (P(None, "frame", "head"), P(None, "frame", "head"))
    return jax.shard_map(body, mesh=mesh, in_specs=in_specs, out_specs=out_specs, check_vma=False)
```

```python
import functools
import math

import jax
import jax.numpy as jnp
import numpy as np
from jax import lax
from jax.experimental import pallas as pl
from jax.experimental.pallas import tpu as pltpu
from jax.sharding import PartitionSpec as P

D = 5120
HD = 128
NB = 14
REACH = 2
MESH = pl.DeviceIdType.MESH

EPSILON = 1e-06

TEXT_BITS = (4, 2, 1, 32, 16, 8)


def text_bits(n_frame):
    return [b for b in TEXT_BITS if b < n_frame]


def squares(tensor):
    values = tensor.astype(jnp.float32)
    return jnp.sum(values * values, axis=-1)


def factor_of(totals):
    return lax.rsqrt(totals / D + EPSILON)[..., None]


def exchange_kernel(kv_own, text_own, kv_nb, text_all, kv_send, kv_recv, tx_send, tx_recv, local_sem,
                    *, n_frame, bits, rows):
    f = lax.axis_index("frame")
    h = lax.axis_index("head")
    has_prev = f >= 1
    has_next = f <= n_frame - 2

    barrier = pltpu.get_barrier_semaphore()

    @pl.when(has_prev)
    def _():
        pl.semaphore_signal(barrier, inc=1, device_id=(f - 1, h), device_id_type=MESH)

    @pl.when(has_next)
    def _():
        pl.semaphore_signal(barrier, inc=1, device_id=(f + 1, h), device_id_type=MESH)

    for b in bits:
        pl.semaphore_signal(barrier, inc=1, device_id=(f ^ b, h), device_id_type=MESH)
    peers = len(bits) + has_prev.astype(jnp.int32) + has_next.astype(jnp.int32)
    pl.semaphore_wait(barrier, peers)

    to_next = pltpu.make_async_remote_copy(
        src_ref=kv_own, dst_ref=kv_nb.at[1], send_sem=kv_send.at[0], recv_sem=kv_recv.at[1],
        device_id=(f + 1, h), device_id_type=MESH)
    to_prev = pltpu.make_async_remote_copy(
        src_ref=kv_own, dst_ref=kv_nb.at[2], send_sem=kv_send.at[1], recv_sem=kv_recv.at[2],
        device_id=(f - 1, h), device_id_type=MESH)

    @pl.when(has_next)
    def _():
        to_next.start()

    @pl.when(has_prev)
    def _():
        to_prev.start()

    pos = 0
    for i, b in enumerate(bits):
        pos = pos + ((f // b) % 2) * (1 << i)
    mine = pltpu.make_async_copy(
        text_own, text_all.at[:, pl.ds(pl.multiple_of(pos * rows, rows), rows)], local_sem.at[0])
    mine.start()
    mine.wait()
    for i, b in enumerate(bits):
        size = rows << i
        start = pl.multiple_of((pos >> i) * size, size)
        swap = pltpu.make_async_remote_copy(
            src_ref=text_all.at[:, pl.ds(start, size)], dst_ref=text_all.at[:, pl.ds(start, size)],
            send_sem=tx_send.at[i], recv_sem=tx_recv.at[i], device_id=(f ^ b, h), device_id_type=MESH)
        swap.start()
        swap.wait_send()
        swap.wait_recv()

    @pl.when(has_next)
    def _():
        to_next.wait_send()
        to_prev.wait_recv()

    @pl.when(has_prev)
    def _():
        to_prev.wait_send()
        to_next.wait_recv()

    fwd_next = pltpu.make_async_remote_copy(
        src_ref=kv_nb.at[1], dst_ref=kv_nb.at[0], send_sem=kv_send.at[2], recv_sem=kv_recv.at[0],
        device_id=(f + 1, h), device_id_type=MESH)
    fwd_prev = pltpu.make_async_remote_copy(
        src_ref=kv_nb.at[2], dst_ref=kv_nb.at[3], send_sem=kv_send.at[3], recv_sem=kv_recv.at[3],
        device_id=(f - 1, h), device_id_type=MESH)
    both = jnp.logical_and(has_prev, has_next)

    @pl.when(both)
    def _():
        fwd_next.start()
        fwd_prev.start()

    @pl.when(f >= 2)
    def _():
        fwd_next.wait_recv()

    @pl.when(f <= n_frame - 3)
    def _():
        fwd_prev.wait_recv()

    @pl.when(both)
    def _():
        fwd_next.wait_send()
        fwd_prev.wait_send()


def exchange(kv_own, text_own, n_frame):
    bits = text_bits(n_frame)
    rows = text_own.shape[1]
    return pl.pallas_call(
        functools.partial(exchange_kernel, n_frame=n_frame, bits=bits, rows=rows),
        out_shape=(
            jax.ShapeDtypeStruct((4,) + kv_own.shape, kv_own.dtype),
            jax.ShapeDtypeStruct((text_own.shape[0], rows * n_frame, text_own.shape[2]), text_own.dtype),
        ),
        in_specs=[pl.BlockSpec(memory_space=pl.ANY)] * 2,
        out_specs=(pl.BlockSpec(memory_space=pl.ANY), pl.BlockSpec(memory_space=pl.ANY)),
        scratch_shapes=[
            pltpu.SemaphoreType.DMA((4,)),
            pltpu.SemaphoreType.DMA((4,)),
            pltpu.SemaphoreType.DMA((len(bits),)),
            pltpu.SemaphoreType.DMA((len(bits),)),
            pltpu.SemaphoreType.DMA((1,)),
        ],
        compiler_params=pltpu.CompilerParams(collective_id=0, has_side_effects=True),
    )(kv_own, text_own)


def softmax_rows(scores):
    row_top = jnp.max(scores, axis=-1, keepdims=True)
    powers = jnp.exp(scores - row_top)
    inverse = 1.0 / jnp.sum(powers, axis=-1, keepdims=True)
    return (powers * inverse).astype(jnp.bfloat16)


def normalized(raw, fac, gain):
    return (raw.astype(jnp.float32) * fac * gain).astype(jnp.bfloat16)


def self_kernel(q_ref, qf_ref, qg_ref, kf_ref, kg_ref, mask_ref, ok_ref, *refs, score_scale, tiles, slots):
    k_refs = refs[:slots]
    v_refs = refs[slots:2 * slots]
    o_ref = refs[2 * slots]
    q = normalized(q_ref[0], qf_ref[0], qg_ref[...])
    span = q.shape[0]
    kg = kg_ref[...]
    parts = []
    for j in range(slots):
        k = normalized(k_refs[j][0], kf_ref[0, j], kg)
        parts.append(lax.dot_general(q, k, (((1,), (1,)), ((), ())), preferred_element_type=jnp.float32))
    scores = jnp.concatenate(parts, axis=1) * score_scale
    key_len = scores.shape[1]
    scores = scores.reshape(tiles, span // tiles, key_len)
    scores = jnp.where(mask_ref[...] > 0, scores, -1e30)
    weights = softmax_rows(scores).reshape(span, key_len)
    out = None
    for j in range(slots):
        v = jnp.where(ok_ref[j:j + 1, :] > 0, v_refs[j][0], jnp.zeros((), v_refs[j].dtype))
        part = jnp.dot(weights[:, j * span:(j + 1) * span], v, preferred_element_type=jnp.float32)
        out = part if out is None else out + part
    o_ref[0] = out.astype(o_ref.dtype)


def cross_kernel(q_ref, qf_ref, qg_ref, k_ref, kf_ref, kg_ref, v_ref, mask_ref, o_ref, *, score_scale):
    q = normalized(q_ref[0], qf_ref[0], qg_ref[...])
    k = normalized(k_ref[0], kf_ref[0], kg_ref[...])
    scores = lax.dot_general(q, k, (((1,), (1,)), ((), ())), preferred_element_type=jnp.float32)
    scores = jnp.where(mask_ref[0] > 0, scores * score_scale, -1e30)
    weights = softmax_rows(scores)
    out = jnp.dot(weights, v_ref[0], preferred_element_type=jnp.float32)
    o_ref[0] = out.astype(o_ref.dtype)


def body(
    q_raw,
    k_raw,
    v_in,
    cross_q_raw,
    text_k_raw,
    text_v,
    q_gain,
    k_gain,
    cross_q_gain,
    text_k_gain,
    nbr,
    nbr_count,
    text_len,
):
    rows_c, tok_dev, width = q_raw.shape
    groups = width // HD
    tiles_dev = nbr.shape[0]
    tile_len = tok_dev // tiles_dev
    n_frame = lax.axis_size("frame")
    me = lax.axis_index("frame")
    score_scale = 1.0 / math.sqrt(HD)
    slots = 2 * REACH + 1

    kv_own = jnp.stack([k_raw, v_in])
    txt_rows = text_k_raw.shape[1]
    text_own = jnp.stack([text_k_raw, text_v]).reshape(2 * rows_c, txt_rows, width)
    kv_nb, text_all = exchange(kv_own, text_own, n_frame)
    text_all = text_all.reshape(2, rows_c, n_frame * txt_rows, width)

    k_nb_sq = squares(kv_nb[:, 0])
    q_total, k_total, k_nb_total, cross_total, text_total = lax.psum(
        (squares(q_raw), squares(k_raw), k_nb_sq, squares(cross_q_raw), squares(text_all[0])), "head"
    )
    k_fac = factor_of(
        jnp.stack([k_nb_total[0], k_nb_total[1], k_total, k_nb_total[2], k_nb_total[3]], axis=1)
    )

    bits = text_bits(n_frame)
    frame_of_pos = np.zeros(n_frame, np.int32)
    for p in range(n_frame):
        frame_of_pos[p] = sum(b for i, b in enumerate(bits) if (p >> i) & 1)
    token_of_row = (frame_of_pos[:, None] * txt_rows + np.arange(txt_rows)[None, :]).reshape(-1)
    text_mask = (jnp.asarray(token_of_row)[None, :] < text_len[:, None]).astype(jnp.int32)[:, None, :]

    text_len_all = n_frame * txt_rows
    cross_out = pl.pallas_call(
        functools.partial(cross_kernel, score_scale=score_scale),
        out_shape=jax.ShapeDtypeStruct(q_raw.shape, jnp.bfloat16),
        grid=(rows_c, groups),
        in_specs=[
            pl.BlockSpec((1, tok_dev, HD), lambda c, h: (c, 0, h)),
            pl.BlockSpec((1, tok_dev, 1), lambda c, h: (c, 0, 0)),
            pl.BlockSpec((1, HD), lambda c, h: (0, h)),
            pl.BlockSpec((1, text_len_all, HD), lambda c, h: (c, 0, h)),
            pl.BlockSpec((1, text_len_all, 1), lambda c, h: (c, 0, 0)),
            pl.BlockSpec((1, HD), lambda c, h: (0, h)),
            pl.BlockSpec((1, text_len_all, HD), lambda c, h: (c, 0, h)),
            pl.BlockSpec((1, 1, text_len_all), lambda c, h: (c, 0, 0)),
        ],
        out_specs=pl.BlockSpec((1, tok_dev, HD), lambda c, h: (c, 0, h)),
        cost_estimate=pl.CostEstimate(
            flops=4 * rows_c * tok_dev * text_len_all * width,
            transcendentals=rows_c * tok_dev * text_len_all * groups,
            bytes_accessed=4 * q_raw.size + 4 * text_all[0].size,
        ),
    )(
        cross_q_raw, factor_of(cross_total), cross_q_gain.reshape(1, width),
        text_all[0], factor_of(text_total), text_k_gain.reshape(1, width),
        text_all[1], text_mask,
    )

    first_tile = (me - REACH) * tiles_dev
    cand = first_tile + jnp.arange(slots * tiles_dev, dtype=jnp.int32)
    live_slot = jnp.arange(NB, dtype=jnp.int32)[None, :] < nbr_count[:, None]
    hit = (nbr[:, :, None] == cand[None, None, :]) & live_slot[:, :, None]
    live = jnp.any(hit, axis=1)
    self_mask = jnp.repeat(live.astype(jnp.int32), tile_len, axis=1)[:, None, :]
    shard_of_slot = me - REACH + jnp.arange(8, dtype=jnp.int32)
    slot_ok = (shard_of_slot >= 0) & (shard_of_slot < n_frame)
    slot_ok = jnp.broadcast_to(slot_ok.astype(jnp.int32)[:, None], (8, 128))

    nb_index = {0: 0, 1: 1, 3: 2, 4: 3}
    k_specs, v_specs, k_args, v_args = [], [], [], []
    for j in range(slots):
        if j == REACH:
            k_specs.append(pl.BlockSpec((1, tok_dev, HD), lambda c, h: (c, 0, h)))
            v_specs.append(pl.BlockSpec((1, tok_dev, HD), lambda c, h: (c, 0, h)))
            k_args.append(k_raw)
            v_args.append(v_in)
        else:
            s = nb_index[j]
            k_specs.append(pl.BlockSpec((None, None, 1, tok_dev, HD), lambda c, h, s=s: (s, 0, c, 0, h)))
            v_specs.append(pl.BlockSpec((None, None, 1, tok_dev, HD), lambda c, h, s=s: (s, 1, c, 0, h)))
            k_args.append(kv_nb)
            v_args.append(kv_nb)

    key_len = slots * tok_dev
    self_out = pl.pallas_call(
        functools.partial(self_kernel, score_scale=score_scale, tiles=tiles_dev, slots=slots),
        out_shape=jax.ShapeDtypeStruct(q_raw.shape, jnp.bfloat16),
        grid=(rows_c, groups),
        in_specs=[
            pl.BlockSpec((1, tok_dev, HD), lambda c, h: (c, 0, h)),
            pl.BlockSpec((1, tok_dev, 1), lambda c, h: (c, 0, 0)),
            pl.BlockSpec((1, HD), lambda c, h: (0, h)),
            pl.BlockSpec((1, slots, tok_dev, 1), lambda c, h: (c, 0, 0, 0)),
            pl.BlockSpec((1, HD), lambda c, h: (0, h)),
            pl.BlockSpec((tiles_dev, 1, key_len), lambda c, h: (0, 0, 0)),
            pl.BlockSpec((8, 128), lambda c, h: (0, 0)),
        ] + k_specs + v_specs,
        out_specs=pl.BlockSpec((1, tok_dev, HD), lambda c, h: (c, 0, h)),
        cost_estimate=pl.CostEstimate(
            flops=4 * rows_c * tok_dev * key_len * width,
            transcendentals=rows_c * tok_dev * key_len * groups,
            bytes_accessed=4 * q_raw.size + 4 * slots * k_raw.size,
        ),
    )(
        q_raw, factor_of(q_total), q_gain.reshape(1, width), k_fac, k_gain.reshape(1, width),
        self_mask, slot_ok, *k_args, *v_args,
    )
    return (self_out, cross_out)


def solution(mesh):
    in_specs = (
        P(None, "frame", "head"),
        P(None, "frame", "head"),
        P(None, "frame", "head"),
        P(None, "frame", "head"),
        P(None, "frame", "head"),
        P(None, "frame", "head"),
        P("head"),
        P("head"),
        P("head"),
        P("head"),
        P("frame", None),
        P("frame"),
        P(),
    )
    out_specs = (P(None, "frame", "head"), P(None, "frame", "head"))
    return jax.shard_map(body, mesh=mesh, in_specs=in_specs, out_specs=out_specs, check_vma=False)
```

```python
import functools
import math

import jax
import jax.numpy as jnp
import numpy as np
from jax import lax
from jax.experimental import pallas as pl
from jax.experimental.pallas import tpu as pltpu
from jax.sharding import PartitionSpec as P

D = 5120
HD = 128
NB = 14
REACH = 2
MESH = pl.DeviceIdType.MESH

EPSILON = 1e-06

TEXT_BITS = (4, 2, 1, 32, 16, 8)
EARLY_TEXT_STEPS = 4


def text_bits(n_frame):
    return [b for b in TEXT_BITS if b < n_frame]


def squares(tensor):
    values = tensor.astype(jnp.float32)
    return jnp.sum(values * values, axis=-1)


def factor_of(totals):
    return lax.rsqrt(totals / D + EPSILON)[..., None]


def exchange_kernel(kv_own, text_own, kv_nb, text_all, kv_send, kv_recv, tx_send, tx_recv, local_sem,
                    *, n_frame, bits, rows):
    f = lax.axis_index("frame")
    h = lax.axis_index("head")
    has_prev = f >= 1
    has_next = f <= n_frame - 2

    barrier = pltpu.get_barrier_semaphore()

    @pl.when(has_prev)
    def _():
        pl.semaphore_signal(barrier, inc=1, device_id=(f - 1, h), device_id_type=MESH)

    @pl.when(has_next)
    def _():
        pl.semaphore_signal(barrier, inc=1, device_id=(f + 1, h), device_id_type=MESH)

    for b in bits:
        pl.semaphore_signal(barrier, inc=1, device_id=(f ^ b, h), device_id_type=MESH)
    peers = len(bits) + has_prev.astype(jnp.int32) + has_next.astype(jnp.int32)
    pl.semaphore_wait(barrier, peers)

    to_next = pltpu.make_async_remote_copy(
        src_ref=kv_own, dst_ref=kv_nb.at[1], send_sem=kv_send.at[0], recv_sem=kv_recv.at[1],
        device_id=(f + 1, h), device_id_type=MESH)
    to_prev = pltpu.make_async_remote_copy(
        src_ref=kv_own, dst_ref=kv_nb.at[2], send_sem=kv_send.at[1], recv_sem=kv_recv.at[2],
        device_id=(f - 1, h), device_id_type=MESH)

    @pl.when(has_next)
    def _():
        to_next.start()

    @pl.when(has_prev)
    def _():
        to_prev.start()

    pos = 0
    for i, b in enumerate(bits):
        pos = pos + ((f // b) % 2) * (1 << i)
    mine = pltpu.make_async_copy(
        text_own, text_all.at[:, pl.ds(pl.multiple_of(pos * rows, rows), rows)], local_sem.at[0])
    mine.start()
    mine.wait()
    def text_step(i, b):
        size = rows << i
        start = pl.multiple_of((pos >> i) * size, size)
        swap = pltpu.make_async_remote_copy(
            src_ref=text_all.at[:, pl.ds(start, size)], dst_ref=text_all.at[:, pl.ds(start, size)],
            send_sem=tx_send.at[i], recv_sem=tx_recv.at[i], device_id=(f ^ b, h), device_id_type=MESH)
        swap.start()
        swap.wait_send()
        swap.wait_recv()

    early = min(EARLY_TEXT_STEPS, len(bits))
    for i in range(early):
        text_step(i, bits[i])

    @pl.when(has_next)
    def _():
        to_next.wait_send()
        to_prev.wait_recv()

    @pl.when(has_prev)
    def _():
        to_prev.wait_send()
        to_next.wait_recv()

    fwd_next = pltpu.make_async_remote_copy(
        src_ref=kv_nb.at[1], dst_ref=kv_nb.at[0], send_sem=kv_send.at[2], recv_sem=kv_recv.at[0],
        device_id=(f + 1, h), device_id_type=MESH)
    fwd_prev = pltpu.make_async_remote_copy(
        src_ref=kv_nb.at[2], dst_ref=kv_nb.at[3], send_sem=kv_send.at[3], recv_sem=kv_recv.at[3],
        device_id=(f - 1, h), device_id_type=MESH)
    both = jnp.logical_and(has_prev, has_next)

    @pl.when(both)
    def _():
        fwd_next.start()
        fwd_prev.start()

    for i in range(early, len(bits)):
        text_step(i, bits[i])

    @pl.when(f >= 2)
    def _():
        fwd_next.wait_recv()

    @pl.when(f <= n_frame - 3)
    def _():
        fwd_prev.wait_recv()

    @pl.when(both)
    def _():
        fwd_next.wait_send()
        fwd_prev.wait_send()


def exchange(kv_own, text_own, n_frame):
    bits = text_bits(n_frame)
    rows = text_own.shape[1]
    return pl.pallas_call(
        functools.partial(exchange_kernel, n_frame=n_frame, bits=bits, rows=rows),
        out_shape=(
            jax.ShapeDtypeStruct((4,) + kv_own.shape, kv_own.dtype),
            jax.ShapeDtypeStruct((text_own.shape[0], rows * n_frame, text_own.shape[2]), text_own.dtype),
        ),
        in_specs=[pl.BlockSpec(memory_space=pl.ANY)] * 2,
        out_specs=(pl.BlockSpec(memory_space=pl.ANY), pl.BlockSpec(memory_space=pl.ANY)),
        scratch_shapes=[
            pltpu.SemaphoreType.DMA((4,)),
            pltpu.SemaphoreType.DMA((4,)),
            pltpu.SemaphoreType.DMA((len(bits),)),
            pltpu.SemaphoreType.DMA((len(bits),)),
            pltpu.SemaphoreType.DMA((1,)),
        ],
        compiler_params=pltpu.CompilerParams(collective_id=0, has_side_effects=True),
    )(kv_own, text_own)


def softmax_rows(scores):
    row_top = jnp.max(scores, axis=-1, keepdims=True)
    powers = jnp.exp(scores - row_top)
    inverse = 1.0 / jnp.sum(powers, axis=-1, keepdims=True)
    return (powers * inverse).astype(jnp.bfloat16)


def normalized(raw, fac, gain):
    return (raw.astype(jnp.float32) * fac * gain).astype(jnp.bfloat16)


def self_kernel(q_ref, qf_ref, qg_ref, kf_ref, kg_ref, mask_ref, ok_ref, *refs, score_scale, tiles, slots):
    k_refs = refs[:slots]
    v_refs = refs[slots:2 * slots]
    o_ref = refs[2 * slots]
    q = normalized(q_ref[0], qf_ref[0], qg_ref[...])
    span = q.shape[0]
    kg = kg_ref[...]
    parts = []
    for j in range(slots):
        k = normalized(k_refs[j][0], kf_ref[0, j], kg)
        parts.append(lax.dot_general(q, k, (((1,), (1,)), ((), ())), preferred_element_type=jnp.float32))
    scores = jnp.concatenate(parts, axis=1) * score_scale
    key_len = scores.shape[1]
    scores = scores.reshape(tiles, span // tiles, key_len)
    scores = jnp.where(mask_ref[...] > 0, scores, -1e30)
    weights = softmax_rows(scores).reshape(span, key_len)
    out = None
    for j in range(slots):
        v = jnp.where(ok_ref[j:j + 1, :] > 0, v_refs[j][0], jnp.zeros((), v_refs[j].dtype))
        part = jnp.dot(weights[:, j * span:(j + 1) * span], v, preferred_element_type=jnp.float32)
        out = part if out is None else out + part
    o_ref[0] = out.astype(o_ref.dtype)


def cross_kernel(q_ref, qf_ref, qg_ref, k_ref, kf_ref, kg_ref, v_ref, mask_ref, o_ref, *, score_scale):
    q = normalized(q_ref[0], qf_ref[0], qg_ref[...])
    k = normalized(k_ref[0], kf_ref[0], kg_ref[...])
    scores = lax.dot_general(q, k, (((1,), (1,)), ((), ())), preferred_element_type=jnp.float32)
    scores = jnp.where(mask_ref[0] > 0, scores * score_scale, -1e30)
    weights = softmax_rows(scores)
    out = jnp.dot(weights, v_ref[0], preferred_element_type=jnp.float32)
    o_ref[0] = out.astype(o_ref.dtype)


def body(
    q_raw,
    k_raw,
    v_in,
    cross_q_raw,
    text_k_raw,
    text_v,
    q_gain,
    k_gain,
    cross_q_gain,
    text_k_gain,
    nbr,
    nbr_count,
    text_len,
):
    rows_c, tok_dev, width = q_raw.shape
    groups = width // HD
    tiles_dev = nbr.shape[0]
    tile_len = tok_dev // tiles_dev
    n_frame = lax.axis_size("frame")
    me = lax.axis_index("frame")
    score_scale = 1.0 / math.sqrt(HD)
    slots = 2 * REACH + 1

    kv_own = jnp.stack([k_raw, v_in])
    txt_rows = text_k_raw.shape[1]
    text_own = jnp.stack([text_k_raw, text_v]).reshape(2 * rows_c, txt_rows, width)
    kv_nb, text_all = exchange(kv_own, text_own, n_frame)
    text_all = text_all.reshape(2, rows_c, n_frame * txt_rows, width)

    k_nb_sq = squares(kv_nb[:, 0])
    q_total, k_total, k_nb_total, cross_total, text_total = lax.psum(
        (squares(q_raw), squares(k_raw), k_nb_sq, squares(cross_q_raw), squares(text_all[0])), "head"
    )
    k_fac = factor_of(
        jnp.stack([k_nb_total[0], k_nb_total[1], k_total, k_nb_total[2], k_nb_total[3]], axis=1)
    )

    bits = text_bits(n_frame)
    frame_of_pos = np.zeros(n_frame, np.int32)
    for p in range(n_frame):
        frame_of_pos[p] = sum(b for i, b in enumerate(bits) if (p >> i) & 1)
    token_of_row = (frame_of_pos[:, None] * txt_rows + np.arange(txt_rows)[None, :]).reshape(-1)
    text_mask = (jnp.asarray(token_of_row)[None, :] < text_len[:, None]).astype(jnp.int32)[:, None, :]

    text_len_all = n_frame * txt_rows
    cross_out = pl.pallas_call(
        functools.partial(cross_kernel, score_scale=score_scale),
        out_shape=jax.ShapeDtypeStruct(q_raw.shape, jnp.bfloat16),
        grid=(rows_c, groups),
        in_specs=[
            pl.BlockSpec((1, tok_dev, HD), lambda c, h: (c, 0, h)),
            pl.BlockSpec((1, tok_dev, 1), lambda c, h: (c, 0, 0)),
            pl.BlockSpec((1, HD), lambda c, h: (0, h)),
            pl.BlockSpec((1, text_len_all, HD), lambda c, h: (c, 0, h)),
            pl.BlockSpec((1, text_len_all, 1), lambda c, h: (c, 0, 0)),
            pl.BlockSpec((1, HD), lambda c, h: (0, h)),
            pl.BlockSpec((1, text_len_all, HD), lambda c, h: (c, 0, h)),
            pl.BlockSpec((1, 1, text_len_all), lambda c, h: (c, 0, 0)),
        ],
        out_specs=pl.BlockSpec((1, tok_dev, HD), lambda c, h: (c, 0, h)),
        cost_estimate=pl.CostEstimate(
            flops=4 * rows_c * tok_dev * text_len_all * width,
            transcendentals=rows_c * tok_dev * text_len_all * groups,
            bytes_accessed=4 * q_raw.size + 4 * text_all[0].size,
        ),
    )(
        cross_q_raw, factor_of(cross_total), cross_q_gain.reshape(1, width),
        text_all[0], factor_of(text_total), text_k_gain.reshape(1, width),
        text_all[1], text_mask,
    )

    first_tile = (me - REACH) * tiles_dev
    cand = first_tile + jnp.arange(slots * tiles_dev, dtype=jnp.int32)
    live_slot = jnp.arange(NB, dtype=jnp.int32)[None, :] < nbr_count[:, None]
    hit = (nbr[:, :, None] == cand[None, None, :]) & live_slot[:, :, None]
    live = jnp.any(hit, axis=1)
    self_mask = jnp.repeat(live.astype(jnp.int32), tile_len, axis=1)[:, None, :]
    shard_of_slot = me - REACH + jnp.arange(8, dtype=jnp.int32)
    slot_ok = (shard_of_slot >= 0) & (shard_of_slot < n_frame)
    slot_ok = jnp.broadcast_to(slot_ok.astype(jnp.int32)[:, None], (8, 128))

    nb_index = {0: 0, 1: 1, 3: 2, 4: 3}
    k_specs, v_specs, k_args, v_args = [], [], [], []
    for j in range(slots):
        if j == REACH:
            k_specs.append(pl.BlockSpec((1, tok_dev, HD), lambda c, h: (c, 0, h)))
            v_specs.append(pl.BlockSpec((1, tok_dev, HD), lambda c, h: (c, 0, h)))
            k_args.append(k_raw)
            v_args.append(v_in)
        else:
            s = nb_index[j]
            k_specs.append(pl.BlockSpec((None, None, 1, tok_dev, HD), lambda c, h, s=s: (s, 0, c, 0, h)))
            v_specs.append(pl.BlockSpec((None, None, 1, tok_dev, HD), lambda c, h, s=s: (s, 1, c, 0, h)))
            k_args.append(kv_nb)
            v_args.append(kv_nb)

    key_len = slots * tok_dev
    self_out = pl.pallas_call(
        functools.partial(self_kernel, score_scale=score_scale, tiles=tiles_dev, slots=slots),
        out_shape=jax.ShapeDtypeStruct(q_raw.shape, jnp.bfloat16),
        grid=(rows_c, groups),
        in_specs=[
            pl.BlockSpec((1, tok_dev, HD), lambda c, h: (c, 0, h)),
            pl.BlockSpec((1, tok_dev, 1), lambda c, h: (c, 0, 0)),
            pl.BlockSpec((1, HD), lambda c, h: (0, h)),
            pl.BlockSpec((1, slots, tok_dev, 1), lambda c, h: (c, 0, 0, 0)),
            pl.BlockSpec((1, HD), lambda c, h: (0, h)),
            pl.BlockSpec((tiles_dev, 1, key_len), lambda c, h: (0, 0, 0)),
            pl.BlockSpec((8, 128), lambda c, h: (0, 0)),
        ] + k_specs + v_specs,
        out_specs=pl.BlockSpec((1, tok_dev, HD), lambda c, h: (c, 0, h)),
        cost_estimate=pl.CostEstimate(
            flops=4 * rows_c * tok_dev * key_len * width,
            transcendentals=rows_c * tok_dev * key_len * groups,
            bytes_accessed=4 * q_raw.size + 4 * slots * k_raw.size,
        ),
    )(
        q_raw, factor_of(q_total), q_gain.reshape(1, width), k_fac, k_gain.reshape(1, width),
        self_mask, slot_ok, *k_args, *v_args,
    )
    return (self_out, cross_out)


def solution(mesh):
    in_specs = (
        P(None, "frame", "head"),
        P(None, "frame", "head"),
        P(None, "frame", "head"),
        P(None, "frame", "head"),
        P(None, "frame", "head"),
        P(None, "frame", "head"),
        P("head"),
        P("head"),
        P("head"),
        P("head"),
        P("frame", None),
        P("frame"),
        P(),
    )
    out_specs = (P(None, "frame", "head"), P(None, "frame", "head"))
    return jax.shard_map(body, mesh=mesh, in_specs=in_specs, out_specs=out_specs, check_vma=False)
```

```python
import functools
import math

import jax
import jax.numpy as jnp
import numpy as np
from jax import lax
from jax.experimental import pallas as pl
from jax.experimental.pallas import tpu as pltpu
from jax.sharding import PartitionSpec as P

D = 5120
HD = 128
NB = 14
REACH = 2
MESH = pl.DeviceIdType.MESH

EPSILON = 1e-06

TEXT_BITS = (4, 2, 32, 16, 8, 1)
EARLY_TEXT_STEPS = 4


def text_bits(n_frame):
    return [b for b in TEXT_BITS if b < n_frame]


def squares(tensor):
    values = tensor.astype(jnp.float32)
    return jnp.sum(values * values, axis=-1)


def factor_of(totals):
    return lax.rsqrt(totals / D + EPSILON)[..., None]


def exchange_kernel(kv_own, text_own, kv_nb, text_all, kv_send, kv_recv, tx_send, tx_recv, local_sem,
                    *, n_frame, bits, rows):
    f = lax.axis_index("frame")
    h = lax.axis_index("head")
    has_prev = f >= 1
    has_next = f <= n_frame - 2

    barrier = pltpu.get_barrier_semaphore()

    @pl.when(has_prev)
    def _():
        pl.semaphore_signal(barrier, inc=1, device_id=(f - 1, h), device_id_type=MESH)

    @pl.when(has_next)
    def _():
        pl.semaphore_signal(barrier, inc=1, device_id=(f + 1, h), device_id_type=MESH)

    for b in bits:
        pl.semaphore_signal(barrier, inc=1, device_id=(f ^ b, h), device_id_type=MESH)
    peers = len(bits) + has_prev.astype(jnp.int32) + has_next.astype(jnp.int32)
    pl.semaphore_wait(barrier, peers)

    to_next = pltpu.make_async_remote_copy(
        src_ref=kv_own, dst_ref=kv_nb.at[1], send_sem=kv_send.at[0], recv_sem=kv_recv.at[1],
        device_id=(f + 1, h), device_id_type=MESH)
    to_prev = pltpu.make_async_remote_copy(
        src_ref=kv_own, dst_ref=kv_nb.at[2], send_sem=kv_send.at[1], recv_sem=kv_recv.at[2],
        device_id=(f - 1, h), device_id_type=MESH)

    @pl.when(has_next)
    def _():
        to_next.start()

    @pl.when(has_prev)
    def _():
        to_prev.start()

    pos = 0
    for i, b in enumerate(bits):
        pos = pos + ((f // b) % 2) * (1 << i)
    mine = pltpu.make_async_copy(
        text_own, text_all.at[:, pl.ds(pl.multiple_of(pos * rows, rows), rows)], local_sem.at[0])
    mine.start()
    mine.wait()
    def text_step(i, b):
        size = rows << i
        start = pl.multiple_of((pos >> i) * size, size)
        swap = pltpu.make_async_remote_copy(
            src_ref=text_all.at[:, pl.ds(start, size)], dst_ref=text_all.at[:, pl.ds(start, size)],
            send_sem=tx_send.at[i], recv_sem=tx_recv.at[i], device_id=(f ^ b, h), device_id_type=MESH)
        swap.start()
        swap.wait_send()
        swap.wait_recv()

    early = min(EARLY_TEXT_STEPS, len(bits))
    for i in range(early):
        text_step(i, bits[i])

    @pl.when(has_next)
    def _():
        to_next.wait_send()
        to_prev.wait_recv()

    @pl.when(has_prev)
    def _():
        to_prev.wait_send()
        to_next.wait_recv()

    fwd_next = pltpu.make_async_remote_copy(
        src_ref=kv_nb.at[1], dst_ref=kv_nb.at[0], send_sem=kv_send.at[2], recv_sem=kv_recv.at[0],
        device_id=(f + 1, h), device_id_type=MESH)
    fwd_prev = pltpu.make_async_remote_copy(
        src_ref=kv_nb.at[2], dst_ref=kv_nb.at[3], send_sem=kv_send.at[3], recv_sem=kv_recv.at[3],
        device_id=(f - 1, h), device_id_type=MESH)
    both = jnp.logical_and(has_prev, has_next)

    @pl.when(both)
    def _():
        fwd_next.start()
        fwd_prev.start()

    for i in range(early, len(bits)):
        text_step(i, bits[i])

    @pl.when(f >= 2)
    def _():
        fwd_next.wait_recv()

    @pl.when(f <= n_frame - 3)
    def _():
        fwd_prev.wait_recv()

    @pl.when(both)
    def _():
        fwd_next.wait_send()
        fwd_prev.wait_send()


def exchange(kv_own, text_own, n_frame):
    bits = text_bits(n_frame)
    rows = text_own.shape[1]
    return pl.pallas_call(
        functools.partial(exchange_kernel, n_frame=n_frame, bits=bits, rows=rows),
        out_shape=(
            jax.ShapeDtypeStruct((4,) + kv_own.shape, kv_own.dtype),
            jax.ShapeDtypeStruct((text_own.shape[0], rows * n_frame, text_own.shape[2]), text_own.dtype),
        ),
        in_specs=[pl.BlockSpec(memory_space=pl.ANY)] * 2,
        out_specs=(pl.BlockSpec(memory_space=pl.ANY), pl.BlockSpec(memory_space=pl.ANY)),
        scratch_shapes=[
            pltpu.SemaphoreType.DMA((4,)),
            pltpu.SemaphoreType.DMA((4,)),
            pltpu.SemaphoreType.DMA((len(bits),)),
            pltpu.SemaphoreType.DMA((len(bits),)),
            pltpu.SemaphoreType.DMA((1,)),
        ],
        compiler_params=pltpu.CompilerParams(collective_id=0, has_side_effects=True),
    )(kv_own, text_own)


def softmax_rows(scores):
    row_top = jnp.max(scores, axis=-1, keepdims=True)
    powers = jnp.exp(scores - row_top)
    inverse = 1.0 / jnp.sum(powers, axis=-1, keepdims=True)
    return (powers * inverse).astype(jnp.bfloat16)


def normalized(raw, fac, gain):
    return (raw.astype(jnp.float32) * fac * gain).astype(jnp.bfloat16)


def self_kernel(q_ref, qf_ref, qg_ref, kf_ref, kg_ref, mask_ref, ok_ref, *refs, score_scale, tiles, slots):
    k_refs = refs[:slots]
    v_refs = refs[slots:2 * slots]
    o_ref = refs[2 * slots]
    q = normalized(q_ref[0], qf_ref[0], qg_ref[...])
    span = q.shape[0]
    kg = kg_ref[...]
    parts = []
    for j in range(slots):
        k = normalized(k_refs[j][0], kf_ref[0, j], kg)
        parts.append(lax.dot_general(q, k, (((1,), (1,)), ((), ())), preferred_element_type=jnp.float32))
    scores = jnp.concatenate(parts, axis=1) * score_scale
    key_len = scores.shape[1]
    scores = scores.reshape(tiles, span // tiles, key_len)
    scores = jnp.where(mask_ref[...] > 0, scores, -1e30)
    weights = softmax_rows(scores).reshape(span, key_len)
    out = None
    for j in range(slots):
        v = jnp.where(ok_ref[j:j + 1, :] > 0, v_refs[j][0], jnp.zeros((), v_refs[j].dtype))
        part = jnp.dot(weights[:, j * span:(j + 1) * span], v, preferred_element_type=jnp.float32)
        out = part if out is None else out + part
    o_ref[0] = out.astype(o_ref.dtype)


def cross_kernel(q_ref, qf_ref, qg_ref, k_ref, kf_ref, kg_ref, v_ref, mask_ref, o_ref, *, score_scale):
    q = normalized(q_ref[0], qf_ref[0], qg_ref[...])
    k = normalized(k_ref[0], kf_ref[0], kg_ref[...])
    scores = lax.dot_general(q, k, (((1,), (1,)), ((), ())), preferred_element_type=jnp.float32)
    scores = jnp.where(mask_ref[0] > 0, scores * score_scale, -1e30)
    weights = softmax_rows(scores)
    out = jnp.dot(weights, v_ref[0], preferred_element_type=jnp.float32)
    o_ref[0] = out.astype(o_ref.dtype)


def body(
    q_raw,
    k_raw,
    v_in,
    cross_q_raw,
    text_k_raw,
    text_v,
    q_gain,
    k_gain,
    cross_q_gain,
    text_k_gain,
    nbr,
    nbr_count,
    text_len,
):
    rows_c, tok_dev, width = q_raw.shape
    groups = width // HD
    tiles_dev = nbr.shape[0]
    tile_len = tok_dev // tiles_dev
    n_frame = lax.axis_size("frame")
    me = lax.axis_index("frame")
    score_scale = 1.0 / math.sqrt(HD)
    slots = 2 * REACH + 1

    kv_own = jnp.stack([k_raw, v_in])
    txt_rows = text_k_raw.shape[1]
    text_own = jnp.stack([text_k_raw, text_v]).reshape(2 * rows_c, txt_rows, width)
    kv_nb, text_all = exchange(kv_own, text_own, n_frame)
    text_all = text_all.reshape(2, rows_c, n_frame * txt_rows, width)

    k_nb_sq = squares(kv_nb[:, 0])
    q_total, k_total, k_nb_total, cross_total, text_total = lax.psum(
        (squares(q_raw), squares(k_raw), k_nb_sq, squares(cross_q_raw), squares(text_all[0])), "head"
    )
    k_fac = factor_of(
        jnp.stack([k_nb_total[0], k_nb_total[1], k_total, k_nb_total[2], k_nb_total[3]], axis=1)
    )

    bits = text_bits(n_frame)
    frame_of_pos = np.zeros(n_frame, np.int32)
    for p in range(n_frame):
        frame_of_pos[p] = sum(b for i, b in enumerate(bits) if (p >> i) & 1)
    token_of_row = (frame_of_pos[:, None] * txt_rows + np.arange(txt_rows)[None, :]).reshape(-1)
    text_mask = (jnp.asarray(token_of_row)[None, :] < text_len[:, None]).astype(jnp.int32)[:, None, :]

    text_len_all = n_frame * txt_rows
    cross_out = pl.pallas_call(
        functools.partial(cross_kernel, score_scale=score_scale),
        out_shape=jax.ShapeDtypeStruct(q_raw.shape, jnp.bfloat16),
        grid=(rows_c, groups),
        in_specs=[
            pl.BlockSpec((1, tok_dev, HD), lambda c, h: (c, 0, h)),
            pl.BlockSpec((1, tok_dev, 1), lambda c, h: (c, 0, 0)),
            pl.BlockSpec((1, HD), lambda c, h: (0, h)),
            pl.BlockSpec((1, text_len_all, HD), lambda c, h: (c, 0, h)),
            pl.BlockSpec((1, text_len_all, 1), lambda c, h: (c, 0, 0)),
            pl.BlockSpec((1, HD), lambda c, h: (0, h)),
            pl.BlockSpec((1, text_len_all, HD), lambda c, h: (c, 0, h)),
            pl.BlockSpec((1, 1, text_len_all), lambda c, h: (c, 0, 0)),
        ],
        out_specs=pl.BlockSpec((1, tok_dev, HD), lambda c, h: (c, 0, h)),
        cost_estimate=pl.CostEstimate(
            flops=4 * rows_c * tok_dev * text_len_all * width,
            transcendentals=rows_c * tok_dev * text_len_all * groups,
            bytes_accessed=4 * q_raw.size + 4 * text_all[0].size,
        ),
    )(
        cross_q_raw, factor_of(cross_total), cross_q_gain.reshape(1, width),
        text_all[0], factor_of(text_total), text_k_gain.reshape(1, width),
        text_all[1], text_mask,
    )

    first_tile = (me - REACH) * tiles_dev
    cand = first_tile + jnp.arange(slots * tiles_dev, dtype=jnp.int32)
    live_slot = jnp.arange(NB, dtype=jnp.int32)[None, :] < nbr_count[:, None]
    hit = (nbr[:, :, None] == cand[None, None, :]) & live_slot[:, :, None]
    live = jnp.any(hit, axis=1)
    self_mask = jnp.repeat(live.astype(jnp.int32), tile_len, axis=1)[:, None, :]
    shard_of_slot = me - REACH + jnp.arange(8, dtype=jnp.int32)
    slot_ok = (shard_of_slot >= 0) & (shard_of_slot < n_frame)
    slot_ok = jnp.broadcast_to(slot_ok.astype(jnp.int32)[:, None], (8, 128))

    nb_index = {0: 0, 1: 1, 3: 2, 4: 3}
    k_specs, v_specs, k_args, v_args = [], [], [], []
    for j in range(slots):
        if j == REACH:
            k_specs.append(pl.BlockSpec((1, tok_dev, HD), lambda c, h: (c, 0, h)))
            v_specs.append(pl.BlockSpec((1, tok_dev, HD), lambda c, h: (c, 0, h)))
            k_args.append(k_raw)
            v_args.append(v_in)
        else:
            s = nb_index[j]
            k_specs.append(pl.BlockSpec((None, None, 1, tok_dev, HD), lambda c, h, s=s: (s, 0, c, 0, h)))
            v_specs.append(pl.BlockSpec((None, None, 1, tok_dev, HD), lambda c, h, s=s: (s, 1, c, 0, h)))
            k_args.append(kv_nb)
            v_args.append(kv_nb)

    key_len = slots * tok_dev
    self_out = pl.pallas_call(
        functools.partial(self_kernel, score_scale=score_scale, tiles=tiles_dev, slots=slots),
        out_shape=jax.ShapeDtypeStruct(q_raw.shape, jnp.bfloat16),
        grid=(rows_c, groups),
        in_specs=[
            pl.BlockSpec((1, tok_dev, HD), lambda c, h: (c, 0, h)),
            pl.BlockSpec((1, tok_dev, 1), lambda c, h: (c, 0, 0)),
            pl.BlockSpec((1, HD), lambda c, h: (0, h)),
            pl.BlockSpec((1, slots, tok_dev, 1), lambda c, h: (c, 0, 0, 0)),
            pl.BlockSpec((1, HD), lambda c, h: (0, h)),
            pl.BlockSpec((tiles_dev, 1, key_len), lambda c, h: (0, 0, 0)),
            pl.BlockSpec((8, 128), lambda c, h: (0, 0)),
        ] + k_specs + v_specs,
        out_specs=pl.BlockSpec((1, tok_dev, HD), lambda c, h: (c, 0, h)),
        cost_estimate=pl.CostEstimate(
            flops=4 * rows_c * tok_dev * key_len * width,
            transcendentals=rows_c * tok_dev * key_len * groups,
            bytes_accessed=4 * q_raw.size + 4 * slots * k_raw.size,
        ),
    )(
        q_raw, factor_of(q_total), q_gain.reshape(1, width), k_fac, k_gain.reshape(1, width),
        self_mask, slot_ok, *k_args, *v_args,
    )
    return (self_out, cross_out)


def solution(mesh):
    in_specs = (
        P(None, "frame", "head"),
        P(None, "frame", "head"),
        P(None, "frame", "head"),
        P(None, "frame", "head"),
        P(None, "frame", "head"),
        P(None, "frame", "head"),
        P("head"),
        P("head"),
        P("head"),
        P("head"),
        P("frame", None),
        P("frame"),
        P(),
    )
    out_specs = (P(None, "frame", "head"), P(None, "frame", "head"))
    return jax.shard_map(body, mesh=mesh, in_specs=in_specs, out_specs=out_specs, check_vma=False)
```

```python
import functools
import math

import jax
import jax.numpy as jnp
import numpy as np
from jax import lax
from jax.experimental import pallas as pl
from jax.experimental.pallas import tpu as pltpu
from jax.sharding import PartitionSpec as P

D = 5120
HD = 128
NB = 14
REACH = 2
MESH = pl.DeviceIdType.MESH

EPSILON = 1e-06

TEXT_BITS = (4, 2, 32, 16, 8, 1)
EARLY_TEXT_STEPS = 4
KV_CHUNKS = 4


def text_bits(n_frame):
    return [b for b in TEXT_BITS if b < n_frame]


def squares(tensor):
    values = tensor.astype(jnp.float32)
    return jnp.sum(values * values, axis=-1)


def factor_of(totals):
    return lax.rsqrt(totals / D + EPSILON)[..., None]


def exchange_kernel(kv_own, text_own, kv_nb, text_all, kv_send, kv_recv, tx_send, tx_recv, local_sem,
                    *, n_frame, bits, rows, chunks):
    f = lax.axis_index("frame")
    h = lax.axis_index("head")
    has_prev = f >= 1
    has_next = f <= n_frame - 2

    barrier = pltpu.get_barrier_semaphore()

    @pl.when(has_prev)
    def _():
        pl.semaphore_signal(barrier, inc=1, device_id=(f - 1, h), device_id_type=MESH)

    @pl.when(has_next)
    def _():
        pl.semaphore_signal(barrier, inc=1, device_id=(f + 1, h), device_id_type=MESH)

    for b in bits:
        pl.semaphore_signal(barrier, inc=1, device_id=(f ^ b, h), device_id_type=MESH)
    peers = len(bits) + has_prev.astype(jnp.int32) + has_next.astype(jnp.int32)
    pl.semaphore_wait(barrier, peers)

    span = kv_own.shape[2] // chunks

    def piece(ref, i):
        return ref.at[:, :, pl.ds(i * span, span)]

    def hop(src, dst, i, step, slot, target):
        return pltpu.make_async_remote_copy(
            src_ref=piece(src, i), dst_ref=piece(kv_nb.at[slot], i),
            send_sem=kv_send.at[step, i], recv_sem=kv_recv.at[slot, i],
            device_id=(target, h), device_id_type=MESH)

    to_next = [hop(kv_own, None, i, 0, 1, f + 1) for i in range(chunks)]
    to_prev = [hop(kv_own, None, i, 1, 2, f - 1) for i in range(chunks)]
    fwd_next = [hop(kv_nb.at[1], None, i, 2, 0, f + 1) for i in range(chunks)]
    fwd_prev = [hop(kv_nb.at[2], None, i, 3, 3, f - 1) for i in range(chunks)]
    both = jnp.logical_and(has_prev, has_next)

    @pl.when(has_next)
    def _():
        for c in to_next:
            c.start()

    @pl.when(has_prev)
    def _():
        for c in to_prev:
            c.start()

    pos = 0
    for i, b in enumerate(bits):
        pos = pos + ((f // b) % 2) * (1 << i)
    mine = pltpu.make_async_copy(
        text_own, text_all.at[:, pl.ds(pl.multiple_of(pos * rows, rows), rows)], local_sem.at[0])
    mine.start()
    mine.wait()

    def text_step(i, b):
        size = rows << i
        start = pl.multiple_of((pos >> i) * size, size)
        swap = pltpu.make_async_remote_copy(
            src_ref=text_all.at[:, pl.ds(start, size)], dst_ref=text_all.at[:, pl.ds(start, size)],
            send_sem=tx_send.at[i], recv_sem=tx_recv.at[i], device_id=(f ^ b, h), device_id_type=MESH)
        swap.start()
        swap.wait_send()
        swap.wait_recv()

    early = min(EARLY_TEXT_STEPS, len(bits))
    for i in range(early):
        text_step(i, bits[i])

    for i in range(chunks):
        @pl.when(has_prev)
        def _():
            to_next[i].wait_recv()

        @pl.when(has_next)
        def _():
            to_prev[i].wait_recv()

        @pl.when(both)
        def _():
            fwd_next[i].start()
            fwd_prev[i].start()

    for i in range(early, len(bits)):
        text_step(i, bits[i])

    for i in range(chunks):
        @pl.when(has_next)
        def _():
            to_next[i].wait_send()

        @pl.when(has_prev)
        def _():
            to_prev[i].wait_send()

        @pl.when(f >= 2)
        def _():
            fwd_next[i].wait_recv()

        @pl.when(f <= n_frame - 3)
        def _():
            fwd_prev[i].wait_recv()

        @pl.when(both)
        def _():
            fwd_next[i].wait_send()
            fwd_prev[i].wait_send()


def exchange(kv_own, text_own, n_frame):
    bits = text_bits(n_frame)
    rows = text_own.shape[1]
    return pl.pallas_call(
        functools.partial(exchange_kernel, n_frame=n_frame, bits=bits, rows=rows, chunks=KV_CHUNKS),
        out_shape=(
            jax.ShapeDtypeStruct((4,) + kv_own.shape, kv_own.dtype),
            jax.ShapeDtypeStruct((text_own.shape[0], rows * n_frame, text_own.shape[2]), text_own.dtype),
        ),
        in_specs=[pl.BlockSpec(memory_space=pl.ANY)] * 2,
        out_specs=(pl.BlockSpec(memory_space=pl.ANY), pl.BlockSpec(memory_space=pl.ANY)),
        scratch_shapes=[
            pltpu.SemaphoreType.DMA((4, KV_CHUNKS)),
            pltpu.SemaphoreType.DMA((4, KV_CHUNKS)),
            pltpu.SemaphoreType.DMA((len(bits),)),
            pltpu.SemaphoreType.DMA((len(bits),)),
            pltpu.SemaphoreType.DMA((1,)),
        ],
        compiler_params=pltpu.CompilerParams(collective_id=0, has_side_effects=True),
    )(kv_own, text_own)


def softmax_rows(scores):
    row_top = jnp.max(scores, axis=-1, keepdims=True)
    powers = jnp.exp(scores - row_top)
    inverse = 1.0 / jnp.sum(powers, axis=-1, keepdims=True)
    return (powers * inverse).astype(jnp.bfloat16)


def normalized(raw, fac, gain):
    return (raw.astype(jnp.float32) * fac * gain).astype(jnp.bfloat16)


def self_kernel(q_ref, qf_ref, qg_ref, kf_ref, kg_ref, mask_ref, ok_ref, *refs, score_scale, tiles, slots):
    k_refs = refs[:slots]
    v_refs = refs[slots:2 * slots]
    o_ref = refs[2 * slots]
    q = normalized(q_ref[0], qf_ref[0], qg_ref[...])
    span = q.shape[0]
    kg = kg_ref[...]
    parts = []
    for j in range(slots):
        k = normalized(k_refs[j][0], kf_ref[0, j], kg)
        parts.append(lax.dot_general(q, k, (((1,), (1,)), ((), ())), preferred_element_type=jnp.float32))
    scores = jnp.concatenate(parts, axis=1) * score_scale
    key_len = scores.shape[1]
    scores = scores.reshape(tiles, span // tiles, key_len)
    scores = jnp.where(mask_ref[...] > 0, scores, -1e30)
    weights = softmax_rows(scores).reshape(span, key_len)
    out = None
    for j in range(slots):
        v = jnp.where(ok_ref[j:j + 1, :] > 0, v_refs[j][0], jnp.zeros((), v_refs[j].dtype))
        part = jnp.dot(weights[:, j * span:(j + 1) * span], v, preferred_element_type=jnp.float32)
        out = part if out is None else out + part
    o_ref[0] = out.astype(o_ref.dtype)


def cross_kernel(q_ref, qf_ref, qg_ref, k_ref, kf_ref, kg_ref, v_ref, mask_ref, o_ref, *, score_scale):
    q = normalized(q_ref[0], qf_ref[0], qg_ref[...])
    k = normalized(k_ref[0], kf_ref[0], kg_ref[...])
    scores = lax.dot_general(q, k, (((1,), (1,)), ((), ())), preferred_element_type=jnp.float32)
    scores = jnp.where(mask_ref[0] > 0, scores * score_scale, -1e30)
    weights = softmax_rows(scores)
    out = jnp.dot(weights, v_ref[0], preferred_element_type=jnp.float32)
    o_ref[0] = out.astype(o_ref.dtype)


def body(
    q_raw,
    k_raw,
    v_in,
    cross_q_raw,
    text_k_raw,
    text_v,
    q_gain,
    k_gain,
    cross_q_gain,
    text_k_gain,
    nbr,
    nbr_count,
    text_len,
):
    rows_c, tok_dev, width = q_raw.shape
    groups = width // HD
    tiles_dev = nbr.shape[0]
    tile_len = tok_dev // tiles_dev
    n_frame = lax.axis_size("frame")
    me = lax.axis_index("frame")
    score_scale = 1.0 / math.sqrt(HD)
    slots = 2 * REACH + 1

    kv_own = jnp.stack([k_raw, v_in])
    txt_rows = text_k_raw.shape[1]
    text_own = jnp.stack([text_k_raw, text_v]).reshape(2 * rows_c, txt_rows, width)
    kv_nb, text_all = exchange(kv_own, text_own, n_frame)
    text_all = text_all.reshape(2, rows_c, n_frame * txt_rows, width)

    k_nb_sq = squares(kv_nb[:, 0])
    q_total, k_total, k_nb_total, cross_total, text_total = lax.psum(
        (squares(q_raw), squares(k_raw), k_nb_sq, squares(cross_q_raw), squares(text_all[0])), "head"
    )
    k_fac = factor_of(
        jnp.stack([k_nb_total[0], k_nb_total[1], k_total, k_nb_total[2], k_nb_total[3]], axis=1)
    )

    bits = text_bits(n_frame)
    frame_of_pos = np.zeros(n_frame, np.int32)
    for p in range(n_frame):
        frame_of_pos[p] = sum(b for i, b in enumerate(bits) if (p >> i) & 1)
    token_of_row = (frame_of_pos[:, None] * txt_rows + np.arange(txt_rows)[None, :]).reshape(-1)
    text_mask = (jnp.asarray(token_of_row)[None, :] < text_len[:, None]).astype(jnp.int32)[:, None, :]

    text_len_all = n_frame * txt_rows
    cross_out = pl.pallas_call(
        functools.partial(cross_kernel, score_scale=score_scale),
        out_shape=jax.ShapeDtypeStruct(q_raw.shape, jnp.bfloat16),
        grid=(rows_c, groups),
        in_specs=[
            pl.BlockSpec((1, tok_dev, HD), lambda c, h: (c, 0, h)),
            pl.BlockSpec((1, tok_dev, 1), lambda c, h: (c, 0, 0)),
            pl.BlockSpec((1, HD), lambda c, h: (0, h)),
            pl.BlockSpec((1, text_len_all, HD), lambda c, h: (c, 0, h)),
            pl.BlockSpec((1, text_len_all, 1), lambda c, h: (c, 0, 0)),
            pl.BlockSpec((1, HD), lambda c, h: (0, h)),
            pl.BlockSpec((1, text_len_all, HD), lambda c, h: (c, 0, h)),
            pl.BlockSpec((1, 1, text_len_all), lambda c, h: (c, 0, 0)),
        ],
        out_specs=pl.BlockSpec((1, tok_dev, HD), lambda c, h: (c, 0, h)),
        cost_estimate=pl.CostEstimate(
            flops=4 * rows_c * tok_dev * text_len_all * width,
            transcendentals=rows_c * tok_dev * text_len_all * groups,
            bytes_accessed=4 * q_raw.size + 4 * text_all[0].size,
        ),
    )(
        cross_q_raw, factor_of(cross_total), cross_q_gain.reshape(1, width),
        text_all[0], factor_of(text_total), text_k_gain.reshape(1, width),
        text_all[1], text_mask,
    )

    first_tile = (me - REACH) * tiles_dev
    cand = first_tile + jnp.arange(slots * tiles_dev, dtype=jnp.int32)
    live_slot = jnp.arange(NB, dtype=jnp.int32)[None, :] < nbr_count[:, None]
    hit = (nbr[:, :, None] == cand[None, None, :]) & live_slot[:, :, None]
    live = jnp.any(hit, axis=1)
    self_mask = jnp.repeat(live.astype(jnp.int32), tile_len, axis=1)[:, None, :]
    shard_of_slot = me - REACH + jnp.arange(8, dtype=jnp.int32)
    slot_ok = (shard_of_slot >= 0) & (shard_of_slot < n_frame)
    slot_ok = jnp.broadcast_to(slot_ok.astype(jnp.int32)[:, None], (8, 128))

    nb_index = {0: 0, 1: 1, 3: 2, 4: 3}
    k_specs, v_specs, k_args, v_args = [], [], [], []
    for j in range(slots):
        if j == REACH:
            k_specs.append(pl.BlockSpec((1, tok_dev, HD), lambda c, h: (c, 0, h)))
            v_specs.append(pl.BlockSpec((1, tok_dev, HD), lambda c, h: (c, 0, h)))
            k_args.append(k_raw)
            v_args.append(v_in)
        else:
            s = nb_index[j]
            k_specs.append(pl.BlockSpec((None, None, 1, tok_dev, HD), lambda c, h, s=s: (s, 0, c, 0, h)))
            v_specs.append(pl.BlockSpec((None, None, 1, tok_dev, HD), lambda c, h, s=s: (s, 1, c, 0, h)))
            k_args.append(kv_nb)
            v_args.append(kv_nb)

    key_len = slots * tok_dev
    self_out = pl.pallas_call(
        functools.partial(self_kernel, score_scale=score_scale, tiles=tiles_dev, slots=slots),
        out_shape=jax.ShapeDtypeStruct(q_raw.shape, jnp.bfloat16),
        grid=(rows_c, groups),
        in_specs=[
            pl.BlockSpec((1, tok_dev, HD), lambda c, h: (c, 0, h)),
            pl.BlockSpec((1, tok_dev, 1), lambda c, h: (c, 0, 0)),
            pl.BlockSpec((1, HD), lambda c, h: (0, h)),
            pl.BlockSpec((1, slots, tok_dev, 1), lambda c, h: (c, 0, 0, 0)),
            pl.BlockSpec((1, HD), lambda c, h: (0, h)),
            pl.BlockSpec((tiles_dev, 1, key_len), lambda c, h: (0, 0, 0)),
            pl.BlockSpec((8, 128), lambda c, h: (0, 0)),
        ] + k_specs + v_specs,
        out_specs=pl.BlockSpec((1, tok_dev, HD), lambda c, h: (c, 0, h)),
        cost_estimate=pl.CostEstimate(
            flops=4 * rows_c * tok_dev * key_len * width,
            transcendentals=rows_c * tok_dev * key_len * groups,
            bytes_accessed=4 * q_raw.size + 4 * slots * k_raw.size,
        ),
    )(
        q_raw, factor_of(q_total), q_gain.reshape(1, width), k_fac, k_gain.reshape(1, width),
        self_mask, slot_ok, *k_args, *v_args,
    )
    return (self_out, cross_out)


def solution(mesh):
    in_specs = (
        P(None, "frame", "head"),
        P(None, "frame", "head"),
        P(None, "frame", "head"),
        P(None, "frame", "head"),
        P(None, "frame", "head"),
        P(None, "frame", "head"),
        P("head"),
        P("head"),
        P("head"),
        P("head"),
        P("frame", None),
        P("frame"),
        P(),
    )
    out_specs = (P(None, "frame", "head"), P(None, "frame", "head"))
    return jax.shard_map(body, mesh=mesh, in_specs=in_specs, out_specs=out_specs, check_vma=False)
```

```python
import functools
import math

import jax
import jax.numpy as jnp
import numpy as np
from jax import lax
from jax.experimental import pallas as pl
from jax.experimental.pallas import tpu as pltpu
from jax.sharding import PartitionSpec as P

D = 5120
HD = 128
NB = 14
REACH = 2
MESH = pl.DeviceIdType.MESH

EPSILON = 1e-06

TEXT_BITS = (4, 2, 32, 16, 8, 1)
EARLY_TEXT_STEPS = 4
KV_CHUNKS = 4


def text_bits(n_frame):
    return [b for b in TEXT_BITS if b < n_frame]


def squares(tensor):
    values = tensor.astype(jnp.float32)
    return jnp.sum(values * values, axis=-1)


def factor_of(totals):
    return lax.rsqrt(totals / D + EPSILON)[..., None]


class _Pair:
    def __init__(self, first, second):
        self.parts = (first, second)

    def start(self):
        for p in self.parts:
            p.start()

    def wait_send(self):
        for p in self.parts:
            p.wait_send()

    def wait_recv(self):
        for p in self.parts:
            p.wait_recv()


def exchange_kernel(k_own, v_own, text_own, kv_nb, text_all, kv_send, kv_recv, tx_send, tx_recv, local_sem,
                    *, n_frame, bits, rows, chunks):
    f = lax.axis_index("frame")
    h = lax.axis_index("head")
    has_prev = f >= 1
    has_next = f <= n_frame - 2

    barrier = pltpu.get_barrier_semaphore()

    @pl.when(has_prev)
    def _():
        pl.semaphore_signal(barrier, inc=1, device_id=(f - 1, h), device_id_type=MESH)

    @pl.when(has_next)
    def _():
        pl.semaphore_signal(barrier, inc=1, device_id=(f + 1, h), device_id_type=MESH)

    for b in bits:
        pl.semaphore_signal(barrier, inc=1, device_id=(f ^ b, h), device_id_type=MESH)
    peers = len(bits) + has_prev.astype(jnp.int32) + has_next.astype(jnp.int32)
    pl.semaphore_wait(barrier, peers)

    span = k_own.shape[1] // chunks

    def hop(src, dst, i, step, slot, target):
        return pltpu.make_async_remote_copy(
            src_ref=src.at[..., pl.ds(i * span, span), :], dst_ref=dst.at[..., pl.ds(i * span, span), :],
            send_sem=kv_send.at[step, i], recv_sem=kv_recv.at[slot, i],
            device_id=(target, h), device_id_type=MESH)

    def own_hop(i, step, slot, target):
        return _Pair(hop(k_own, kv_nb.at[slot, 0], i, step, slot, target),
                     hop(v_own, kv_nb.at[slot, 1], i, step + 4, slot + 4, target))

    to_next = [own_hop(i, 0, 1, f + 1) for i in range(chunks)]
    to_prev = [own_hop(i, 1, 2, f - 1) for i in range(chunks)]
    fwd_next = [hop(kv_nb.at[1], kv_nb.at[0], i, 2, 0, f + 1) for i in range(chunks)]
    fwd_prev = [hop(kv_nb.at[2], kv_nb.at[3], i, 3, 3, f - 1) for i in range(chunks)]
    both = jnp.logical_and(has_prev, has_next)

    @pl.when(has_next)
    def _():
        for c in to_next:
            c.start()

    @pl.when(has_prev)
    def _():
        for c in to_prev:
            c.start()

    pos = 0
    for i, b in enumerate(bits):
        pos = pos + ((f // b) % 2) * (1 << i)
    mine = pltpu.make_async_copy(
        text_own, text_all.at[:, pl.ds(pl.multiple_of(pos * rows, rows), rows)], local_sem.at[0])
    mine.start()
    mine.wait()

    def text_step(i, b):
        size = rows << i
        start = pl.multiple_of((pos >> i) * size, size)
        swap = pltpu.make_async_remote_copy(
            src_ref=text_all.at[:, pl.ds(start, size)], dst_ref=text_all.at[:, pl.ds(start, size)],
            send_sem=tx_send.at[i], recv_sem=tx_recv.at[i], device_id=(f ^ b, h), device_id_type=MESH)
        swap.start()
        swap.wait_send()
        swap.wait_recv()

    early = min(EARLY_TEXT_STEPS, len(bits))
    for i in range(early):
        text_step(i, bits[i])

    for i in range(chunks):
        @pl.when(has_prev)
        def _():
            to_next[i].wait_recv()

        @pl.when(has_next)
        def _():
            to_prev[i].wait_recv()

        @pl.when(both)
        def _():
            fwd_next[i].start()
            fwd_prev[i].start()

    for i in range(early, len(bits)):
        text_step(i, bits[i])

    for i in range(chunks):
        @pl.when(has_next)
        def _():
            to_next[i].wait_send()

        @pl.when(has_prev)
        def _():
            to_prev[i].wait_send()

        @pl.when(f >= 2)
        def _():
            fwd_next[i].wait_recv()

        @pl.when(f <= n_frame - 3)
        def _():
            fwd_prev[i].wait_recv()

        @pl.when(both)
        def _():
            fwd_next[i].wait_send()
            fwd_prev[i].wait_send()


def exchange(k_own, v_own, text_own, n_frame):
    kv_shape = (2,) + k_own.shape
    bits = text_bits(n_frame)
    rows = text_own.shape[1]
    return pl.pallas_call(
        functools.partial(exchange_kernel, n_frame=n_frame, bits=bits, rows=rows, chunks=KV_CHUNKS),
        out_shape=(
            jax.ShapeDtypeStruct((4,) + kv_shape, k_own.dtype),
            jax.ShapeDtypeStruct((text_own.shape[0], rows * n_frame, text_own.shape[2]), text_own.dtype),
        ),
        in_specs=[pl.BlockSpec(memory_space=pl.ANY)] * 3,
        out_specs=(pl.BlockSpec(memory_space=pl.ANY), pl.BlockSpec(memory_space=pl.ANY)),
        scratch_shapes=[
            pltpu.SemaphoreType.DMA((8, KV_CHUNKS)),
            pltpu.SemaphoreType.DMA((8, KV_CHUNKS)),
            pltpu.SemaphoreType.DMA((len(bits),)),
            pltpu.SemaphoreType.DMA((len(bits),)),
            pltpu.SemaphoreType.DMA((1,)),
        ],
        compiler_params=pltpu.CompilerParams(collective_id=0, has_side_effects=True),
    )(k_own, v_own, text_own)


def softmax_rows(scores):
    row_top = jnp.max(scores, axis=-1, keepdims=True)
    powers = jnp.exp(scores - row_top)
    inverse = 1.0 / jnp.sum(powers, axis=-1, keepdims=True)
    return (powers * inverse).astype(jnp.bfloat16)


def normalized(raw, fac, gain):
    return (raw.astype(jnp.float32) * fac * gain).astype(jnp.bfloat16)


def self_kernel(q_ref, qf_ref, qg_ref, kf_ref, kg_ref, mask_ref, ok_ref, *refs, score_scale, tiles, slots):
    k_refs = refs[:slots]
    v_refs = refs[slots:2 * slots]
    o_ref = refs[2 * slots]
    q = normalized(q_ref[0], qf_ref[0], qg_ref[...])
    span = q.shape[0]
    kg = kg_ref[...]
    parts = []
    for j in range(slots):
        k = normalized(k_refs[j][0], kf_ref[0, j], kg)
        parts.append(lax.dot_general(q, k, (((1,), (1,)), ((), ())), preferred_element_type=jnp.float32))
    scores = jnp.concatenate(parts, axis=1) * score_scale
    key_len = scores.shape[1]
    scores = scores.reshape(tiles, span // tiles, key_len)
    scores = jnp.where(mask_ref[...] > 0, scores, -1e30)
    weights = softmax_rows(scores).reshape(span, key_len)
    out = None
    for j in range(slots):
        v = jnp.where(ok_ref[j:j + 1, :] > 0, v_refs[j][0], jnp.zeros((), v_refs[j].dtype))
        part = jnp.dot(weights[:, j * span:(j + 1) * span], v, preferred_element_type=jnp.float32)
        out = part if out is None else out + part
    o_ref[0] = out.astype(o_ref.dtype)


def cross_kernel(q_ref, qf_ref, qg_ref, k_ref, kf_ref, kg_ref, v_ref, mask_ref, o_ref, *, score_scale):
    q = normalized(q_ref[0], qf_ref[0], qg_ref[...])
    k = normalized(k_ref[0], kf_ref[0], kg_ref[...])
    scores = lax.dot_general(q, k, (((1,), (1,)), ((), ())), preferred_element_type=jnp.float32)
    scores = jnp.where(mask_ref[0] > 0, scores * score_scale, -1e30)
    weights = softmax_rows(scores)
    out = jnp.dot(weights, v_ref[0], preferred_element_type=jnp.float32)
    o_ref[0] = out.astype(o_ref.dtype)


def body(
    q_raw,
    k_raw,
    v_in,
    cross_q_raw,
    text_k_raw,
    text_v,
    q_gain,
    k_gain,
    cross_q_gain,
    text_k_gain,
    nbr,
    nbr_count,
    text_len,
):
    rows_c, tok_dev, width = q_raw.shape
    groups = width // HD
    tiles_dev = nbr.shape[0]
    tile_len = tok_dev // tiles_dev
    n_frame = lax.axis_size("frame")
    me = lax.axis_index("frame")
    score_scale = 1.0 / math.sqrt(HD)
    slots = 2 * REACH + 1

    txt_rows = text_k_raw.shape[1]
    text_own = jnp.stack([text_k_raw, text_v]).reshape(2 * rows_c, txt_rows, width)
    kv_nb, text_all = exchange(k_raw, v_in, text_own, n_frame)
    text_all = text_all.reshape(2, rows_c, n_frame * txt_rows, width)

    k_nb_sq = squares(kv_nb[:, 0])
    q_total, k_total, k_nb_total, cross_total, text_total = lax.psum(
        (squares(q_raw), squares(k_raw), k_nb_sq, squares(cross_q_raw), squares(text_all[0])), "head"
    )
    k_fac = factor_of(
        jnp.stack([k_nb_total[0], k_nb_total[1], k_total, k_nb_total[2], k_nb_total[3]], axis=1)
    )

    bits = text_bits(n_frame)
    frame_of_pos = np.zeros(n_frame, np.int32)
    for p in range(n_frame):
        frame_of_pos[p] = sum(b for i, b in enumerate(bits) if (p >> i) & 1)
    token_of_row = (frame_of_pos[:, None] * txt_rows + np.arange(txt_rows)[None, :]).reshape(-1)
    text_mask = (jnp.asarray(token_of_row)[None, :] < text_len[:, None]).astype(jnp.int32)[:, None, :]

    text_len_all = n_frame * txt_rows
    cross_out = pl.pallas_call(
        functools.partial(cross_kernel, score_scale=score_scale),
        out_shape=jax.ShapeDtypeStruct(q_raw.shape, jnp.bfloat16),
        grid=(rows_c, groups),
        in_specs=[
            pl.BlockSpec((1, tok_dev, HD), lambda c, h: (c, 0, h)),
            pl.BlockSpec((1, tok_dev, 1), lambda c, h: (c, 0, 0)),
            pl.BlockSpec((1, HD), lambda c, h: (0, h)),
            pl.BlockSpec((1, text_len_all, HD), lambda c, h: (c, 0, h)),
            pl.BlockSpec((1, text_len_all, 1), lambda c, h: (c, 0, 0)),
            pl.BlockSpec((1, HD), lambda c, h: (0, h)),
            pl.BlockSpec((1, text_len_all, HD), lambda c, h: (c, 0, h)),
            pl.BlockSpec((1, 1, text_len_all), lambda c, h: (c, 0, 0)),
        ],
        out_specs=pl.BlockSpec((1, tok_dev, HD), lambda c, h: (c, 0, h)),
        cost_estimate=pl.CostEstimate(
            flops=4 * rows_c * tok_dev * text_len_all * width,
            transcendentals=rows_c * tok_dev * text_len_all * groups,
            bytes_accessed=4 * q_raw.size + 4 * text_all[0].size,
        ),
    )(
        cross_q_raw, factor_of(cross_total), cross_q_gain.reshape(1, width),
        text_all[0], factor_of(text_total), text_k_gain.reshape(1, width),
        text_all[1], text_mask,
    )

    first_tile = (me - REACH) * tiles_dev
    cand = first_tile + jnp.arange(slots * tiles_dev, dtype=jnp.int32)
    live_slot = jnp.arange(NB, dtype=jnp.int32)[None, :] < nbr_count[:, None]
    hit = (nbr[:, :, None] == cand[None, None, :]) & live_slot[:, :, None]
    live = jnp.any(hit, axis=1)
    self_mask = jnp.repeat(live.astype(jnp.int32), tile_len, axis=1)[:, None, :]
    shard_of_slot = me - REACH + jnp.arange(8, dtype=jnp.int32)
    slot_ok = (shard_of_slot >= 0) & (shard_of_slot < n_frame)
    slot_ok = jnp.broadcast_to(slot_ok.astype(jnp.int32)[:, None], (8, 128))

    nb_index = {0: 0, 1: 1, 3: 2, 4: 3}
    k_specs, v_specs, k_args, v_args = [], [], [], []
    for j in range(slots):
        if j == REACH:
            k_specs.append(pl.BlockSpec((1, tok_dev, HD), lambda c, h: (c, 0, h)))
            v_specs.append(pl.BlockSpec((1, tok_dev, HD), lambda c, h: (c, 0, h)))
            k_args.append(k_raw)
            v_args.append(v_in)
        else:
            s = nb_index[j]
            k_specs.append(pl.BlockSpec((None, None, 1, tok_dev, HD), lambda c, h, s=s: (s, 0, c, 0, h)))
            v_specs.append(pl.BlockSpec((None, None, 1, tok_dev, HD), lambda c, h, s=s: (s, 1, c, 0, h)))
            k_args.append(kv_nb)
            v_args.append(kv_nb)

    key_len = slots * tok_dev
    self_out = pl.pallas_call(
        functools.partial(self_kernel, score_scale=score_scale, tiles=tiles_dev, slots=slots),
        out_shape=jax.ShapeDtypeStruct(q_raw.shape, jnp.bfloat16),
        grid=(rows_c, groups),
        in_specs=[
            pl.BlockSpec((1, tok_dev, HD), lambda c, h: (c, 0, h)),
            pl.BlockSpec((1, tok_dev, 1), lambda c, h: (c, 0, 0)),
            pl.BlockSpec((1, HD), lambda c, h: (0, h)),
            pl.BlockSpec((1, slots, tok_dev, 1), lambda c, h: (c, 0, 0, 0)),
            pl.BlockSpec((1, HD), lambda c, h: (0, h)),
            pl.BlockSpec((tiles_dev, 1, key_len), lambda c, h: (0, 0, 0)),
            pl.BlockSpec((8, 128), lambda c, h: (0, 0)),
        ] + k_specs + v_specs,
        out_specs=pl.BlockSpec((1, tok_dev, HD), lambda c, h: (c, 0, h)),
        cost_estimate=pl.CostEstimate(
            flops=4 * rows_c * tok_dev * key_len * width,
            transcendentals=rows_c * tok_dev * key_len * groups,
            bytes_accessed=4 * q_raw.size + 4 * slots * k_raw.size,
        ),
    )(
        q_raw, factor_of(q_total), q_gain.reshape(1, width), k_fac, k_gain.reshape(1, width),
        self_mask, slot_ok, *k_args, *v_args,
    )
    return (self_out, cross_out)


def solution(mesh):
    in_specs = (
        P(None, "frame", "head"),
        P(None, "frame", "head"),
        P(None, "frame", "head"),
        P(None, "frame", "head"),
        P(None, "frame", "head"),
        P(None, "frame", "head"),
        P("head"),
        P("head"),
        P("head"),
        P("head"),
        P("frame", None),
        P("frame"),
        P(),
    )
    out_specs = (P(None, "frame", "head"), P(None, "frame", "head"))
    return jax.shard_map(body, mesh=mesh, in_specs=in_specs, out_specs=out_specs, check_vma=False)
```

```python
import functools
import math

import jax
import jax.numpy as jnp
import numpy as np
from jax import lax
from jax.experimental import pallas as pl
from jax.experimental.pallas import tpu as pltpu
from jax.sharding import PartitionSpec as P

D = 5120
HD = 128
NB = 14
REACH = 2
MESH = pl.DeviceIdType.MESH

EPSILON = 1e-06

TEXT_BITS = (4, 2, 32, 16, 8, 1)
EARLY_TEXT_STEPS = 4
KV_CHUNKS = 4


def text_bits(n_frame):
    return [b for b in TEXT_BITS if b < n_frame]


def squares(tensor):
    values = tensor.astype(jnp.float32)
    return jnp.sum(values * values, axis=-1)


def factor_of(totals):
    return lax.rsqrt(totals / D + EPSILON)[..., None]


class _Pair:
    def __init__(self, first, second):
        self.parts = (first, second)

    def start(self):
        for p in self.parts:
            p.start()

    def wait_send(self):
        for p in self.parts:
            p.wait_send()

    def wait_recv(self):
        for p in self.parts:
            p.wait_recv()


def exchange_kernel(k_own, v_own, text_own, kv_nb, text_all, kv_send, kv_recv, tx_send, tx_recv, local_sem,
                    *, n_frame, bits, rows, chunks):
    f = lax.axis_index("frame")
    h = lax.axis_index("head")
    has_prev = f >= 1
    has_next = f <= n_frame - 2

    barrier = pltpu.get_barrier_semaphore()

    @pl.when(has_prev)
    def _():
        pl.semaphore_signal(barrier, inc=1, device_id=(f - 1, h), device_id_type=MESH)

    @pl.when(has_next)
    def _():
        pl.semaphore_signal(barrier, inc=1, device_id=(f + 1, h), device_id_type=MESH)

    for b in bits:
        pl.semaphore_signal(barrier, inc=1, device_id=(f ^ b, h), device_id_type=MESH)
    peers = len(bits) + has_prev.astype(jnp.int32) + has_next.astype(jnp.int32)
    pl.semaphore_wait(barrier, peers)

    span = k_own.shape[1] // chunks

    def hop(src, dst, i, step, slot, target):
        return pltpu.make_async_remote_copy(
            src_ref=src.at[..., pl.ds(i * span, span), :], dst_ref=dst.at[..., pl.ds(i * span, span), :],
            send_sem=kv_send.at[step, i], recv_sem=kv_recv.at[slot, i],
            device_id=(target, h), device_id_type=MESH)

    def own_hop(i, step, slot, target):
        return _Pair(hop(k_own, kv_nb.at[slot, 0], i, step, slot, target),
                     hop(v_own, kv_nb.at[slot, 1], i, step + 4, slot + 4, target))

    to_next = [own_hop(i, 0, 1, f + 1) for i in range(chunks)]
    to_prev = [own_hop(i, 1, 2, f - 1) for i in range(chunks)]
    fwd_next = [hop(kv_nb.at[1], kv_nb.at[0], i, 2, 0, f + 1) for i in range(chunks)]
    fwd_prev = [hop(kv_nb.at[2], kv_nb.at[3], i, 3, 3, f - 1) for i in range(chunks)]
    both = jnp.logical_and(has_prev, has_next)

    @pl.when(has_next)
    def _():
        for c in to_next:
            c.start()

    @pl.when(has_prev)
    def _():
        for c in to_prev:
            c.start()

    pos = 0
    for i, b in enumerate(bits):
        pos = pos + ((f // b) % 2) * (1 << i)
    mine = pltpu.make_async_copy(
        text_own, text_all.at[:, pl.ds(pl.multiple_of(pos * rows, rows), rows)], local_sem.at[0])
    mine.start()
    mine.wait()

    def text_step(i, b):
        size = rows << i
        start = pl.multiple_of((pos >> i) * size, size)
        swap = pltpu.make_async_remote_copy(
            src_ref=text_all.at[:, pl.ds(start, size)], dst_ref=text_all.at[:, pl.ds(start, size)],
            send_sem=tx_send.at[i], recv_sem=tx_recv.at[i], device_id=(f ^ b, h), device_id_type=MESH)
        swap.start()
        swap.wait_send()
        swap.wait_recv()

    early = min(EARLY_TEXT_STEPS, len(bits))
    for i in range(early):
        text_step(i, bits[i])

    for i in range(chunks):
        @pl.when(has_prev)
        def _():
            to_next[i].wait_recv()

        @pl.when(has_next)
        def _():
            to_prev[i].wait_recv()

        @pl.when(both)
        def _():
            fwd_next[i].start()
            fwd_prev[i].start()

    for i in range(early, len(bits)):
        text_step(i, bits[i])

    for i in range(chunks):
        @pl.when(has_next)
        def _():
            to_next[i].wait_send()

        @pl.when(has_prev)
        def _():
            to_prev[i].wait_send()

        @pl.when(f >= 2)
        def _():
            fwd_next[i].wait_recv()

        @pl.when(f <= n_frame - 3)
        def _():
            fwd_prev[i].wait_recv()

        @pl.when(both)
        def _():
            fwd_next[i].wait_send()
            fwd_prev[i].wait_send()


def exchange(k_own, v_own, text_own, n_frame, ready):
    ready = lax.optimization_barrier(ready)
    kv_shape = (2,) + k_own.shape
    bits = text_bits(n_frame)
    rows = text_own.shape[1]
    k_own, v_own, text_own, ready = lax.optimization_barrier((k_own, v_own, text_own, ready))
    kv_nb, text_all = pl.pallas_call(
        functools.partial(exchange_kernel, n_frame=n_frame, bits=bits, rows=rows, chunks=KV_CHUNKS),
        out_shape=(
            jax.ShapeDtypeStruct((4,) + kv_shape, k_own.dtype),
            jax.ShapeDtypeStruct((text_own.shape[0], rows * n_frame, text_own.shape[2]), text_own.dtype),
        ),
        in_specs=[pl.BlockSpec(memory_space=pl.ANY)] * 3,
        out_specs=(pl.BlockSpec(memory_space=pl.ANY), pl.BlockSpec(memory_space=pl.ANY)),
        scratch_shapes=[
            pltpu.SemaphoreType.DMA((8, KV_CHUNKS)),
            pltpu.SemaphoreType.DMA((8, KV_CHUNKS)),
            pltpu.SemaphoreType.DMA((len(bits),)),
            pltpu.SemaphoreType.DMA((len(bits),)),
            pltpu.SemaphoreType.DMA((1,)),
        ],
        compiler_params=pltpu.CompilerParams(collective_id=0, has_side_effects=True),
    )(k_own, v_own, text_own)
    kv_nb, text_all, ready = lax.optimization_barrier((kv_nb, text_all, ready))
    return kv_nb, text_all, ready


def softmax_rows(scores):
    row_top = jnp.max(scores, axis=-1, keepdims=True)
    powers = jnp.exp(scores - row_top)
    inverse = 1.0 / jnp.sum(powers, axis=-1, keepdims=True)
    return (powers * inverse).astype(jnp.bfloat16)


def normalized(raw, fac, gain):
    return (raw.astype(jnp.float32) * fac * gain).astype(jnp.bfloat16)


def self_kernel(q_ref, qf_ref, qg_ref, kf_ref, kg_ref, mask_ref, ok_ref, *refs, score_scale, tiles, slots):
    k_refs = refs[:slots]
    v_refs = refs[slots:2 * slots]
    o_ref = refs[2 * slots]
    q = normalized(q_ref[0], qf_ref[0], qg_ref[...])
    span = q.shape[0]
    kg = kg_ref[...]
    parts = []
    for j in range(slots):
        k = normalized(k_refs[j][0], kf_ref[0, j], kg)
        parts.append(lax.dot_general(q, k, (((1,), (1,)), ((), ())), preferred_element_type=jnp.float32))
    scores = jnp.concatenate(parts, axis=1) * score_scale
    key_len = scores.shape[1]
    scores = scores.reshape(tiles, span // tiles, key_len)
    scores = jnp.where(mask_ref[...] > 0, scores, -1e30)
    weights = softmax_rows(scores).reshape(span, key_len)
    out = None
    for j in range(slots):
        v = jnp.where(ok_ref[j:j + 1, :] > 0, v_refs[j][0], jnp.zeros((), v_refs[j].dtype))
        part = jnp.dot(weights[:, j * span:(j + 1) * span], v, preferred_element_type=jnp.float32)
        out = part if out is None else out + part
    o_ref[0] = out.astype(o_ref.dtype)


def cross_kernel(q_ref, qf_ref, qg_ref, k_ref, kf_ref, kg_ref, v_ref, mask_ref, o_ref, *, score_scale):
    q = normalized(q_ref[0], qf_ref[0], qg_ref[...])
    k = normalized(k_ref[0], kf_ref[0], kg_ref[...])
    scores = lax.dot_general(q, k, (((1,), (1,)), ((), ())), preferred_element_type=jnp.float32)
    scores = jnp.where(mask_ref[0] > 0, scores * score_scale, -1e30)
    weights = softmax_rows(scores)
    out = jnp.dot(weights, v_ref[0], preferred_element_type=jnp.float32)
    o_ref[0] = out.astype(o_ref.dtype)


def body(
    q_raw,
    k_raw,
    v_in,
    cross_q_raw,
    text_k_raw,
    text_v,
    q_gain,
    k_gain,
    cross_q_gain,
    text_k_gain,
    nbr,
    nbr_count,
    text_len,
):
    rows_c, tok_dev, width = q_raw.shape
    groups = width // HD
    tiles_dev = nbr.shape[0]
    tile_len = tok_dev // tiles_dev
    n_frame = lax.axis_size("frame")
    me = lax.axis_index("frame")
    score_scale = 1.0 / math.sqrt(HD)
    slots = 2 * REACH + 1

    txt_rows = text_k_raw.shape[1]
    text_own = jnp.stack([text_k_raw, text_v]).reshape(2 * rows_c, txt_rows, width)
    own_sq = (squares(q_raw), squares(k_raw), squares(cross_q_raw))
    kv_nb, text_all, own_sq = exchange(k_raw, v_in, text_own, n_frame, own_sq)
    text_all = text_all.reshape(2, rows_c, n_frame * txt_rows, width)

    k_nb_sq = squares(kv_nb[:, 0])
    q_total, k_total, k_nb_total, cross_total, text_total = lax.psum(
        (own_sq[0], own_sq[1], k_nb_sq, own_sq[2], squares(text_all[0])), "head"
    )
    k_fac = factor_of(
        jnp.stack([k_nb_total[0], k_nb_total[1], k_total, k_nb_total[2], k_nb_total[3]], axis=1)
    )

    bits = text_bits(n_frame)
    frame_of_pos = np.zeros(n_frame, np.int32)
    for p in range(n_frame):
        frame_of_pos[p] = sum(b for i, b in enumerate(bits) if (p >> i) & 1)
    token_of_row = (frame_of_pos[:, None] * txt_rows + np.arange(txt_rows)[None, :]).reshape(-1)
    text_mask = (jnp.asarray(token_of_row)[None, :] < text_len[:, None]).astype(jnp.int32)[:, None, :]

    text_len_all = n_frame * txt_rows
    cross_out = pl.pallas_call(
        functools.partial(cross_kernel, score_scale=score_scale),
        out_shape=jax.ShapeDtypeStruct(q_raw.shape, jnp.bfloat16),
        grid=(rows_c, groups),
        in_specs=[
            pl.BlockSpec((1, tok_dev, HD), lambda c, h: (c, 0, h)),
            pl.BlockSpec((1, tok_dev, 1), lambda c, h: (c, 0, 0)),
            pl.BlockSpec((1, HD), lambda c, h: (0, h)),
            pl.BlockSpec((1, text_len_all, HD), lambda c, h: (c, 0, h)),
            pl.BlockSpec((1, text_len_all, 1), lambda c, h: (c, 0, 0)),
            pl.BlockSpec((1, HD), lambda c, h: (0, h)),
            pl.BlockSpec((1, text_len_all, HD), lambda c, h: (c, 0, h)),
            pl.BlockSpec((1, 1, text_len_all), lambda c, h: (c, 0, 0)),
        ],
        out_specs=pl.BlockSpec((1, tok_dev, HD), lambda c, h: (c, 0, h)),
        cost_estimate=pl.CostEstimate(
            flops=4 * rows_c * tok_dev * text_len_all * width,
            transcendentals=rows_c * tok_dev * text_len_all * groups,
            bytes_accessed=4 * q_raw.size + 4 * text_all[0].size,
        ),
    )(
        cross_q_raw, factor_of(cross_total), cross_q_gain.reshape(1, width),
        text_all[0], factor_of(text_total), text_k_gain.reshape(1, width),
        text_all[1], text_mask,
    )

    first_tile = (me - REACH) * tiles_dev
    cand = first_tile + jnp.arange(slots * tiles_dev, dtype=jnp.int32)
    live_slot = jnp.arange(NB, dtype=jnp.int32)[None, :] < nbr_count[:, None]
    hit = (nbr[:, :, None] == cand[None, None, :]) & live_slot[:, :, None]
    live = jnp.any(hit, axis=1)
    self_mask = jnp.repeat(live.astype(jnp.int32), tile_len, axis=1)[:, None, :]
    shard_of_slot = me - REACH + jnp.arange(8, dtype=jnp.int32)
    slot_ok = (shard_of_slot >= 0) & (shard_of_slot < n_frame)
    slot_ok = jnp.broadcast_to(slot_ok.astype(jnp.int32)[:, None], (8, 128))

    nb_index = {0: 0, 1: 1, 3: 2, 4: 3}
    k_specs, v_specs, k_args, v_args = [], [], [], []
    for j in range(slots):
        if j == REACH:
            k_specs.append(pl.BlockSpec((1, tok_dev, HD), lambda c, h: (c, 0, h)))
            v_specs.append(pl.BlockSpec((1, tok_dev, HD), lambda c, h: (c, 0, h)))
            k_args.append(k_raw)
            v_args.append(v_in)
        else:
            s = nb_index[j]
            k_specs.append(pl.BlockSpec((None, None, 1, tok_dev, HD), lambda c, h, s=s: (s, 0, c, 0, h)))
            v_specs.append(pl.BlockSpec((None, None, 1, tok_dev, HD), lambda c, h, s=s: (s, 1, c, 0, h)))
            k_args.append(kv_nb)
            v_args.append(kv_nb)

    key_len = slots * tok_dev
    self_out = pl.pallas_call(
        functools.partial(self_kernel, score_scale=score_scale, tiles=tiles_dev, slots=slots),
        out_shape=jax.ShapeDtypeStruct(q_raw.shape, jnp.bfloat16),
        grid=(rows_c, groups),
        in_specs=[
            pl.BlockSpec((1, tok_dev, HD), lambda c, h: (c, 0, h)),
            pl.BlockSpec((1, tok_dev, 1), lambda c, h: (c, 0, 0)),
            pl.BlockSpec((1, HD), lambda c, h: (0, h)),
            pl.BlockSpec((1, slots, tok_dev, 1), lambda c, h: (c, 0, 0, 0)),
            pl.BlockSpec((1, HD), lambda c, h: (0, h)),
            pl.BlockSpec((tiles_dev, 1, key_len), lambda c, h: (0, 0, 0)),
            pl.BlockSpec((8, 128), lambda c, h: (0, 0)),
        ] + k_specs + v_specs,
        out_specs=pl.BlockSpec((1, tok_dev, HD), lambda c, h: (c, 0, h)),
        cost_estimate=pl.CostEstimate(
            flops=4 * rows_c * tok_dev * key_len * width,
            transcendentals=rows_c * tok_dev * key_len * groups,
            bytes_accessed=4 * q_raw.size + 4 * slots * k_raw.size,
        ),
    )(
        q_raw, factor_of(q_total), q_gain.reshape(1, width), k_fac, k_gain.reshape(1, width),
        self_mask, slot_ok, *k_args, *v_args,
    )
    return (self_out, cross_out)


def solution(mesh):
    in_specs = (
        P(None, "frame", "head"),
        P(None, "frame", "head"),
        P(None, "frame", "head"),
        P(None, "frame", "head"),
        P(None, "frame", "head"),
        P(None, "frame", "head"),
        P("head"),
        P("head"),
        P("head"),
        P("head"),
        P("frame", None),
        P("frame"),
        P(),
    )
    out_specs = (P(None, "frame", "head"), P(None, "frame", "head"))
    return jax.shard_map(body, mesh=mesh, in_specs=in_specs, out_specs=out_specs, check_vma=False)
```

```python
import functools
import math

import jax
import jax.numpy as jnp
import numpy as np
from jax import lax
from jax.experimental import pallas as pl
from jax.experimental.pallas import tpu as pltpu
from jax.sharding import PartitionSpec as P

D = 5120
HD = 128
NB = 14
REACH = 2
MESH = pl.DeviceIdType.MESH

EPSILON = 1e-06

TEXT_BITS = (4, 2, 1, 32, 16, 8)
EARLY_TEXT_STEPS = 4
KV_CHUNKS = 4


def text_bits(n_frame):
    return [b for b in TEXT_BITS if b < n_frame]


def squares(tensor):
    values = tensor.astype(jnp.float32)
    return jnp.sum(values * values, axis=-1)


def factor_of(totals):
    return lax.rsqrt(totals / D + EPSILON)[..., None]


class _Pair:
    def __init__(self, first, second):
        self.parts = (first, second)

    def start(self):
        for p in self.parts:
            p.start()

    def wait_send(self):
        for p in self.parts:
            p.wait_send()

    def wait_recv(self):
        for p in self.parts:
            p.wait_recv()


def kv_kernel(k_own, v_own, kv_nb, kv_send, kv_recv, *, n_frame, chunks):
    f = lax.axis_index("frame")
    h = lax.axis_index("head")
    has_prev = f >= 1
    has_next = f <= n_frame - 2

    barrier = pltpu.get_barrier_semaphore()

    @pl.when(has_prev)
    def _():
        pl.semaphore_signal(barrier, inc=1, device_id=(f - 1, h), device_id_type=MESH)

    @pl.when(has_next)
    def _():
        pl.semaphore_signal(barrier, inc=1, device_id=(f + 1, h), device_id_type=MESH)

    pl.semaphore_wait(barrier, has_prev.astype(jnp.int32) + has_next.astype(jnp.int32))

    span = k_own.shape[1] // chunks

    def hop(src, dst, i, step, slot, target):
        return pltpu.make_async_remote_copy(
            src_ref=src.at[..., pl.ds(i * span, span), :], dst_ref=dst.at[..., pl.ds(i * span, span), :],
            send_sem=kv_send.at[step, i], recv_sem=kv_recv.at[slot, i],
            device_id=(target, h), device_id_type=MESH)

    def own_hop(i, step, slot, target):
        return _Pair(hop(k_own, kv_nb.at[slot, 0], i, step, slot, target),
                     hop(v_own, kv_nb.at[slot, 1], i, step + 4, slot + 4, target))

    to_next = [own_hop(i, 0, 1, f + 1) for i in range(chunks)]
    to_prev = [own_hop(i, 1, 2, f - 1) for i in range(chunks)]
    fwd_next = [hop(kv_nb.at[1], kv_nb.at[0], i, 2, 0, f + 1) for i in range(chunks)]
    fwd_prev = [hop(kv_nb.at[2], kv_nb.at[3], i, 3, 3, f - 1) for i in range(chunks)]
    both = jnp.logical_and(has_prev, has_next)

    @pl.when(has_next)
    def _():
        for c in to_next:
            c.start()

    @pl.when(has_prev)
    def _():
        for c in to_prev:
            c.start()

    for i in range(chunks):
        @pl.when(has_prev)
        def _():
            to_next[i].wait_recv()

        @pl.when(has_next)
        def _():
            to_prev[i].wait_recv()

        @pl.when(both)
        def _():
            fwd_next[i].start()
            fwd_prev[i].start()

    for i in range(chunks):
        @pl.when(has_next)
        def _():
            to_next[i].wait_send()

        @pl.when(has_prev)
        def _():
            to_prev[i].wait_send()

        @pl.when(f >= 2)
        def _():
            fwd_next[i].wait_recv()

        @pl.when(f <= n_frame - 3)
        def _():
            fwd_prev[i].wait_recv()

        @pl.when(both)
        def _():
            fwd_next[i].wait_send()
            fwd_prev[i].wait_send()


def text_kernel(text_own, text_all, tx_send, tx_recv, local_sem, *, bits, rows):
    f = lax.axis_index("frame")
    h = lax.axis_index("head")
    barrier = pltpu.get_barrier_semaphore()
    for b in bits:
        pl.semaphore_signal(barrier, inc=1, device_id=(f ^ b, h), device_id_type=MESH)
    pl.semaphore_wait(barrier, len(bits))

    pos = 0
    for i, b in enumerate(bits):
        pos = pos + ((f // b) % 2) * (1 << i)
    mine = pltpu.make_async_copy(
        text_own, text_all.at[:, pl.ds(pl.multiple_of(pos * rows, rows), rows)], local_sem.at[0])
    mine.start()
    mine.wait()
    for i, b in enumerate(bits):
        size = rows << i
        start = pl.multiple_of((pos >> i) * size, size)
        swap = pltpu.make_async_remote_copy(
            src_ref=text_all.at[:, pl.ds(start, size)], dst_ref=text_all.at[:, pl.ds(start, size)],
            send_sem=tx_send.at[i], recv_sem=tx_recv.at[i], device_id=(f ^ b, h), device_id_type=MESH)
        swap.start()
        swap.wait_send()
        swap.wait_recv()


def exchange(k_own, v_own, text_own, n_frame):
    kv_shape = (2,) + k_own.shape
    kv_nb = pl.pallas_call(
        functools.partial(kv_kernel, n_frame=n_frame, chunks=KV_CHUNKS),
        out_shape=jax.ShapeDtypeStruct((4,) + kv_shape, k_own.dtype),
        in_specs=[pl.BlockSpec(memory_space=pl.ANY)] * 2,
        out_specs=pl.BlockSpec(memory_space=pl.ANY),
        scratch_shapes=[
            pltpu.SemaphoreType.DMA((8, KV_CHUNKS)),
            pltpu.SemaphoreType.DMA((8, KV_CHUNKS)),
        ],
        compiler_params=pltpu.CompilerParams(collective_id=0, has_side_effects=True),
    )(k_own, v_own)
    bits = text_bits(n_frame)
    rows = text_own.shape[1]
    text_all = pl.pallas_call(
        functools.partial(text_kernel, bits=bits, rows=rows),
        out_shape=jax.ShapeDtypeStruct((text_own.shape[0], rows * n_frame, text_own.shape[2]), text_own.dtype),
        in_specs=[pl.BlockSpec(memory_space=pl.ANY)],
        out_specs=pl.BlockSpec(memory_space=pl.ANY),
        scratch_shapes=[
            pltpu.SemaphoreType.DMA((len(bits),)),
            pltpu.SemaphoreType.DMA((len(bits),)),
            pltpu.SemaphoreType.DMA((1,)),
        ],
        compiler_params=pltpu.CompilerParams(collective_id=1, has_side_effects=True),
    )(text_own)
    return kv_nb, text_all


def softmax_rows(scores):
    row_top = jnp.max(scores, axis=-1, keepdims=True)
    powers = jnp.exp(scores - row_top)
    inverse = 1.0 / jnp.sum(powers, axis=-1, keepdims=True)
    return (powers * inverse).astype(jnp.bfloat16)


def normalized(raw, fac, gain):
    return (raw.astype(jnp.float32) * fac * gain).astype(jnp.bfloat16)


def self_kernel(q_ref, qf_ref, qg_ref, kf_ref, kg_ref, mask_ref, ok_ref, *refs, score_scale, tiles, slots):
    k_refs = refs[:slots]
    v_refs = refs[slots:2 * slots]
    o_ref = refs[2 * slots]
    q = normalized(q_ref[0], qf_ref[0], qg_ref[...])
    span = q.shape[0]
    kg = kg_ref[...]
    parts = []
    for j in range(slots):
        k = normalized(k_refs[j][0], kf_ref[0, j], kg)
        parts.append(lax.dot_general(q, k, (((1,), (1,)), ((), ())), preferred_element_type=jnp.float32))
    scores = jnp.concatenate(parts, axis=1) * score_scale
    key_len = scores.shape[1]
    scores = scores.reshape(tiles, span // tiles, key_len)
    scores = jnp.where(mask_ref[...] > 0, scores, -1e30)
    weights = softmax_rows(scores).reshape(span, key_len)
    out = None
    for j in range(slots):
        v = jnp.where(ok_ref[j:j + 1, :] > 0, v_refs[j][0], jnp.zeros((), v_refs[j].dtype))
        part = jnp.dot(weights[:, j * span:(j + 1) * span], v, preferred_element_type=jnp.float32)
        out = part if out is None else out + part
    o_ref[0] = out.astype(o_ref.dtype)


def cross_kernel(q_ref, qf_ref, qg_ref, k_ref, kf_ref, kg_ref, v_ref, mask_ref, o_ref, *, score_scale):
    q = normalized(q_ref[0], qf_ref[0], qg_ref[...])
    k = normalized(k_ref[0], kf_ref[0], kg_ref[...])
    scores = lax.dot_general(q, k, (((1,), (1,)), ((), ())), preferred_element_type=jnp.float32)
    scores = jnp.where(mask_ref[0] > 0, scores * score_scale, -1e30)
    weights = softmax_rows(scores)
    out = jnp.dot(weights, v_ref[0], preferred_element_type=jnp.float32)
    o_ref[0] = out.astype(o_ref.dtype)


def body(
    q_raw,
    k_raw,
    v_in,
    cross_q_raw,
    text_k_raw,
    text_v,
    q_gain,
    k_gain,
    cross_q_gain,
    text_k_gain,
    nbr,
    nbr_count,
    text_len,
):
    rows_c, tok_dev, width = q_raw.shape
    groups = width // HD
    tiles_dev = nbr.shape[0]
    tile_len = tok_dev // tiles_dev
    n_frame = lax.axis_size("frame")
    me = lax.axis_index("frame")
    score_scale = 1.0 / math.sqrt(HD)
    slots = 2 * REACH + 1

    txt_rows = text_k_raw.shape[1]
    text_own = jnp.stack([text_k_raw, text_v]).reshape(2 * rows_c, txt_rows, width)
    kv_nb, text_all = exchange(k_raw, v_in, text_own, n_frame)
    text_all = text_all.reshape(2, rows_c, n_frame * txt_rows, width)

    k_nb_sq = squares(kv_nb[:, 0])
    q_total, k_total, k_nb_total, cross_total, text_total = lax.psum(
        (squares(q_raw), squares(k_raw), k_nb_sq, squares(cross_q_raw), squares(text_all[0])), "head"
    )
    k_fac = factor_of(
        jnp.stack([k_nb_total[0], k_nb_total[1], k_total, k_nb_total[2], k_nb_total[3]], axis=1)
    )

    bits = text_bits(n_frame)
    frame_of_pos = np.zeros(n_frame, np.int32)
    for p in range(n_frame):
        frame_of_pos[p] = sum(b for i, b in enumerate(bits) if (p >> i) & 1)
    token_of_row = (frame_of_pos[:, None] * txt_rows + np.arange(txt_rows)[None, :]).reshape(-1)
    text_mask = (jnp.asarray(token_of_row)[None, :] < text_len[:, None]).astype(jnp.int32)[:, None, :]

    text_len_all = n_frame * txt_rows
    cross_out = pl.pallas_call(
        functools.partial(cross_kernel, score_scale=score_scale),
        out_shape=jax.ShapeDtypeStruct(q_raw.shape, jnp.bfloat16),
        grid=(rows_c, groups),
        in_specs=[
            pl.BlockSpec((1, tok_dev, HD), lambda c, h: (c, 0, h)),
            pl.BlockSpec((1, tok_dev, 1), lambda c, h: (c, 0, 0)),
            pl.BlockSpec((1, HD), lambda c, h: (0, h)),
            pl.BlockSpec((1, text_len_all, HD), lambda c, h: (c, 0, h)),
            pl.BlockSpec((1, text_len_all, 1), lambda c, h: (c, 0, 0)),
            pl.BlockSpec((1, HD), lambda c, h: (0, h)),
            pl.BlockSpec((1, text_len_all, HD), lambda c, h: (c, 0, h)),
            pl.BlockSpec((1, 1, text_len_all), lambda c, h: (c, 0, 0)),
        ],
        out_specs=pl.BlockSpec((1, tok_dev, HD), lambda c, h: (c, 0, h)),
        cost_estimate=pl.CostEstimate(
            flops=4 * rows_c * tok_dev * text_len_all * width,
            transcendentals=rows_c * tok_dev * text_len_all * groups,
            bytes_accessed=4 * q_raw.size + 4 * text_all[0].size,
        ),
    )(
        cross_q_raw, factor_of(cross_total), cross_q_gain.reshape(1, width),
        text_all[0], factor_of(text_total), text_k_gain.reshape(1, width),
        text_all[1], text_mask,
    )

    first_tile = (me - REACH) * tiles_dev
    cand = first_tile + jnp.arange(slots * tiles_dev, dtype=jnp.int32)
    live_slot = jnp.arange(NB, dtype=jnp.int32)[None, :] < nbr_count[:, None]
    hit = (nbr[:, :, None] == cand[None, None, :]) & live_slot[:, :, None]
    live = jnp.any(hit, axis=1)
    self_mask = jnp.repeat(live.astype(jnp.int32), tile_len, axis=1)[:, None, :]
    shard_of_slot = me - REACH + jnp.arange(8, dtype=jnp.int32)
    slot_ok = (shard_of_slot >= 0) & (shard_of_slot < n_frame)
    slot_ok = jnp.broadcast_to(slot_ok.astype(jnp.int32)[:, None], (8, 128))

    nb_index = {0: 0, 1: 1, 3: 2, 4: 3}
    k_specs, v_specs, k_args, v_args = [], [], [], []
    for j in range(slots):
        if j == REACH:
            k_specs.append(pl.BlockSpec((1, tok_dev, HD), lambda c, h: (c, 0, h)))
            v_specs.append(pl.BlockSpec((1, tok_dev, HD), lambda c, h: (c, 0, h)))
            k_args.append(k_raw)
            v_args.append(v_in)
        else:
            s = nb_index[j]
            k_specs.append(pl.BlockSpec((None, None, 1, tok_dev, HD), lambda c, h, s=s: (s, 0, c, 0, h)))
            v_specs.append(pl.BlockSpec((None, None, 1, tok_dev, HD), lambda c, h, s=s: (s, 1, c, 0, h)))
            k_args.append(kv_nb)
            v_args.append(kv_nb)

    key_len = slots * tok_dev
    self_out = pl.pallas_call(
        functools.partial(self_kernel, score_scale=score_scale, tiles=tiles_dev, slots=slots),
        out_shape=jax.ShapeDtypeStruct(q_raw.shape, jnp.bfloat16),
        grid=(rows_c, groups),
        in_specs=[
            pl.BlockSpec((1, tok_dev, HD), lambda c, h: (c, 0, h)),
            pl.BlockSpec((1, tok_dev, 1), lambda c, h: (c, 0, 0)),
            pl.BlockSpec((1, HD), lambda c, h: (0, h)),
            pl.BlockSpec((1, slots, tok_dev, 1), lambda c, h: (c, 0, 0, 0)),
            pl.BlockSpec((1, HD), lambda c, h: (0, h)),
            pl.BlockSpec((tiles_dev, 1, key_len), lambda c, h: (0, 0, 0)),
            pl.BlockSpec((8, 128), lambda c, h: (0, 0)),
        ] + k_specs + v_specs,
        out_specs=pl.BlockSpec((1, tok_dev, HD), lambda c, h: (c, 0, h)),
        cost_estimate=pl.CostEstimate(
            flops=4 * rows_c * tok_dev * key_len * width,
            transcendentals=rows_c * tok_dev * key_len * groups,
            bytes_accessed=4 * q_raw.size + 4 * slots * k_raw.size,
        ),
    )(
        q_raw, factor_of(q_total), q_gain.reshape(1, width), k_fac, k_gain.reshape(1, width),
        self_mask, slot_ok, *k_args, *v_args,
    )
    return (self_out, cross_out)


def solution(mesh):
    in_specs = (
        P(None, "frame", "head"),
        P(None, "frame", "head"),
        P(None, "frame", "head"),
        P(None, "frame", "head"),
        P(None, "frame", "head"),
        P(None, "frame", "head"),
        P("head"),
        P("head"),
        P("head"),
        P("head"),
        P("frame", None),
        P("frame"),
        P(),
    )
    out_specs = (P(None, "frame", "head"), P(None, "frame", "head"))
    return jax.shard_map(body, mesh=mesh, in_specs=in_specs, out_specs=out_specs, check_vma=False)
```

```python
import functools
import math

import jax
import jax.numpy as jnp
import numpy as np
from jax import lax
from jax.experimental import pallas as pl
from jax.experimental.pallas import tpu as pltpu
from jax.sharding import PartitionSpec as P

D = 5120
HD = 128
NB = 14
REACH = 2
MESH = pl.DeviceIdType.MESH

EPSILON = 1e-06

TEXT_BITS = (4, 2, 1, 32, 16, 8)
EARLY_TEXT_STEPS = 4
KV_CHUNKS = 4


def text_bits(n_frame):
    return [b for b in TEXT_BITS if b < n_frame]


def text_orders(n_frame):
    first = text_bits(n_frame)
    second = first[:-2] + first[-2:][::-1] if len(first) >= 2 else first
    return [first, second]


def squares(tensor):
    values = tensor.astype(jnp.float32)
    return jnp.sum(values * values, axis=-1)


def factor_of(totals):
    return lax.rsqrt(totals / D + EPSILON)[..., None]


class _Pair:
    def __init__(self, first, second):
        self.parts = (first, second)

    def start(self):
        for p in self.parts:
            p.start()

    def wait_send(self):
        for p in self.parts:
            p.wait_send()

    def wait_recv(self):
        for p in self.parts:
            p.wait_recv()


def kv_kernel(k_own, v_own, kv_nb, kv_send, kv_recv, *, n_frame, chunks):
    f = lax.axis_index("frame")
    h = lax.axis_index("head")
    has_prev = f >= 1
    has_next = f <= n_frame - 2

    barrier = pltpu.get_barrier_semaphore()

    @pl.when(has_prev)
    def _():
        pl.semaphore_signal(barrier, inc=1, device_id=(f - 1, h), device_id_type=MESH)

    @pl.when(has_next)
    def _():
        pl.semaphore_signal(barrier, inc=1, device_id=(f + 1, h), device_id_type=MESH)

    pl.semaphore_wait(barrier, has_prev.astype(jnp.int32) + has_next.astype(jnp.int32))

    span = k_own.shape[1] // chunks

    def hop(src, dst, i, step, slot, target):
        return pltpu.make_async_remote_copy(
            src_ref=src.at[..., pl.ds(i * span, span), :], dst_ref=dst.at[..., pl.ds(i * span, span), :],
            send_sem=kv_send.at[step, i], recv_sem=kv_recv.at[slot, i],
            device_id=(target, h), device_id_type=MESH)

    def own_hop(i, step, slot, target):
        return _Pair(hop(k_own, kv_nb.at[slot, 0], i, step, slot, target),
                     hop(v_own, kv_nb.at[slot, 1], i, step + 4, slot + 4, target))

    to_next = [own_hop(i, 0, 1, f + 1) for i in range(chunks)]
    to_prev = [own_hop(i, 1, 2, f - 1) for i in range(chunks)]
    fwd_next = [hop(kv_nb.at[1], kv_nb.at[0], i, 2, 0, f + 1) for i in range(chunks)]
    fwd_prev = [hop(kv_nb.at[2], kv_nb.at[3], i, 3, 3, f - 1) for i in range(chunks)]
    both = jnp.logical_and(has_prev, has_next)

    @pl.when(has_next)
    def _():
        for c in to_next:
            c.start()

    @pl.when(has_prev)
    def _():
        for c in to_prev:
            c.start()

    for i in range(chunks):
        @pl.when(has_prev)
        def _():
            to_next[i].wait_recv()

        @pl.when(has_next)
        def _():
            to_prev[i].wait_recv()

        @pl.when(both)
        def _():
            fwd_next[i].start()
            fwd_prev[i].start()

    for i in range(chunks):
        @pl.when(has_next)
        def _():
            to_next[i].wait_send()

        @pl.when(has_prev)
        def _():
            to_prev[i].wait_send()

        @pl.when(f >= 2)
        def _():
            fwd_next[i].wait_recv()

        @pl.when(f <= n_frame - 3)
        def _():
            fwd_prev[i].wait_recv()

        @pl.when(both)
        def _():
            fwd_next[i].wait_send()
            fwd_prev[i].wait_send()


def text_kernel(text_own, text_all, tx_send, tx_recv, local_sem, *, orders, rows):
    f = lax.axis_index("frame")
    h = lax.axis_index("head")
    barrier = pltpu.get_barrier_semaphore()
    for b in orders[0]:
        pl.semaphore_signal(barrier, inc=1, device_id=(f ^ b, h), device_id_type=MESH)
    pl.semaphore_wait(barrier, len(orders[0]))

    streams = len(orders)
    lanes = text_own.shape[0] // streams
    positions = []
    for s, bits in enumerate(orders):
        pos = 0
        for i, b in enumerate(bits):
            pos = pos + ((f // b) % 2) * (1 << i)
        positions.append(pos)
        mine = pltpu.make_async_copy(
            text_own.at[pl.ds(s * lanes, lanes)],
            text_all.at[pl.ds(s * lanes, lanes), pl.ds(pl.multiple_of(pos * rows, rows), rows)],
            local_sem.at[s])
        mine.start()
        mine.wait()
    for i in range(len(orders[0])):
        swaps = []
        for s, bits in enumerate(orders):
            size = rows << i
            start = pl.multiple_of((positions[s] >> i) * size, size)
            block = text_all.at[pl.ds(s * lanes, lanes), pl.ds(start, size)]
            swap = pltpu.make_async_remote_copy(
                src_ref=block, dst_ref=block, send_sem=tx_send.at[s, i], recv_sem=tx_recv.at[s, i],
                device_id=(f ^ bits[i], h), device_id_type=MESH)
            swap.start()
            swaps.append(swap)
        for swap in swaps:
            swap.wait_send()
            swap.wait_recv()


def exchange(k_own, v_own, text_own, n_frame):
    kv_shape = (2,) + k_own.shape
    kv_nb = pl.pallas_call(
        functools.partial(kv_kernel, n_frame=n_frame, chunks=KV_CHUNKS),
        out_shape=jax.ShapeDtypeStruct((4,) + kv_shape, k_own.dtype),
        in_specs=[pl.BlockSpec(memory_space=pl.ANY)] * 2,
        out_specs=pl.BlockSpec(memory_space=pl.ANY),
        scratch_shapes=[
            pltpu.SemaphoreType.DMA((8, KV_CHUNKS)),
            pltpu.SemaphoreType.DMA((8, KV_CHUNKS)),
        ],
        compiler_params=pltpu.CompilerParams(collective_id=0, has_side_effects=True),
    )(k_own, v_own)
    orders = text_orders(n_frame)
    rows = text_own.shape[1]
    text_all = pl.pallas_call(
        functools.partial(text_kernel, orders=orders, rows=rows),
        out_shape=jax.ShapeDtypeStruct((text_own.shape[0], rows * n_frame, text_own.shape[2]), text_own.dtype),
        in_specs=[pl.BlockSpec(memory_space=pl.ANY)],
        out_specs=pl.BlockSpec(memory_space=pl.ANY),
        scratch_shapes=[
            pltpu.SemaphoreType.DMA((len(orders), len(orders[0]))),
            pltpu.SemaphoreType.DMA((len(orders), len(orders[0]))),
            pltpu.SemaphoreType.DMA((len(orders),)),
        ],
        compiler_params=pltpu.CompilerParams(collective_id=1, has_side_effects=True),
    )(text_own)
    return kv_nb, text_all


def softmax_rows(scores):
    row_top = jnp.max(scores, axis=-1, keepdims=True)
    powers = jnp.exp(scores - row_top)
    inverse = 1.0 / jnp.sum(powers, axis=-1, keepdims=True)
    return (powers * inverse).astype(jnp.bfloat16)


def normalized(raw, fac, gain):
    return (raw.astype(jnp.float32) * fac * gain).astype(jnp.bfloat16)


def self_kernel(q_ref, qf_ref, qg_ref, kf_ref, kg_ref, mask_ref, ok_ref, *refs, score_scale, tiles, slots):
    k_refs = refs[:slots]
    v_refs = refs[slots:2 * slots]
    o_ref = refs[2 * slots]
    q = normalized(q_ref[0], qf_ref[0], qg_ref[...])
    span = q.shape[0]
    kg = kg_ref[...]
    parts = []
    for j in range(slots):
        k = normalized(k_refs[j][0], kf_ref[0, j], kg)
        parts.append(lax.dot_general(q, k, (((1,), (1,)), ((), ())), preferred_element_type=jnp.float32))
    scores = jnp.concatenate(parts, axis=1) * score_scale
    key_len = scores.shape[1]
    scores = scores.reshape(tiles, span // tiles, key_len)
    scores = jnp.where(mask_ref[...] > 0, scores, -1e30)
    weights = softmax_rows(scores).reshape(span, key_len)
    out = None
    for j in range(slots):
        v = jnp.where(ok_ref[j:j + 1, :] > 0, v_refs[j][0], jnp.zeros((), v_refs[j].dtype))
        part = jnp.dot(weights[:, j * span:(j + 1) * span], v, preferred_element_type=jnp.float32)
        out = part if out is None else out + part
    o_ref[0] = out.astype(o_ref.dtype)


def cross_kernel(q_ref, qf_ref, qg_ref, k_ref, kf_ref, kg_ref, v_ref, mask_ref, o_ref, *, score_scale):
    q = normalized(q_ref[0], qf_ref[0], qg_ref[...])
    k = normalized(k_ref[0], kf_ref[0], kg_ref[...])
    scores = lax.dot_general(q, k, (((1,), (1,)), ((), ())), preferred_element_type=jnp.float32)
    scores = jnp.where(mask_ref[0] > 0, scores * score_scale, -1e30)
    weights = softmax_rows(scores)
    out = jnp.dot(weights, v_ref[0], preferred_element_type=jnp.float32)
    o_ref[0] = out.astype(o_ref.dtype)


def body(
    q_raw,
    k_raw,
    v_in,
    cross_q_raw,
    text_k_raw,
    text_v,
    q_gain,
    k_gain,
    cross_q_gain,
    text_k_gain,
    nbr,
    nbr_count,
    text_len,
):
    rows_c, tok_dev, width = q_raw.shape
    groups = width // HD
    tiles_dev = nbr.shape[0]
    tile_len = tok_dev // tiles_dev
    n_frame = lax.axis_size("frame")
    me = lax.axis_index("frame")
    score_scale = 1.0 / math.sqrt(HD)
    slots = 2 * REACH + 1

    txt_rows = text_k_raw.shape[1]
    text_own = jnp.stack([text_k_raw, text_v], axis=1).reshape(2 * rows_c, txt_rows, width)
    kv_nb, text_all = exchange(k_raw, v_in, text_own, n_frame)
    text_all = jnp.swapaxes(text_all.reshape(rows_c, 2, n_frame * txt_rows, width), 0, 1)

    k_nb_sq = squares(kv_nb[:, 0])
    q_total, k_total, k_nb_total, cross_total, text_total = lax.psum(
        (squares(q_raw), squares(k_raw), k_nb_sq, squares(cross_q_raw), squares(text_all[0])), "head"
    )
    k_fac = factor_of(
        jnp.stack([k_nb_total[0], k_nb_total[1], k_total, k_nb_total[2], k_nb_total[3]], axis=1)
    )

    token_rows = []
    for bits in text_orders(n_frame):
        frame_of_pos = np.zeros(n_frame, np.int32)
        for p in range(n_frame):
            frame_of_pos[p] = sum(b for i, b in enumerate(bits) if (p >> i) & 1)
        token_rows.append((frame_of_pos[:, None] * txt_rows + np.arange(txt_rows)[None, :]).reshape(-1))
    token_of_row = np.stack(token_rows)
    text_mask = (jnp.asarray(token_of_row) < text_len[:, None]).astype(jnp.int32)[:, None, :]

    text_len_all = n_frame * txt_rows
    cross_out = pl.pallas_call(
        functools.partial(cross_kernel, score_scale=score_scale),
        out_shape=jax.ShapeDtypeStruct(q_raw.shape, jnp.bfloat16),
        grid=(rows_c, groups),
        in_specs=[
            pl.BlockSpec((1, tok_dev, HD), lambda c, h: (c, 0, h)),
            pl.BlockSpec((1, tok_dev, 1), lambda c, h: (c, 0, 0)),
            pl.BlockSpec((1, HD), lambda c, h: (0, h)),
            pl.BlockSpec((1, text_len_all, HD), lambda c, h: (c, 0, h)),
            pl.BlockSpec((1, text_len_all, 1), lambda c, h: (c, 0, 0)),
            pl.BlockSpec((1, HD), lambda c, h: (0, h)),
            pl.BlockSpec((1, text_len_all, HD), lambda c, h: (c, 0, h)),
            pl.BlockSpec((1, 1, text_len_all), lambda c, h: (c, 0, 0)),
        ],
        out_specs=pl.BlockSpec((1, tok_dev, HD), lambda c, h: (c, 0, h)),
        cost_estimate=pl.CostEstimate(
            flops=4 * rows_c * tok_dev * text_len_all * width,
            transcendentals=rows_c * tok_dev * text_len_all * groups,
            bytes_accessed=4 * q_raw.size + 4 * text_all[0].size,
        ),
    )(
        cross_q_raw, factor_of(cross_total), cross_q_gain.reshape(1, width),
        text_all[0], factor_of(text_total), text_k_gain.reshape(1, width),
        text_all[1], text_mask,
    )

    first_tile = (me - REACH) * tiles_dev
    cand = first_tile + jnp.arange(slots * tiles_dev, dtype=jnp.int32)
    live_slot = jnp.arange(NB, dtype=jnp.int32)[None, :] < nbr_count[:, None]
    hit = (nbr[:, :, None] == cand[None, None, :]) & live_slot[:, :, None]
    live = jnp.any(hit, axis=1)
    self_mask = jnp.repeat(live.astype(jnp.int32), tile_len, axis=1)[:, None, :]
    shard_of_slot = me - REACH + jnp.arange(8, dtype=jnp.int32)
    slot_ok = (shard_of_slot >= 0) & (shard_of_slot < n_frame)
    slot_ok = jnp.broadcast_to(slot_ok.astype(jnp.int32)[:, None], (8, 128))

    nb_index = {0: 0, 1: 1, 3: 2, 4: 3}
    k_specs, v_specs, k_args, v_args = [], [], [], []
    for j in range(slots):
        if j == REACH:
            k_specs.append(pl.BlockSpec((1, tok_dev, HD), lambda c, h: (c, 0, h)))
            v_specs.append(pl.BlockSpec((1, tok_dev, HD), lambda c, h: (c, 0, h)))
            k_args.append(k_raw)
            v_args.append(v_in)
        else:
            s = nb_index[j]
            k_specs.append(pl.BlockSpec((None, None, 1, tok_dev, HD), lambda c, h, s=s: (s, 0, c, 0, h)))
            v_specs.append(pl.BlockSpec((None, None, 1, tok_dev, HD), lambda c, h, s=s: (s, 1, c, 0, h)))
            k_args.append(kv_nb)
            v_args.append(kv_nb)

    key_len = slots * tok_dev
    self_out = pl.pallas_call(
        functools.partial(self_kernel, score_scale=score_scale, tiles=tiles_dev, slots=slots),
        out_shape=jax.ShapeDtypeStruct(q_raw.shape, jnp.bfloat16),
        grid=(rows_c, groups),
        in_specs=[
            pl.BlockSpec((1, tok_dev, HD), lambda c, h: (c, 0, h)),
            pl.BlockSpec((1, tok_dev, 1), lambda c, h: (c, 0, 0)),
            pl.BlockSpec((1, HD), lambda c, h: (0, h)),
            pl.BlockSpec((1, slots, tok_dev, 1), lambda c, h: (c, 0, 0, 0)),
            pl.BlockSpec((1, HD), lambda c, h: (0, h)),
            pl.BlockSpec((tiles_dev, 1, key_len), lambda c, h: (0, 0, 0)),
            pl.BlockSpec((8, 128), lambda c, h: (0, 0)),
        ] + k_specs + v_specs,
        out_specs=pl.BlockSpec((1, tok_dev, HD), lambda c, h: (c, 0, h)),
        cost_estimate=pl.CostEstimate(
            flops=4 * rows_c * tok_dev * key_len * width,
            transcendentals=rows_c * tok_dev * key_len * groups,
            bytes_accessed=4 * q_raw.size + 4 * slots * k_raw.size,
        ),
    )(
        q_raw, factor_of(q_total), q_gain.reshape(1, width), k_fac, k_gain.reshape(1, width),
        self_mask, slot_ok, *k_args, *v_args,
    )
    return (self_out, cross_out)


def solution(mesh):
    in_specs = (
        P(None, "frame", "head"),
        P(None, "frame", "head"),
        P(None, "frame", "head"),
        P(None, "frame", "head"),
        P(None, "frame", "head"),
        P(None, "frame", "head"),
        P("head"),
        P("head"),
        P("head"),
        P("head"),
        P("frame", None),
        P("frame"),
        P(),
    )
    out_specs = (P(None, "frame", "head"), P(None, "frame", "head"))
    return jax.shard_map(body, mesh=mesh, in_specs=in_specs, out_specs=out_specs, check_vma=False)
```

```python
import functools
import math

import jax
import jax.numpy as jnp
import numpy as np
from jax import lax
from jax.experimental import pallas as pl
from jax.experimental.pallas import tpu as pltpu
from jax.sharding import PartitionSpec as P

D = 5120
HD = 128
NB = 14
REACH = 2
MESH = pl.DeviceIdType.MESH

EPSILON = 1e-06

TEXT_BITS = (4, 2, 1, 32, 16, 8)
EARLY_TEXT_STEPS = 4
KV_CHUNKS = 4


def text_bits(n_frame):
    return [b for b in TEXT_BITS if b < n_frame]


def text_orders(n_frame):
    first = text_bits(n_frame)
    second = first[:-2] + first[-2:][::-1] if len(first) >= 2 else first
    return [first, second]


def direct_steps(orders):
    shared = 0
    while shared < min(3, len(orders[0])) and all(o[shared] == orders[0][shared] for o in orders):
        shared += 1
    return shared


def squares(tensor):
    values = tensor.astype(jnp.float32)
    return jnp.sum(values * values, axis=-1)


def factor_of(totals):
    return lax.rsqrt(totals / D + EPSILON)[..., None]


class _Pair:
    def __init__(self, first, second):
        self.parts = (first, second)

    def start(self):
        for p in self.parts:
            p.start()

    def wait_send(self):
        for p in self.parts:
            p.wait_send()

    def wait_recv(self):
        for p in self.parts:
            p.wait_recv()


def kv_kernel(k_own, v_own, kv_nb, kv_send, kv_recv, *, n_frame, chunks):
    f = lax.axis_index("frame")
    h = lax.axis_index("head")
    has_prev = f >= 1
    has_next = f <= n_frame - 2

    barrier = pltpu.get_barrier_semaphore()

    @pl.when(has_prev)
    def _():
        pl.semaphore_signal(barrier, inc=1, device_id=(f - 1, h), device_id_type=MESH)

    @pl.when(has_next)
    def _():
        pl.semaphore_signal(barrier, inc=1, device_id=(f + 1, h), device_id_type=MESH)

    pl.semaphore_wait(barrier, has_prev.astype(jnp.int32) + has_next.astype(jnp.int32))

    span = k_own.shape[1] // chunks

    def hop(src, dst, i, step, slot, target):
        return pltpu.make_async_remote_copy(
            src_ref=src.at[..., pl.ds(i * span, span), :], dst_ref=dst.at[..., pl.ds(i * span, span), :],
            send_sem=kv_send.at[step, i], recv_sem=kv_recv.at[slot, i],
            device_id=(target, h), device_id_type=MESH)

    def own_hop(i, step, slot, target):
        return _Pair(hop(k_own, kv_nb.at[slot, 0], i, step, slot, target),
                     hop(v_own, kv_nb.at[slot, 1], i, step + 4, slot + 4, target))

    to_next = [own_hop(i, 0, 1, f + 1) for i in range(chunks)]
    to_prev = [own_hop(i, 1, 2, f - 1) for i in range(chunks)]
    fwd_next = [hop(kv_nb.at[1], kv_nb.at[0], i, 2, 0, f + 1) for i in range(chunks)]
    fwd_prev = [hop(kv_nb.at[2], kv_nb.at[3], i, 3, 3, f - 1) for i in range(chunks)]
    both = jnp.logical_and(has_prev, has_next)

    @pl.when(has_next)
    def _():
        for c in to_next:
            c.start()

    @pl.when(has_prev)
    def _():
        for c in to_prev:
            c.start()

    for i in range(chunks):
        @pl.when(has_prev)
        def _():
            to_next[i].wait_recv()

        @pl.when(has_next)
        def _():
            to_prev[i].wait_recv()

        @pl.when(both)
        def _():
            fwd_next[i].start()
            fwd_prev[i].start()

    for i in range(chunks):
        @pl.when(has_next)
        def _():
            to_next[i].wait_send()

        @pl.when(has_prev)
        def _():
            to_prev[i].wait_send()

        @pl.when(f >= 2)
        def _():
            fwd_next[i].wait_recv()

        @pl.when(f <= n_frame - 3)
        def _():
            fwd_prev[i].wait_recv()

        @pl.when(both)
        def _():
            fwd_next[i].wait_send()
            fwd_prev[i].wait_send()


def text_kernel(text_own, text_all, tx_send, tx_recv, dx_send, dx_recv, local_sem, *, orders, rows):
    f = lax.axis_index("frame")
    h = lax.axis_index("head")
    barrier = pltpu.get_barrier_semaphore()
    shared = direct_steps(orders)
    masks = [sum(orders[0][i] for i in range(shared) if (d >> i) & 1) for d in range(1, 1 << shared)]
    masks += list(orders[0][shared:])
    for m in masks:
        pl.semaphore_signal(barrier, inc=1, device_id=(f ^ m, h), device_id_type=MESH)
    pl.semaphore_wait(barrier, len(masks))

    streams = len(orders)
    lanes = text_own.shape[0] // streams
    shared = direct_steps(orders)
    positions = []
    for s, bits in enumerate(orders):
        pos = 0
        for i, b in enumerate(bits):
            pos = pos + ((f // b) % 2) * (1 << i)
        positions.append(pos)
        mine = pltpu.make_async_copy(
            text_own.at[pl.ds(s * lanes, lanes)],
            text_all.at[pl.ds(s * lanes, lanes), pl.ds(pl.multiple_of(pos * rows, rows), rows)],
            local_sem.at[s])
        mine.start()
        mine.wait()
    sends = []
    for s in range(streams):
        own_rows = text_all.at[pl.ds(s * lanes, lanes), pl.ds(pl.multiple_of(positions[s] * rows, rows), rows)]
        for d in range(1, 1 << shared):
            mask = sum(orders[0][i] for i in range(shared) if (d >> i) & 1)
            copy = pltpu.make_async_remote_copy(
                src_ref=own_rows, dst_ref=own_rows, send_sem=dx_send.at[s, d - 1],
                recv_sem=dx_recv.at[s, d - 1], device_id=(f ^ mask, h), device_id_type=MESH)
            copy.start()
            sends.append(copy)
    for copy in sends:
        copy.wait_send()
        copy.wait_recv()
    for i in range(shared, len(orders[0])):
        swaps = []
        for s, bits in enumerate(orders):
            size = rows << i
            start = pl.multiple_of((positions[s] >> i) * size, size)
            block = text_all.at[pl.ds(s * lanes, lanes), pl.ds(start, size)]
            swap = pltpu.make_async_remote_copy(
                src_ref=block, dst_ref=block, send_sem=tx_send.at[s, i], recv_sem=tx_recv.at[s, i],
                device_id=(f ^ bits[i], h), device_id_type=MESH)
            swap.start()
            swaps.append(swap)
        for swap in swaps:
            swap.wait_send()
            swap.wait_recv()


def exchange(k_own, v_own, text_own, n_frame):
    kv_shape = (2,) + k_own.shape
    kv_nb = pl.pallas_call(
        functools.partial(kv_kernel, n_frame=n_frame, chunks=KV_CHUNKS),
        out_shape=jax.ShapeDtypeStruct((4,) + kv_shape, k_own.dtype),
        in_specs=[pl.BlockSpec(memory_space=pl.ANY)] * 2,
        out_specs=pl.BlockSpec(memory_space=pl.ANY),
        scratch_shapes=[
            pltpu.SemaphoreType.DMA((8, KV_CHUNKS)),
            pltpu.SemaphoreType.DMA((8, KV_CHUNKS)),
        ],
        compiler_params=pltpu.CompilerParams(collective_id=0, has_side_effects=True),
    )(k_own, v_own)
    orders = text_orders(n_frame)
    rows = text_own.shape[1]
    text_all = pl.pallas_call(
        functools.partial(text_kernel, orders=orders, rows=rows),
        out_shape=jax.ShapeDtypeStruct((text_own.shape[0], rows * n_frame, text_own.shape[2]), text_own.dtype),
        in_specs=[pl.BlockSpec(memory_space=pl.ANY)],
        out_specs=pl.BlockSpec(memory_space=pl.ANY),
        scratch_shapes=[
            pltpu.SemaphoreType.DMA((len(orders), len(orders[0]))),
            pltpu.SemaphoreType.DMA((len(orders), len(orders[0]))),
            pltpu.SemaphoreType.DMA((len(orders), (1 << direct_steps(orders)) - 1)),
            pltpu.SemaphoreType.DMA((len(orders), (1 << direct_steps(orders)) - 1)),
            pltpu.SemaphoreType.DMA((len(orders),)),
        ],
        compiler_params=pltpu.CompilerParams(collective_id=1, has_side_effects=True),
    )(text_own)
    return kv_nb, text_all


def softmax_rows(scores):
    row_top = jnp.max(scores, axis=-1, keepdims=True)
    powers = jnp.exp(scores - row_top)
    inverse = 1.0 / jnp.sum(powers, axis=-1, keepdims=True)
    return (powers * inverse).astype(jnp.bfloat16)


def normalized(raw, fac, gain):
    return (raw.astype(jnp.float32) * fac * gain).astype(jnp.bfloat16)


def self_kernel(q_ref, qf_ref, qg_ref, kf_ref, kg_ref, mask_ref, ok_ref, *refs, score_scale, tiles, slots):
    k_refs = refs[:slots]
    v_refs = refs[slots:2 * slots]
    o_ref = refs[2 * slots]
    q = normalized(q_ref[0], qf_ref[0], qg_ref[...])
    span = q.shape[0]
    kg = kg_ref[...]
    parts = []
    for j in range(slots):
        k = normalized(k_refs[j][0], kf_ref[0, j], kg)
        parts.append(lax.dot_general(q, k, (((1,), (1,)), ((), ())), preferred_element_type=jnp.float32))
    scores = jnp.concatenate(parts, axis=1) * score_scale
    key_len = scores.shape[1]
    scores = scores.reshape(tiles, span // tiles, key_len)
    scores = jnp.where(mask_ref[...] > 0, scores, -1e30)
    weights = softmax_rows(scores).reshape(span, key_len)
    out = None
    for j in range(slots):
        v = jnp.where(ok_ref[j:j + 1, :] > 0, v_refs[j][0], jnp.zeros((), v_refs[j].dtype))
        part = jnp.dot(weights[:, j * span:(j + 1) * span], v, preferred_element_type=jnp.float32)
        out = part if out is None else out + part
    o_ref[0] = out.astype(o_ref.dtype)


def cross_kernel(q_ref, qf_ref, qg_ref, k_ref, kf_ref, kg_ref, v_ref, mask_ref, o_ref, *, score_scale):
    q = normalized(q_ref[0], qf_ref[0], qg_ref[...])
    k = normalized(k_ref[0], kf_ref[0], kg_ref[...])
    scores = lax.dot_general(q, k, (((1,), (1,)), ((), ())), preferred_element_type=jnp.float32)
    scores = jnp.where(mask_ref[0] > 0, scores * score_scale, -1e30)
    weights = softmax_rows(scores)
    out = jnp.dot(weights, v_ref[0], preferred_element_type=jnp.float32)
    o_ref[0] = out.astype(o_ref.dtype)


def body(
    q_raw,
    k_raw,
    v_in,
    cross_q_raw,
    text_k_raw,
    text_v,
    q_gain,
    k_gain,
    cross_q_gain,
    text_k_gain,
    nbr,
    nbr_count,
    text_len,
):
    rows_c, tok_dev, width = q_raw.shape
    groups = width // HD
    tiles_dev = nbr.shape[0]
    tile_len = tok_dev // tiles_dev
    n_frame = lax.axis_size("frame")
    me = lax.axis_index("frame")
    score_scale = 1.0 / math.sqrt(HD)
    slots = 2 * REACH + 1

    txt_rows = text_k_raw.shape[1]
    text_own = jnp.stack([text_k_raw, text_v], axis=1).reshape(2 * rows_c, txt_rows, width)
    kv_nb, text_all = exchange(k_raw, v_in, text_own, n_frame)
    text_all = jnp.swapaxes(text_all.reshape(rows_c, 2, n_frame * txt_rows, width), 0, 1)

    k_nb_sq = squares(kv_nb[:, 0])
    q_total, k_total, k_nb_total, cross_total, text_total = lax.psum(
        (squares(q_raw), squares(k_raw), k_nb_sq, squares(cross_q_raw), squares(text_all[0])), "head"
    )
    k_fac = factor_of(
        jnp.stack([k_nb_total[0], k_nb_total[1], k_total, k_nb_total[2], k_nb_total[3]], axis=1)
    )

    token_rows = []
    for bits in text_orders(n_frame):
        frame_of_pos = np.zeros(n_frame, np.int32)
        for p in range(n_frame):
            frame_of_pos[p] = sum(b for i, b in enumerate(bits) if (p >> i) & 1)
        token_rows.append((frame_of_pos[:, None] * txt_rows + np.arange(txt_rows)[None, :]).reshape(-1))
    token_of_row = np.stack(token_rows)
    text_mask = (jnp.asarray(token_of_row) < text_len[:, None]).astype(jnp.int32)[:, None, :]

    text_len_all = n_frame * txt_rows
    cross_out = pl.pallas_call(
        functools.partial(cross_kernel, score_scale=score_scale),
        out_shape=jax.ShapeDtypeStruct(q_raw.shape, jnp.bfloat16),
        grid=(rows_c, groups),
        in_specs=[
            pl.BlockSpec((1, tok_dev, HD), lambda c, h: (c, 0, h)),
            pl.BlockSpec((1, tok_dev, 1), lambda c, h: (c, 0, 0)),
            pl.BlockSpec((1, HD), lambda c, h: (0, h)),
            pl.BlockSpec((1, text_len_all, HD), lambda c, h: (c, 0, h)),
            pl.BlockSpec((1, text_len_all, 1), lambda c, h: (c, 0, 0)),
            pl.BlockSpec((1, HD), lambda c, h: (0, h)),
            pl.BlockSpec((1, text_len_all, HD), lambda c, h: (c, 0, h)),
            pl.BlockSpec((1, 1, text_len_all), lambda c, h: (c, 0, 0)),
        ],
        out_specs=pl.BlockSpec((1, tok_dev, HD), lambda c, h: (c, 0, h)),
        cost_estimate=pl.CostEstimate(
            flops=4 * rows_c * tok_dev * text_len_all * width,
            transcendentals=rows_c * tok_dev * text_len_all * groups,
            bytes_accessed=4 * q_raw.size + 4 * text_all[0].size,
        ),
    )(
        cross_q_raw, factor_of(cross_total), cross_q_gain.reshape(1, width),
        text_all[0], factor_of(text_total), text_k_gain.reshape(1, width),
        text_all[1], text_mask,
    )

    first_tile = (me - REACH) * tiles_dev
    cand = first_tile + jnp.arange(slots * tiles_dev, dtype=jnp.int32)
    live_slot = jnp.arange(NB, dtype=jnp.int32)[None, :] < nbr_count[:, None]
    hit = (nbr[:, :, None] == cand[None, None, :]) & live_slot[:, :, None]
    live = jnp.any(hit, axis=1)
    self_mask = jnp.repeat(live.astype(jnp.int32), tile_len, axis=1)[:, None, :]
    shard_of_slot = me - REACH + jnp.arange(8, dtype=jnp.int32)
    slot_ok = (shard_of_slot >= 0) & (shard_of_slot < n_frame)
    slot_ok = jnp.broadcast_to(slot_ok.astype(jnp.int32)[:, None], (8, 128))

    nb_index = {0: 0, 1: 1, 3: 2, 4: 3}
    k_specs, v_specs, k_args, v_args = [], [], [], []
    for j in range(slots):
        if j == REACH:
            k_specs.append(pl.BlockSpec((1, tok_dev, HD), lambda c, h: (c, 0, h)))
            v_specs.append(pl.BlockSpec((1, tok_dev, HD), lambda c, h: (c, 0, h)))
            k_args.append(k_raw)
            v_args.append(v_in)
        else:
            s = nb_index[j]
            k_specs.append(pl.BlockSpec((None, None, 1, tok_dev, HD), lambda c, h, s=s: (s, 0, c, 0, h)))
            v_specs.append(pl.BlockSpec((None, None, 1, tok_dev, HD), lambda c, h, s=s: (s, 1, c, 0, h)))
            k_args.append(kv_nb)
            v_args.append(kv_nb)

    key_len = slots * tok_dev
    self_out = pl.pallas_call(
        functools.partial(self_kernel, score_scale=score_scale, tiles=tiles_dev, slots=slots),
        out_shape=jax.ShapeDtypeStruct(q_raw.shape, jnp.bfloat16),
        grid=(rows_c, groups),
        in_specs=[
            pl.BlockSpec((1, tok_dev, HD), lambda c, h: (c, 0, h)),
            pl.BlockSpec((1, tok_dev, 1), lambda c, h: (c, 0, 0)),
            pl.BlockSpec((1, HD), lambda c, h: (0, h)),
            pl.BlockSpec((1, slots, tok_dev, 1), lambda c, h: (c, 0, 0, 0)),
            pl.BlockSpec((1, HD), lambda c, h: (0, h)),
            pl.BlockSpec((tiles_dev, 1, key_len), lambda c, h: (0, 0, 0)),
            pl.BlockSpec((8, 128), lambda c, h: (0, 0)),
        ] + k_specs + v_specs,
        out_specs=pl.BlockSpec((1, tok_dev, HD), lambda c, h: (c, 0, h)),
        cost_estimate=pl.CostEstimate(
            flops=4 * rows_c * tok_dev * key_len * width,
            transcendentals=rows_c * tok_dev * key_len * groups,
            bytes_accessed=4 * q_raw.size + 4 * slots * k_raw.size,
        ),
    )(
        q_raw, factor_of(q_total), q_gain.reshape(1, width), k_fac, k_gain.reshape(1, width),
        self_mask, slot_ok, *k_args, *v_args,
    )
    return (self_out, cross_out)


def solution(mesh):
    in_specs = (
        P(None, "frame", "head"),
        P(None, "frame", "head"),
        P(None, "frame", "head"),
        P(None, "frame", "head"),
        P(None, "frame", "head"),
        P(None, "frame", "head"),
        P("head"),
        P("head"),
        P("head"),
        P("head"),
        P("frame", None),
        P("frame"),
        P(),
    )
    out_specs = (P(None, "frame", "head"), P(None, "frame", "head"))
    return jax.shard_map(body, mesh=mesh, in_specs=in_specs, out_specs=out_specs, check_vma=False)
```

```python
import functools
import math

import jax
import jax.numpy as jnp
import numpy as np
from jax import lax
from jax.experimental import pallas as pl
from jax.experimental.pallas import tpu as pltpu
from jax.sharding import PartitionSpec as P

D = 5120
HD = 128
NB = 14
REACH = 2
MESH = pl.DeviceIdType.MESH

EPSILON = 1e-06

TEXT_BITS = (4, 2, 1, 32, 16, 8)
EARLY_TEXT_STEPS = 4
KV_CHUNKS = 4


def text_bits(n_frame):
    return [b for b in TEXT_BITS if b < n_frame]


def text_orders(n_frame):
    first = text_bits(n_frame)
    second = first[:-2] + first[-2:][::-1] if len(first) >= 2 else first
    return [first, second]


def direct_steps(orders):
    shared = 0
    while shared < min(4, len(orders[0])) and all(o[shared] == orders[0][shared] for o in orders):
        shared += 1
    return shared


def squares(tensor):
    values = tensor.astype(jnp.float32)
    return jnp.sum(values * values, axis=-1)


def factor_of(totals):
    return lax.rsqrt(totals / D + EPSILON)[..., None]


class _Pair:
    def __init__(self, first, second):
        self.parts = (first, second)

    def start(self):
        for p in self.parts:
            p.start()

    def wait_send(self):
        for p in self.parts:
            p.wait_send()

    def wait_recv(self):
        for p in self.parts:
            p.wait_recv()


def kv_kernel(k_own, v_own, kv_nb, kv_send, kv_recv, *, n_frame, chunks):
    f = lax.axis_index("frame")
    h = lax.axis_index("head")
    has_prev = f >= 1
    has_next = f <= n_frame - 2

    barrier = pltpu.get_barrier_semaphore()

    @pl.when(has_prev)
    def _():
        pl.semaphore_signal(barrier, inc=1, device_id=(f - 1, h), device_id_type=MESH)

    @pl.when(has_next)
    def _():
        pl.semaphore_signal(barrier, inc=1, device_id=(f + 1, h), device_id_type=MESH)

    pl.semaphore_wait(barrier, has_prev.astype(jnp.int32) + has_next.astype(jnp.int32))

    span = k_own.shape[1] // chunks

    def hop(src, dst, i, step, slot, target):
        return pltpu.make_async_remote_copy(
            src_ref=src.at[..., pl.ds(i * span, span), :], dst_ref=dst.at[..., pl.ds(i * span, span), :],
            send_sem=kv_send.at[step, i], recv_sem=kv_recv.at[slot, i],
            device_id=(target, h), device_id_type=MESH)

    def own_hop(i, step, slot, target):
        return _Pair(hop(k_own, kv_nb.at[slot, 0], i, step, slot, target),
                     hop(v_own, kv_nb.at[slot, 1], i, step + 4, slot + 4, target))

    to_next = [own_hop(i, 0, 1, f + 1) for i in range(chunks)]
    to_prev = [own_hop(i, 1, 2, f - 1) for i in range(chunks)]
    fwd_next = [hop(kv_nb.at[1], kv_nb.at[0], i, 2, 0, f + 1) for i in range(chunks)]
    fwd_prev = [hop(kv_nb.at[2], kv_nb.at[3], i, 3, 3, f - 1) for i in range(chunks)]
    both = jnp.logical_and(has_prev, has_next)

    @pl.when(has_next)
    def _():
        for c in to_next:
            c.start()

    @pl.when(has_prev)
    def _():
        for c in to_prev:
            c.start()

    for i in range(chunks):
        @pl.when(has_prev)
        def _():
            to_next[i].wait_recv()

        @pl.when(has_next)
        def _():
            to_prev[i].wait_recv()

        @pl.when(both)
        def _():
            fwd_next[i].start()
            fwd_prev[i].start()

    for i in range(chunks):
        @pl.when(has_next)
        def _():
            to_next[i].wait_send()

        @pl.when(has_prev)
        def _():
            to_prev[i].wait_send()

        @pl.when(f >= 2)
        def _():
            fwd_next[i].wait_recv()

        @pl.when(f <= n_frame - 3)
        def _():
            fwd_prev[i].wait_recv()

        @pl.when(both)
        def _():
            fwd_next[i].wait_send()
            fwd_prev[i].wait_send()


def text_kernel(text_own, text_all, tx_send, tx_recv, dx_send, dx_recv, local_sem, *, orders, rows):
    f = lax.axis_index("frame")
    h = lax.axis_index("head")
    barrier = pltpu.get_barrier_semaphore()
    shared = direct_steps(orders)
    masks = [sum(orders[0][i] for i in range(shared) if (d >> i) & 1) for d in range(1, 1 << shared)]
    masks += list(orders[0][shared:])
    for m in masks:
        pl.semaphore_signal(barrier, inc=1, device_id=(f ^ m, h), device_id_type=MESH)
    pl.semaphore_wait(barrier, len(masks))

    streams = len(orders)
    lanes = text_own.shape[0] // streams
    shared = direct_steps(orders)
    positions = []
    for s, bits in enumerate(orders):
        pos = 0
        for i, b in enumerate(bits):
            pos = pos + ((f // b) % 2) * (1 << i)
        positions.append(pos)
        mine = pltpu.make_async_copy(
            text_own.at[pl.ds(s * lanes, lanes)],
            text_all.at[pl.ds(s * lanes, lanes), pl.ds(pl.multiple_of(pos * rows, rows), rows)],
            local_sem.at[s])
        mine.start()
        mine.wait()
    sends = []
    for s in range(streams):
        own_rows = text_all.at[pl.ds(s * lanes, lanes), pl.ds(pl.multiple_of(positions[s] * rows, rows), rows)]
        for d in range(1, 1 << shared):
            mask = sum(orders[0][i] for i in range(shared) if (d >> i) & 1)
            copy = pltpu.make_async_remote_copy(
                src_ref=own_rows, dst_ref=own_rows, send_sem=dx_send.at[s, d - 1],
                recv_sem=dx_recv.at[s, d - 1], device_id=(f ^ mask, h), device_id_type=MESH)
            copy.start()
            sends.append(copy)
    for copy in sends:
        copy.wait_send()
        copy.wait_recv()
    for i in range(shared, len(orders[0])):
        swaps = []
        for s, bits in enumerate(orders):
            size = rows << i
            start = pl.multiple_of((positions[s] >> i) * size, size)
            block = text_all.at[pl.ds(s * lanes, lanes), pl.ds(start, size)]
            swap = pltpu.make_async_remote_copy(
                src_ref=block, dst_ref=block, send_sem=tx_send.at[s, i], recv_sem=tx_recv.at[s, i],
                device_id=(f ^ bits[i], h), device_id_type=MESH)
            swap.start()
            swaps.append(swap)
        for swap in swaps:
            swap.wait_send()
            swap.wait_recv()


def exchange(k_own, v_own, text_own, n_frame):
    kv_shape = (2,) + k_own.shape
    kv_nb = pl.pallas_call(
        functools.partial(kv_kernel, n_frame=n_frame, chunks=KV_CHUNKS),
        out_shape=jax.ShapeDtypeStruct((4,) + kv_shape, k_own.dtype),
        in_specs=[pl.BlockSpec(memory_space=pl.ANY)] * 2,
        out_specs=pl.BlockSpec(memory_space=pl.ANY),
        scratch_shapes=[
            pltpu.SemaphoreType.DMA((8, KV_CHUNKS)),
            pltpu.SemaphoreType.DMA((8, KV_CHUNKS)),
        ],
        compiler_params=pltpu.CompilerParams(collective_id=0, has_side_effects=True),
    )(k_own, v_own)
    orders = text_orders(n_frame)
    rows = text_own.shape[1]
    text_all = pl.pallas_call(
        functools.partial(text_kernel, orders=orders, rows=rows),
        out_shape=jax.ShapeDtypeStruct((text_own.shape[0], rows * n_frame, text_own.shape[2]), text_own.dtype),
        in_specs=[pl.BlockSpec(memory_space=pl.ANY)],
        out_specs=pl.BlockSpec(memory_space=pl.ANY),
        scratch_shapes=[
            pltpu.SemaphoreType.DMA((len(orders), len(orders[0]))),
            pltpu.SemaphoreType.DMA((len(orders), len(orders[0]))),
            pltpu.SemaphoreType.DMA((len(orders), (1 << direct_steps(orders)) - 1)),
            pltpu.SemaphoreType.DMA((len(orders), (1 << direct_steps(orders)) - 1)),
            pltpu.SemaphoreType.DMA((len(orders),)),
        ],
        compiler_params=pltpu.CompilerParams(collective_id=1, has_side_effects=True),
    )(text_own)
    return kv_nb, text_all


def softmax_rows(scores):
    row_top = jnp.max(scores, axis=-1, keepdims=True)
    powers = jnp.exp(scores - row_top)
    inverse = 1.0 / jnp.sum(powers, axis=-1, keepdims=True)
    return (powers * inverse).astype(jnp.bfloat16)


def normalized(raw, fac, gain):
    return (raw.astype(jnp.float32) * fac * gain).astype(jnp.bfloat16)


def self_kernel(q_ref, qf_ref, qg_ref, kf_ref, kg_ref, mask_ref, ok_ref, *refs, score_scale, tiles, slots):
    k_refs = refs[:slots]
    v_refs = refs[slots:2 * slots]
    o_ref = refs[2 * slots]
    q = normalized(q_ref[0], qf_ref[0], qg_ref[...])
    span = q.shape[0]
    kg = kg_ref[...]
    parts = []
    for j in range(slots):
        k = normalized(k_refs[j][0], kf_ref[0, j], kg)
        parts.append(lax.dot_general(q, k, (((1,), (1,)), ((), ())), preferred_element_type=jnp.float32))
    scores = jnp.concatenate(parts, axis=1) * score_scale
    key_len = scores.shape[1]
    scores = scores.reshape(tiles, span // tiles, key_len)
    scores = jnp.where(mask_ref[...] > 0, scores, -1e30)
    weights = softmax_rows(scores).reshape(span, key_len)
    out = None
    for j in range(slots):
        v = jnp.where(ok_ref[j:j + 1, :] > 0, v_refs[j][0], jnp.zeros((), v_refs[j].dtype))
        part = jnp.dot(weights[:, j * span:(j + 1) * span], v, preferred_element_type=jnp.float32)
        out = part if out is None else out + part
    o_ref[0] = out.astype(o_ref.dtype)


def cross_kernel(q_ref, qf_ref, qg_ref, k_ref, kf_ref, kg_ref, v_ref, mask_ref, o_ref, *, score_scale):
    q = normalized(q_ref[0], qf_ref[0], qg_ref[...])
    k = normalized(k_ref[0], kf_ref[0], kg_ref[...])
    scores = lax.dot_general(q, k, (((1,), (1,)), ((), ())), preferred_element_type=jnp.float32)
    scores = jnp.where(mask_ref[0] > 0, scores * score_scale, -1e30)
    weights = softmax_rows(scores)
    out = jnp.dot(weights, v_ref[0], preferred_element_type=jnp.float32)
    o_ref[0] = out.astype(o_ref.dtype)


def body(
    q_raw,
    k_raw,
    v_in,
    cross_q_raw,
    text_k_raw,
    text_v,
    q_gain,
    k_gain,
    cross_q_gain,
    text_k_gain,
    nbr,
    nbr_count,
    text_len,
):
    rows_c, tok_dev, width = q_raw.shape
    groups = width // HD
    tiles_dev = nbr.shape[0]
    tile_len = tok_dev // tiles_dev
    n_frame = lax.axis_size("frame")
    me = lax.axis_index("frame")
    score_scale = 1.0 / math.sqrt(HD)
    slots = 2 * REACH + 1

    txt_rows = text_k_raw.shape[1]
    text_own = jnp.stack([text_k_raw, text_v], axis=1).reshape(2 * rows_c, txt_rows, width)
    kv_nb, text_all = exchange(k_raw, v_in, text_own, n_frame)
    text_all = jnp.swapaxes(text_all.reshape(rows_c, 2, n_frame * txt_rows, width), 0, 1)

    k_nb_sq = squares(kv_nb[:, 0])
    q_total, k_total, k_nb_total, cross_total, text_total = lax.psum(
        (squares(q_raw), squares(k_raw), k_nb_sq, squares(cross_q_raw), squares(text_all[0])), "head"
    )
    k_fac = factor_of(
        jnp.stack([k_nb_total[0], k_nb_total[1], k_total, k_nb_total[2], k_nb_total[3]], axis=1)
    )

    token_rows = []
    for bits in text_orders(n_frame):
        frame_of_pos = np.zeros(n_frame, np.int32)
        for p in range(n_frame):
            frame_of_pos[p] = sum(b for i, b in enumerate(bits) if (p >> i) & 1)
        token_rows.append((frame_of_pos[:, None] * txt_rows + np.arange(txt_rows)[None, :]).reshape(-1))
    token_of_row = np.stack(token_rows)
    text_mask = (jnp.asarray(token_of_row) < text_len[:, None]).astype(jnp.int32)[:, None, :]

    text_len_all = n_frame * txt_rows
    cross_out = pl.pallas_call(
        functools.partial(cross_kernel, score_scale=score_scale),
        out_shape=jax.ShapeDtypeStruct(q_raw.shape, jnp.bfloat16),
        grid=(rows_c, groups),
        in_specs=[
            pl.BlockSpec((1, tok_dev, HD), lambda c, h: (c, 0, h)),
            pl.BlockSpec((1, tok_dev, 1), lambda c, h: (c, 0, 0)),
            pl.BlockSpec((1, HD), lambda c, h: (0, h)),
            pl.BlockSpec((1, text_len_all, HD), lambda c, h: (c, 0, h)),
            pl.BlockSpec((1, text_len_all, 1), lambda c, h: (c, 0, 0)),
            pl.BlockSpec((1, HD), lambda c, h: (0, h)),
            pl.BlockSpec((1, text_len_all, HD), lambda c, h: (c, 0, h)),
            pl.BlockSpec((1, 1, text_len_all), lambda c, h: (c, 0, 0)),
        ],
        out_specs=pl.BlockSpec((1, tok_dev, HD), lambda c, h: (c, 0, h)),
        cost_estimate=pl.CostEstimate(
            flops=4 * rows_c * tok_dev * text_len_all * width,
            transcendentals=rows_c * tok_dev * text_len_all * groups,
            bytes_accessed=4 * q_raw.size + 4 * text_all[0].size,
        ),
    )(
        cross_q_raw, factor_of(cross_total), cross_q_gain.reshape(1, width),
        text_all[0], factor_of(text_total), text_k_gain.reshape(1, width),
        text_all[1], text_mask,
    )

    first_tile = (me - REACH) * tiles_dev
    cand = first_tile + jnp.arange(slots * tiles_dev, dtype=jnp.int32)
    live_slot = jnp.arange(NB, dtype=jnp.int32)[None, :] < nbr_count[:, None]
    hit = (nbr[:, :, None] == cand[None, None, :]) & live_slot[:, :, None]
    live = jnp.any(hit, axis=1)
    self_mask = jnp.repeat(live.astype(jnp.int32), tile_len, axis=1)[:, None, :]
    shard_of_slot = me - REACH + jnp.arange(8, dtype=jnp.int32)
    slot_ok = (shard_of_slot >= 0) & (shard_of_slot < n_frame)
    slot_ok = jnp.broadcast_to(slot_ok.astype(jnp.int32)[:, None], (8, 128))

    nb_index = {0: 0, 1: 1, 3: 2, 4: 3}
    k_specs, v_specs, k_args, v_args = [], [], [], []
    for j in range(slots):
        if j == REACH:
            k_specs.append(pl.BlockSpec((1, tok_dev, HD), lambda c, h: (c, 0, h)))
            v_specs.append(pl.BlockSpec((1, tok_dev, HD), lambda c, h: (c, 0, h)))
            k_args.append(k_raw)
            v_args.append(v_in)
        else:
            s = nb_index[j]
            k_specs.append(pl.BlockSpec((None, None, 1, tok_dev, HD), lambda c, h, s=s: (s, 0, c, 0, h)))
            v_specs.append(pl.BlockSpec((None, None, 1, tok_dev, HD), lambda c, h, s=s: (s, 1, c, 0, h)))
            k_args.append(kv_nb)
            v_args.append(kv_nb)

    key_len = slots * tok_dev
    self_out = pl.pallas_call(
        functools.partial(self_kernel, score_scale=score_scale, tiles=tiles_dev, slots=slots),
        out_shape=jax.ShapeDtypeStruct(q_raw.shape, jnp.bfloat16),
        grid=(rows_c, groups),
        in_specs=[
            pl.BlockSpec((1, tok_dev, HD), lambda c, h: (c, 0, h)),
            pl.BlockSpec((1, tok_dev, 1), lambda c, h: (c, 0, 0)),
            pl.BlockSpec((1, HD), lambda c, h: (0, h)),
            pl.BlockSpec((1, slots, tok_dev, 1), lambda c, h: (c, 0, 0, 0)),
            pl.BlockSpec((1, HD), lambda c, h: (0, h)),
            pl.BlockSpec((tiles_dev, 1, key_len), lambda c, h: (0, 0, 0)),
            pl.BlockSpec((8, 128), lambda c, h: (0, 0)),
        ] + k_specs + v_specs,
        out_specs=pl.BlockSpec((1, tok_dev, HD), lambda c, h: (c, 0, h)),
        cost_estimate=pl.CostEstimate(
            flops=4 * rows_c * tok_dev * key_len * width,
            transcendentals=rows_c * tok_dev * key_len * groups,
            bytes_accessed=4 * q_raw.size + 4 * slots * k_raw.size,
        ),
    )(
        q_raw, factor_of(q_total), q_gain.reshape(1, width), k_fac, k_gain.reshape(1, width),
        self_mask, slot_ok, *k_args, *v_args,
    )
    return (self_out, cross_out)


def solution(mesh):
    in_specs = (
        P(None, "frame", "head"),
        P(None, "frame", "head"),
        P(None, "frame", "head"),
        P(None, "frame", "head"),
        P(None, "frame", "head"),
        P(None, "frame", "head"),
        P("head"),
        P("head"),
        P("head"),
        P("head"),
        P("frame", None),
        P("frame"),
        P(),
    )
    out_specs = (P(None, "frame", "head"), P(None, "frame", "head"))
    return jax.shard_map(body, mesh=mesh, in_specs=in_specs, out_specs=out_specs, check_vma=False)
```

```python
import functools
import math

import jax
import jax.numpy as jnp
import numpy as np
from jax import lax
from jax.experimental import pallas as pl
from jax.experimental.pallas import tpu as pltpu
from jax.sharding import PartitionSpec as P

D = 5120
HD = 128
NB = 14
REACH = 2
MESH = pl.DeviceIdType.MESH

EPSILON = 1e-06

TEXT_BITS = (4, 2, 1, 32, 16, 8)
EARLY_TEXT_STEPS = 4
KV_CHUNKS = 4


def text_bits(n_frame):
    return [b for b in TEXT_BITS if b < n_frame]


def text_orders(n_frame):
    first = text_bits(n_frame)
    second = first[:-2] + first[-2:][::-1] if len(first) >= 2 else first
    return [first, second]


def direct_steps(orders):
    shared = 0
    while shared < min(3, len(orders[0])) and all(o[shared] == orders[0][shared] for o in orders):
        shared += 1
    return shared


def squares(tensor):
    values = tensor.astype(jnp.float32)
    return jnp.sum(values * values, axis=-1)


def factor_of(totals):
    return lax.rsqrt(totals / D + EPSILON)[..., None]


class _Pair:
    def __init__(self, first, second):
        self.parts = (first, second)

    def start(self):
        for p in self.parts:
            p.start()

    def wait_send(self):
        for p in self.parts:
            p.wait_send()

    def wait_recv(self):
        for p in self.parts:
            p.wait_recv()


def kv_kernel(k_own, v_own, kv_nb, kv_send, kv_recv, *, n_frame, chunks):
    f = lax.axis_index("frame")
    h = lax.axis_index("head")
    has_prev = f >= 1
    has_next = f <= n_frame - 2

    barrier = pltpu.get_barrier_semaphore()

    @pl.when(has_prev)
    def _():
        pl.semaphore_signal(barrier, inc=1, device_id=(f - 1, h), device_id_type=MESH)

    @pl.when(has_next)
    def _():
        pl.semaphore_signal(barrier, inc=1, device_id=(f + 1, h), device_id_type=MESH)

    pl.semaphore_wait(barrier, has_prev.astype(jnp.int32) + has_next.astype(jnp.int32))

    span = k_own.shape[1] // chunks

    def hop(src, dst, i, step, slot, target):
        return pltpu.make_async_remote_copy(
            src_ref=src.at[..., pl.ds(i * span, span), :], dst_ref=dst.at[..., pl.ds(i * span, span), :],
            send_sem=kv_send.at[step, i], recv_sem=kv_recv.at[slot, i],
            device_id=(target, h), device_id_type=MESH)

    def own_hop(i, step, slot, target):
        return _Pair(hop(k_own, kv_nb.at[slot, 0], i, step, slot, target),
                     hop(v_own, kv_nb.at[slot, 1], i, step + 4, slot + 4, target))

    to_next = [own_hop(i, 0, 1, f + 1) for i in range(chunks)]
    to_prev = [own_hop(i, 1, 2, f - 1) for i in range(chunks)]
    fwd_next = [hop(kv_nb.at[1], kv_nb.at[0], i, 2, 0, f + 1) for i in range(chunks)]
    fwd_prev = [hop(kv_nb.at[2], kv_nb.at[3], i, 3, 3, f - 1) for i in range(chunks)]
    both = jnp.logical_and(has_prev, has_next)

    @pl.when(has_next)
    def _():
        for c in to_next:
            c.start()

    @pl.when(has_prev)
    def _():
        for c in to_prev:
            c.start()

    for i in range(chunks):
        @pl.when(has_prev)
        def _():
            to_next[i].wait_recv()

        @pl.when(has_next)
        def _():
            to_prev[i].wait_recv()

        @pl.when(both)
        def _():
            fwd_next[i].start()
            fwd_prev[i].start()

    for i in range(chunks):
        @pl.when(has_next)
        def _():
            to_next[i].wait_send()

        @pl.when(has_prev)
        def _():
            to_prev[i].wait_send()

        @pl.when(f >= 2)
        def _():
            fwd_next[i].wait_recv()

        @pl.when(f <= n_frame - 3)
        def _():
            fwd_prev[i].wait_recv()

        @pl.when(both)
        def _():
            fwd_next[i].wait_send()
            fwd_prev[i].wait_send()


def text_kernel(text_own, text_all, tx_send, tx_recv, dx_send, dx_recv, local_sem, *, orders, rows):
    f = lax.axis_index("frame")
    h = lax.axis_index("head")
    barrier = pltpu.get_barrier_semaphore()
    shared = direct_steps(orders)
    masks = [sum(orders[0][i] for i in range(shared) if (d >> i) & 1) for d in range(1, 1 << shared)]
    masks += list(orders[0][shared:])
    for m in masks:
        pl.semaphore_signal(barrier, inc=1, device_id=(f ^ m, h), device_id_type=MESH)
    pl.semaphore_wait(barrier, len(masks))

    streams = len(orders)
    lanes = text_own.shape[0] // streams
    shared = direct_steps(orders)
    positions = []
    for s, bits in enumerate(orders):
        pos = 0
        for i, b in enumerate(bits):
            pos = pos + ((f // b) % 2) * (1 << i)
        positions.append(pos)
        mine = pltpu.make_async_copy(
            text_own.at[pl.ds(s * lanes, lanes)],
            text_all.at[pl.ds(s * lanes, lanes), pl.ds(pl.multiple_of(pos * rows, rows), rows)],
            local_sem.at[s])
        mine.start()
        mine.wait()
    sends = []
    for s in range(streams):
        own_rows = text_all.at[pl.ds(s * lanes, lanes), pl.ds(pl.multiple_of(positions[s] * rows, rows), rows)]
        for d in range(1, 1 << shared):
            mask = sum(orders[0][i] for i in range(shared) if (d >> i) & 1)
            copy = pltpu.make_async_remote_copy(
                src_ref=own_rows, dst_ref=own_rows, send_sem=dx_send.at[s, d - 1],
                recv_sem=dx_recv.at[s, d - 1], device_id=(f ^ mask, h), device_id_type=MESH)
            copy.start()
            sends.append(copy)
    for copy in sends:
        copy.wait_send()
        copy.wait_recv()
    for i in range(shared, len(orders[0])):
        swaps = []
        for s, bits in enumerate(orders):
            size = rows << i
            start = pl.multiple_of((positions[s] >> i) * size, size)
            block = text_all.at[pl.ds(s * lanes, lanes), pl.ds(start, size)]
            swap = pltpu.make_async_remote_copy(
                src_ref=block, dst_ref=block, send_sem=tx_send.at[s, i], recv_sem=tx_recv.at[s, i],
                device_id=(f ^ bits[i], h), device_id_type=MESH)
            swap.start()
            swaps.append(swap)
        for swap in swaps:
            swap.wait_send()
            swap.wait_recv()


def exchange(k_own, v_own, text_own, n_frame):
    kv_shape = (2,) + k_own.shape
    kv_nb = pl.pallas_call(
        functools.partial(kv_kernel, n_frame=n_frame, chunks=KV_CHUNKS),
        out_shape=jax.ShapeDtypeStruct((4,) + kv_shape, k_own.dtype),
        in_specs=[pl.BlockSpec(memory_space=pl.ANY)] * 2,
        out_specs=pl.BlockSpec(memory_space=pl.ANY),
        scratch_shapes=[
            pltpu.SemaphoreType.DMA((8, KV_CHUNKS)),
            pltpu.SemaphoreType.DMA((8, KV_CHUNKS)),
        ],
        compiler_params=pltpu.CompilerParams(collective_id=0, has_side_effects=True),
    )(k_own, v_own)
    orders = text_orders(n_frame)
    rows = text_own.shape[1]
    text_all = pl.pallas_call(
        functools.partial(text_kernel, orders=orders, rows=rows),
        out_shape=jax.ShapeDtypeStruct((text_own.shape[0], rows * n_frame, text_own.shape[2]), text_own.dtype),
        in_specs=[pl.BlockSpec(memory_space=pl.ANY)],
        out_specs=pl.BlockSpec(memory_space=pl.ANY),
        scratch_shapes=[
            pltpu.SemaphoreType.DMA((len(orders), len(orders[0]))),
            pltpu.SemaphoreType.DMA((len(orders), len(orders[0]))),
            pltpu.SemaphoreType.DMA((len(orders), (1 << direct_steps(orders)) - 1)),
            pltpu.SemaphoreType.DMA((len(orders), (1 << direct_steps(orders)) - 1)),
            pltpu.SemaphoreType.DMA((len(orders),)),
        ],
        compiler_params=pltpu.CompilerParams(collective_id=1, has_side_effects=True),
    )(text_own)
    return kv_nb, text_all


def softmax_rows(scores):
    row_top = jnp.max(scores, axis=-1, keepdims=True)
    powers = jnp.exp(scores - row_top)
    inverse = 1.0 / jnp.sum(powers, axis=-1, keepdims=True)
    return (powers * inverse).astype(jnp.bfloat16)


def normalized(raw, fac, gain):
    return (raw.astype(jnp.float32) * fac * gain).astype(jnp.bfloat16)


def self_kernel(q_ref, qf_ref, qg_ref, kf_ref, kfo_ref, kg_ref, mask_ref, ok_ref, *refs, score_scale, tiles, slots):
    k_refs = refs[:slots]
    v_refs = refs[slots:2 * slots]
    o_ref = refs[2 * slots]
    q = normalized(q_ref[0], qf_ref[0], qg_ref[...])
    span = q.shape[0]
    kg = kg_ref[...]
    parts = []
    for j in range(slots):
        fac = kfo_ref[0] if j == slots // 2 else kf_ref[j if j < slots // 2 else j - 1, 0]
        k = normalized(k_refs[j][0], fac, kg)
        parts.append(lax.dot_general(q, k, (((1,), (1,)), ((), ())), preferred_element_type=jnp.float32))
    scores = jnp.concatenate(parts, axis=1) * score_scale
    key_len = scores.shape[1]
    scores = scores.reshape(tiles, span // tiles, key_len)
    scores = jnp.where(mask_ref[...] > 0, scores, -1e30)
    weights = softmax_rows(scores).reshape(span, key_len)
    out = None
    for j in range(slots):
        v = jnp.where(ok_ref[j:j + 1, :] > 0, v_refs[j][0], jnp.zeros((), v_refs[j].dtype))
        part = jnp.dot(weights[:, j * span:(j + 1) * span], v, preferred_element_type=jnp.float32)
        out = part if out is None else out + part
    o_ref[0] = out.astype(o_ref.dtype)


def cross_kernel(q_ref, qf_ref, qg_ref, k_ref, kf_ref, kg_ref, v_ref, mask_ref, o_ref, *, score_scale):
    q = normalized(q_ref[0], qf_ref[0], qg_ref[...])
    k = normalized(k_ref[0], kf_ref[0], kg_ref[...])
    scores = lax.dot_general(q, k, (((1,), (1,)), ((), ())), preferred_element_type=jnp.float32)
    scores = jnp.where(mask_ref[0] > 0, scores * score_scale, -1e30)
    weights = softmax_rows(scores)
    out = jnp.dot(weights, v_ref[0], preferred_element_type=jnp.float32)
    o_ref[0] = out.astype(o_ref.dtype)


def body(
    q_raw,
    k_raw,
    v_in,
    cross_q_raw,
    text_k_raw,
    text_v,
    q_gain,
    k_gain,
    cross_q_gain,
    text_k_gain,
    nbr,
    nbr_count,
    text_len,
):
    rows_c, tok_dev, width = q_raw.shape
    groups = width // HD
    tiles_dev = nbr.shape[0]
    tile_len = tok_dev // tiles_dev
    n_frame = lax.axis_size("frame")
    me = lax.axis_index("frame")
    score_scale = 1.0 / math.sqrt(HD)
    slots = 2 * REACH + 1

    txt_rows = text_k_raw.shape[1]
    text_own = jnp.stack([text_k_raw, text_v], axis=1).reshape(2 * rows_c, txt_rows, width)
    kv_nb, text_all = exchange(k_raw, v_in, text_own, n_frame)

    k_nb_sq = squares(kv_nb[:, 0])
    q_total, k_total, k_nb_total, cross_total, text_total = lax.psum(
        (squares(q_raw), squares(k_raw), k_nb_sq, squares(cross_q_raw), squares(text_all[0::2])), "head"
    )
    k_fac = factor_of(
        jnp.stack([k_nb_total[0], k_nb_total[1], k_total, k_nb_total[2], k_nb_total[3]], axis=1)
    )

    token_rows = []
    for bits in text_orders(n_frame):
        frame_of_pos = np.zeros(n_frame, np.int32)
        for p in range(n_frame):
            frame_of_pos[p] = sum(b for i, b in enumerate(bits) if (p >> i) & 1)
        token_rows.append((frame_of_pos[:, None] * txt_rows + np.arange(txt_rows)[None, :]).reshape(-1))
    token_of_row = np.stack(token_rows)
    text_mask = (jnp.asarray(token_of_row) < text_len[:, None]).astype(jnp.int32)[:, None, :]

    text_len_all = n_frame * txt_rows
    cross_out = pl.pallas_call(
        functools.partial(cross_kernel, score_scale=score_scale),
        out_shape=jax.ShapeDtypeStruct(q_raw.shape, jnp.bfloat16),
        grid=(rows_c, groups),
        in_specs=[
            pl.BlockSpec((1, tok_dev, HD), lambda c, h: (c, 0, h)),
            pl.BlockSpec((1, tok_dev, 1), lambda c, h: (c, 0, 0)),
            pl.BlockSpec((1, HD), lambda c, h: (0, h)),
            pl.BlockSpec((1, text_len_all, HD), lambda c, h: (2 * c, 0, h)),
            pl.BlockSpec((1, text_len_all, 1), lambda c, h: (c, 0, 0)),
            pl.BlockSpec((1, HD), lambda c, h: (0, h)),
            pl.BlockSpec((1, text_len_all, HD), lambda c, h: (2 * c + 1, 0, h)),
            pl.BlockSpec((1, 1, text_len_all), lambda c, h: (c, 0, 0)),
        ],
        out_specs=pl.BlockSpec((1, tok_dev, HD), lambda c, h: (c, 0, h)),
        cost_estimate=pl.CostEstimate(
            flops=4 * rows_c * tok_dev * text_len_all * width,
            transcendentals=rows_c * tok_dev * text_len_all * groups,
            bytes_accessed=4 * q_raw.size + 2 * text_all.size,
        ),
    )(
        cross_q_raw, factor_of(cross_total), cross_q_gain.reshape(1, width),
        text_all, factor_of(text_total), text_k_gain.reshape(1, width),
        text_all, text_mask,
    )

    first_tile = (me - REACH) * tiles_dev
    cand = first_tile + jnp.arange(slots * tiles_dev, dtype=jnp.int32)
    live_slot = jnp.arange(NB, dtype=jnp.int32)[None, :] < nbr_count[:, None]
    hit = (nbr[:, :, None] == cand[None, None, :]) & live_slot[:, :, None]
    live = jnp.any(hit, axis=1)
    self_mask = jnp.repeat(live.astype(jnp.int32), tile_len, axis=1)[:, None, :]
    shard_of_slot = me - REACH + jnp.arange(8, dtype=jnp.int32)
    slot_ok = (shard_of_slot >= 0) & (shard_of_slot < n_frame)
    slot_ok = jnp.broadcast_to(slot_ok.astype(jnp.int32)[:, None], (8, 128))

    nb_index = {0: 0, 1: 1, 3: 2, 4: 3}
    k_specs, v_specs, k_args, v_args = [], [], [], []
    for j in range(slots):
        if j == REACH:
            k_specs.append(pl.BlockSpec((1, tok_dev, HD), lambda c, h: (c, 0, h)))
            v_specs.append(pl.BlockSpec((1, tok_dev, HD), lambda c, h: (c, 0, h)))
            k_args.append(k_raw)
            v_args.append(v_in)
        else:
            s = nb_index[j]
            k_specs.append(pl.BlockSpec((None, None, 1, tok_dev, HD), lambda c, h, s=s: (s, 0, c, 0, h)))
            v_specs.append(pl.BlockSpec((None, None, 1, tok_dev, HD), lambda c, h, s=s: (s, 1, c, 0, h)))
            k_args.append(kv_nb)
            v_args.append(kv_nb)

    key_len = slots * tok_dev
    self_out = pl.pallas_call(
        functools.partial(self_kernel, score_scale=score_scale, tiles=tiles_dev, slots=slots),
        out_shape=jax.ShapeDtypeStruct(q_raw.shape, jnp.bfloat16),
        grid=(rows_c, groups),
        in_specs=[
            pl.BlockSpec((1, tok_dev, HD), lambda c, h: (c, 0, h)),
            pl.BlockSpec((1, tok_dev, 1), lambda c, h: (c, 0, 0)),
            pl.BlockSpec((1, HD), lambda c, h: (0, h)),
            pl.BlockSpec((slots - 1, 1, tok_dev, 1), lambda c, h: (0, c, 0, 0)),
            pl.BlockSpec((1, tok_dev, 1), lambda c, h: (c, 0, 0)),
            pl.BlockSpec((1, HD), lambda c, h: (0, h)),
            pl.BlockSpec((tiles_dev, 1, key_len), lambda c, h: (0, 0, 0)),
            pl.BlockSpec((8, 128), lambda c, h: (0, 0)),
        ] + k_specs + v_specs,
        out_specs=pl.BlockSpec((1, tok_dev, HD), lambda c, h: (c, 0, h)),
        cost_estimate=pl.CostEstimate(
            flops=4 * rows_c * tok_dev * key_len * width,
            transcendentals=rows_c * tok_dev * key_len * groups,
            bytes_accessed=4 * q_raw.size + 4 * slots * k_raw.size,
        ),
    )(
        q_raw, factor_of(q_total), q_gain.reshape(1, width), factor_of(k_nb_total), factor_of(k_total), k_gain.reshape(1, width),
        self_mask, slot_ok, *k_args, *v_args,
    )
    return (self_out, cross_out)


def solution(mesh):
    in_specs = (
        P(None, "frame", "head"),
        P(None, "frame", "head"),
        P(None, "frame", "head"),
        P(None, "frame", "head"),
        P(None, "frame", "head"),
        P(None, "frame", "head"),
        P("head"),
        P("head"),
        P("head"),
        P("head"),
        P("frame", None),
        P("frame"),
        P(),
    )
    out_specs = (P(None, "frame", "head"), P(None, "frame", "head"))
    return jax.shard_map(body, mesh=mesh, in_specs=in_specs, out_specs=out_specs, check_vma=False)
```

```python
import functools
import math

import jax
import jax.numpy as jnp
import numpy as np
from jax import lax
from jax.experimental import pallas as pl
from jax.experimental.pallas import tpu as pltpu
from jax.sharding import PartitionSpec as P

D = 5120
HD = 128
NB = 14
REACH = 2
MESH = pl.DeviceIdType.MESH

EPSILON = 1e-06

TEXT_BITS = (4, 2, 1, 32, 16, 8)
EARLY_TEXT_STEPS = 4
KV_CHUNKS = 2


def text_bits(n_frame):
    return [b for b in TEXT_BITS if b < n_frame]


def text_orders(n_frame):
    first = text_bits(n_frame)
    second = first[:-2] + first[-2:][::-1] if len(first) >= 2 else first
    return [first, second]


def direct_steps(orders):
    shared = 0
    while shared < min(3, len(orders[0])) and all(o[shared] == orders[0][shared] for o in orders):
        shared += 1
    return shared


def squares(tensor):
    values = tensor.astype(jnp.float32)
    return jnp.sum(values * values, axis=-1)


def factor_of(totals):
    return lax.rsqrt(totals / D + EPSILON)[..., None]


class _Pair:
    def __init__(self, first, second):
        self.parts = (first, second)

    def start(self):
        for p in self.parts:
            p.start()

    def wait_send(self):
        for p in self.parts:
            p.wait_send()

    def wait_recv(self):
        for p in self.parts:
            p.wait_recv()


def kv_kernel(k_own, v_own, kv_nb, kv_send, kv_recv, *, n_frame, chunks):
    f = lax.axis_index("frame")
    h = lax.axis_index("head")
    has_prev = f >= 1
    has_next = f <= n_frame - 2

    barrier = pltpu.get_barrier_semaphore()

    @pl.when(has_prev)
    def _():
        pl.semaphore_signal(barrier, inc=1, device_id=(f - 1, h), device_id_type=MESH)

    @pl.when(has_next)
    def _():
        pl.semaphore_signal(barrier, inc=1, device_id=(f + 1, h), device_id_type=MESH)

    pl.semaphore_wait(barrier, has_prev.astype(jnp.int32) + has_next.astype(jnp.int32))

    span = k_own.shape[1] // chunks

    def hop(src, dst, i, step, slot, target):
        return pltpu.make_async_remote_copy(
            src_ref=src.at[..., pl.ds(i * span, span), :], dst_ref=dst.at[..., pl.ds(i * span, span), :],
            send_sem=kv_send.at[step, i], recv_sem=kv_recv.at[slot, i],
            device_id=(target, h), device_id_type=MESH)

    def own_hop(i, step, slot, target):
        return _Pair(hop(k_own, kv_nb.at[slot, 0], i, step, slot, target),
                     hop(v_own, kv_nb.at[slot, 1], i, step + 4, slot + 4, target))

    to_next = [own_hop(i, 0, 1, f + 1) for i in range(chunks)]
    to_prev = [own_hop(i, 1, 2, f - 1) for i in range(chunks)]
    fwd_next = [hop(kv_nb.at[1], kv_nb.at[0], i, 2, 0, f + 1) for i in range(chunks)]
    fwd_prev = [hop(kv_nb.at[2], kv_nb.at[3], i, 3, 3, f - 1) for i in range(chunks)]
    both = jnp.logical_and(has_prev, has_next)

    @pl.when(has_next)
    def _():
        for c in to_next:
            c.start()

    @pl.when(has_prev)
    def _():
        for c in to_prev:
            c.start()

    for i in range(chunks):
        @pl.when(has_prev)
        def _():
            to_next[i].wait_recv()

        @pl.when(has_next)
        def _():
            to_prev[i].wait_recv()

        @pl.when(both)
        def _():
            fwd_next[i].start()
            fwd_prev[i].start()

    for i in range(chunks):
        @pl.when(has_next)
        def _():
            to_next[i].wait_send()

        @pl.when(has_prev)
        def _():
            to_prev[i].wait_send()

        @pl.when(f >= 2)
        def _():
            fwd_next[i].wait_recv()

        @pl.when(f <= n_frame - 3)
        def _():
            fwd_prev[i].wait_recv()

        @pl.when(both)
        def _():
            fwd_next[i].wait_send()
            fwd_prev[i].wait_send()


def text_kernel(text_own, text_all, tx_send, tx_recv, dx_send, dx_recv, local_sem, *, orders, rows):
    f = lax.axis_index("frame")
    h = lax.axis_index("head")
    barrier = pltpu.get_barrier_semaphore()
    shared = direct_steps(orders)
    masks = [sum(orders[0][i] for i in range(shared) if (d >> i) & 1) for d in range(1, 1 << shared)]
    masks += list(orders[0][shared:])
    for m in masks:
        pl.semaphore_signal(barrier, inc=1, device_id=(f ^ m, h), device_id_type=MESH)
    pl.semaphore_wait(barrier, len(masks))

    streams = len(orders)
    lanes = text_own.shape[0] // streams
    shared = direct_steps(orders)
    positions = []
    for s, bits in enumerate(orders):
        pos = 0
        for i, b in enumerate(bits):
            pos = pos + ((f // b) % 2) * (1 << i)
        positions.append(pos)
        mine = pltpu.make_async_copy(
            text_own.at[pl.ds(s * lanes, lanes)],
            text_all.at[pl.ds(s * lanes, lanes), pl.ds(pl.multiple_of(pos * rows, rows), rows)],
            local_sem.at[s])
        mine.start()
        mine.wait()
    sends = []
    for s in range(streams):
        own_rows = text_all.at[pl.ds(s * lanes, lanes), pl.ds(pl.multiple_of(positions[s] * rows, rows), rows)]
        for d in range(1, 1 << shared):
            mask = sum(orders[0][i] for i in range(shared) if (d >> i) & 1)
            copy = pltpu.make_async_remote_copy(
                src_ref=own_rows, dst_ref=own_rows, send_sem=dx_send.at[s, d - 1],
                recv_sem=dx_recv.at[s, d - 1], device_id=(f ^ mask, h), device_id_type=MESH)
            copy.start()
            sends.append(copy)
    for copy in sends:
        copy.wait_send()
        copy.wait_recv()
    for i in range(shared, len(orders[0])):
        swaps = []
        for s, bits in enumerate(orders):
            size = rows << i
            start = pl.multiple_of((positions[s] >> i) * size, size)
            block = text_all.at[pl.ds(s * lanes, lanes), pl.ds(start, size)]
            swap = pltpu.make_async_remote_copy(
                src_ref=block, dst_ref=block, send_sem=tx_send.at[s, i], recv_sem=tx_recv.at[s, i],
                device_id=(f ^ bits[i], h), device_id_type=MESH)
            swap.start()
            swaps.append(swap)
        for swap in swaps:
            swap.wait_send()
            swap.wait_recv()


def exchange(k_own, v_own, text_own, n_frame):
    kv_shape = (2,) + k_own.shape
    kv_nb = pl.pallas_call(
        functools.partial(kv_kernel, n_frame=n_frame, chunks=KV_CHUNKS),
        out_shape=jax.ShapeDtypeStruct((4,) + kv_shape, k_own.dtype),
        in_specs=[pl.BlockSpec(memory_space=pl.ANY)] * 2,
        out_specs=pl.BlockSpec(memory_space=pl.ANY),
        scratch_shapes=[
            pltpu.SemaphoreType.DMA((8, KV_CHUNKS)),
            pltpu.SemaphoreType.DMA((8, KV_CHUNKS)),
        ],
        compiler_params=pltpu.CompilerParams(collective_id=0, has_side_effects=True),
    )(k_own, v_own)
    orders = text_orders(n_frame)
    rows = text_own.shape[1]
    text_all = pl.pallas_call(
        functools.partial(text_kernel, orders=orders, rows=rows),
        out_shape=jax.ShapeDtypeStruct((text_own.shape[0], rows * n_frame, text_own.shape[2]), text_own.dtype),
        in_specs=[pl.BlockSpec(memory_space=pl.ANY)],
        out_specs=pl.BlockSpec(memory_space=pl.ANY),
        scratch_shapes=[
            pltpu.SemaphoreType.DMA((len(orders), len(orders[0]))),
            pltpu.SemaphoreType.DMA((len(orders), len(orders[0]))),
            pltpu.SemaphoreType.DMA((len(orders), (1 << direct_steps(orders)) - 1)),
            pltpu.SemaphoreType.DMA((len(orders), (1 << direct_steps(orders)) - 1)),
            pltpu.SemaphoreType.DMA((len(orders),)),
        ],
        compiler_params=pltpu.CompilerParams(collective_id=1, has_side_effects=True),
    )(text_own)
    return kv_nb, text_all


def softmax_rows(scores):
    row_top = jnp.max(scores, axis=-1, keepdims=True)
    powers = jnp.exp(scores - row_top)
    inverse = 1.0 / jnp.sum(powers, axis=-1, keepdims=True)
    return (powers * inverse).astype(jnp.bfloat16)


def normalized(raw, fac, gain):
    return (raw.astype(jnp.float32) * fac * gain).astype(jnp.bfloat16)


def self_kernel(q_ref, qf_ref, qg_ref, kf_ref, kg_ref, mask_ref, ok_ref, *refs, score_scale, tiles, slots):
    k_refs = refs[:slots]
    v_refs = refs[slots:2 * slots]
    o_ref = refs[2 * slots]
    q = normalized(q_ref[0], qf_ref[0], qg_ref[...])
    span = q.shape[0]
    kg = kg_ref[...]
    parts = []
    for j in range(slots):
        k = normalized(k_refs[j][0], kf_ref[0, j], kg)
        parts.append(lax.dot_general(q, k, (((1,), (1,)), ((), ())), preferred_element_type=jnp.float32))
    scores = jnp.concatenate(parts, axis=1) * score_scale
    key_len = scores.shape[1]
    scores = scores.reshape(tiles, span // tiles, key_len)
    scores = jnp.where(mask_ref[...] > 0, scores, -1e30)
    weights = softmax_rows(scores).reshape(span, key_len)
    out = None
    for j in range(slots):
        v = jnp.where(ok_ref[j:j + 1, :] > 0, v_refs[j][0], jnp.zeros((), v_refs[j].dtype))
        part = jnp.dot(weights[:, j * span:(j + 1) * span], v, preferred_element_type=jnp.float32)
        out = part if out is None else out + part
    o_ref[0] = out.astype(o_ref.dtype)


def cross_kernel(q_ref, qf_ref, qg_ref, k_ref, kf_ref, kg_ref, v_ref, mask_ref, o_ref, *, score_scale):
    q = normalized(q_ref[0], qf_ref[0], qg_ref[...])
    k = normalized(k_ref[0], kf_ref[0], kg_ref[...])
    scores = lax.dot_general(q, k, (((1,), (1,)), ((), ())), preferred_element_type=jnp.float32)
    scores = jnp.where(mask_ref[0] > 0, scores * score_scale, -1e30)
    weights = softmax_rows(scores)
    out = jnp.dot(weights, v_ref[0], preferred_element_type=jnp.float32)
    o_ref[0] = out.astype(o_ref.dtype)


def body(
    q_raw,
    k_raw,
    v_in,
    cross_q_raw,
    text_k_raw,
    text_v,
    q_gain,
    k_gain,
    cross_q_gain,
    text_k_gain,
    nbr,
    nbr_count,
    text_len,
):
    rows_c, tok_dev, width = q_raw.shape
    groups = width // HD
    tiles_dev = nbr.shape[0]
    tile_len = tok_dev // tiles_dev
    n_frame = lax.axis_size("frame")
    me = lax.axis_index("frame")
    score_scale = 1.0 / math.sqrt(HD)
    slots = 2 * REACH + 1

    txt_rows = text_k_raw.shape[1]
    text_own = jnp.stack([text_k_raw, text_v], axis=1).reshape(2 * rows_c, txt_rows, width)
    kv_nb, text_all = exchange(k_raw, v_in, text_own, n_frame)

    k_nb_sq = squares(kv_nb[:, 0])
    q_total, k_total, k_nb_total, cross_total, text_total = lax.psum(
        (squares(q_raw), squares(k_raw), k_nb_sq, squares(cross_q_raw), squares(text_all[0::2])), "head"
    )
    k_fac = factor_of(
        jnp.stack([k_nb_total[0], k_nb_total[1], k_total, k_nb_total[2], k_nb_total[3]], axis=1)
    )

    token_rows = []
    for bits in text_orders(n_frame):
        frame_of_pos = np.zeros(n_frame, np.int32)
        for p in range(n_frame):
            frame_of_pos[p] = sum(b for i, b in enumerate(bits) if (p >> i) & 1)
        token_rows.append((frame_of_pos[:, None] * txt_rows + np.arange(txt_rows)[None, :]).reshape(-1))
    token_of_row = np.stack(token_rows)
    text_mask = (jnp.asarray(token_of_row) < text_len[:, None]).astype(jnp.int32)[:, None, :]

    text_len_all = n_frame * txt_rows
    cross_out = pl.pallas_call(
        functools.partial(cross_kernel, score_scale=score_scale),
        out_shape=jax.ShapeDtypeStruct(q_raw.shape, jnp.bfloat16),
        grid=(rows_c, groups),
        in_specs=[
            pl.BlockSpec((1, tok_dev, HD), lambda c, h: (c, 0, h)),
            pl.BlockSpec((1, tok_dev, 1), lambda c, h: (c, 0, 0)),
            pl.BlockSpec((1, HD), lambda c, h: (0, h)),
            pl.BlockSpec((1, text_len_all, HD), lambda c, h: (2 * c, 0, h)),
            pl.BlockSpec((1, text_len_all, 1), lambda c, h: (c, 0, 0)),
            pl.BlockSpec((1, HD), lambda c, h: (0, h)),
            pl.BlockSpec((1, text_len_all, HD), lambda c, h: (2 * c + 1, 0, h)),
            pl.BlockSpec((1, 1, text_len_all), lambda c, h: (c, 0, 0)),
        ],
        out_specs=pl.BlockSpec((1, tok_dev, HD), lambda c, h: (c, 0, h)),
        cost_estimate=pl.CostEstimate(
            flops=4 * rows_c * tok_dev * text_len_all * width,
            transcendentals=rows_c * tok_dev * text_len_all * groups,
            bytes_accessed=4 * q_raw.size + 2 * text_all.size,
        ),
    )(
        cross_q_raw, factor_of(cross_total), cross_q_gain.reshape(1, width),
        text_all, factor_of(text_total), text_k_gain.reshape(1, width),
        text_all, text_mask,
    )

    first_tile = (me - REACH) * tiles_dev
    cand = first_tile + jnp.arange(slots * tiles_dev, dtype=jnp.int32)
    live_slot = jnp.arange(NB, dtype=jnp.int32)[None, :] < nbr_count[:, None]
    hit = (nbr[:, :, None] == cand[None, None, :]) & live_slot[:, :, None]
    live = jnp.any(hit, axis=1)
    self_mask = jnp.repeat(live.astype(jnp.int32), tile_len, axis=1)[:, None, :]
    shard_of_slot = me - REACH + jnp.arange(8, dtype=jnp.int32)
    slot_ok = (shard_of_slot >= 0) & (shard_of_slot < n_frame)
    slot_ok = jnp.broadcast_to(slot_ok.astype(jnp.int32)[:, None], (8, 128))

    nb_index = {0: 0, 1: 1, 3: 2, 4: 3}
    k_specs, v_specs, k_args, v_args = [], [], [], []
    for j in range(slots):
        if j == REACH:
            k_specs.append(pl.BlockSpec((1, tok_dev, HD), lambda c, h: (c, 0, h)))
            v_specs.append(pl.BlockSpec((1, tok_dev, HD), lambda c, h: (c, 0, h)))
            k_args.append(k_raw)
            v_args.append(v_in)
        else:
            s = nb_index[j]
            k_specs.append(pl.BlockSpec((None, None, 1, tok_dev, HD), lambda c, h, s=s: (s, 0, c, 0, h)))
            v_specs.append(pl.BlockSpec((None, None, 1, tok_dev, HD), lambda c, h, s=s: (s, 1, c, 0, h)))
            k_args.append(kv_nb)
            v_args.append(kv_nb)

    key_len = slots * tok_dev
    self_out = pl.pallas_call(
        functools.partial(self_kernel, score_scale=score_scale, tiles=tiles_dev, slots=slots),
        out_shape=jax.ShapeDtypeStruct(q_raw.shape, jnp.bfloat16),
        grid=(rows_c, groups),
        in_specs=[
            pl.BlockSpec((1, tok_dev, HD), lambda c, h: (c, 0, h)),
            pl.BlockSpec((1, tok_dev, 1), lambda c, h: (c, 0, 0)),
            pl.BlockSpec((1, HD), lambda c, h: (0, h)),
            pl.BlockSpec((1, slots, tok_dev, 1), lambda c, h: (c, 0, 0, 0)),
            pl.BlockSpec((1, HD), lambda c, h: (0, h)),
            pl.BlockSpec((tiles_dev, 1, key_len), lambda c, h: (0, 0, 0)),
            pl.BlockSpec((8, 128), lambda c, h: (0, 0)),
        ] + k_specs + v_specs,
        out_specs=pl.BlockSpec((1, tok_dev, HD), lambda c, h: (c, 0, h)),
        cost_estimate=pl.CostEstimate(
            flops=4 * rows_c * tok_dev * key_len * width,
            transcendentals=rows_c * tok_dev * key_len * groups,
            bytes_accessed=4 * q_raw.size + 4 * slots * k_raw.size,
        ),
    )(
        q_raw, factor_of(q_total), q_gain.reshape(1, width), k_fac, k_gain.reshape(1, width),
        self_mask, slot_ok, *k_args, *v_args,
    )
    return (self_out, cross_out)


def solution(mesh):
    in_specs = (
        P(None, "frame", "head"),
        P(None, "frame", "head"),
        P(None, "frame", "head"),
        P(None, "frame", "head"),
        P(None, "frame", "head"),
        P(None, "frame", "head"),
        P("head"),
        P("head"),
        P("head"),
        P("head"),
        P("frame", None),
        P("frame"),
        P(),
    )
    out_specs = (P(None, "frame", "head"), P(None, "frame", "head"))
    return jax.shard_map(body, mesh=mesh, in_specs=in_specs, out_specs=out_specs, check_vma=False)
```
